32 devices in a mesh: ctx: 4 (over z), dom: 2 (over y), rep: 4 (over x, core).
Axes of the slice: x: 2, y: 2, z: 4, core: 2. Of those that a mesh axis runs over, the one named last changes fastest.
Arguments:
- hidden: bfloat16 [4, 2, 512, 2048], P('rep', 'dom', 'ctx'), may hold values from -6 to 6
- bmat: bfloat16 [4, 2, 512, 128], P('rep', 'dom', 'ctx'), may hold values from -0.5 to 0.5
- cmat: bfloat16 [4, 2, 512, 128], P('rep', 'dom', 'ctx'), may hold values from -6 to 6
- tokens: int32 [4, 2, 512], P('rep', 'dom', 'ctx'), may hold values from 0 to 3
- table: float32 [4, 128], replicated, may hold values from -0.5 to 0.5
- step_size: float32 [4, 2, 512, 16], P('rep', 'dom', 'ctx'), may hold values from 0.005 to 0.05
- log_decay: float32 [4, 2, 512, 16], P('rep', 'dom', 'ctx'), may hold values from 0 to 1.5
- skip_gain: float32 [16], replicated, may hold values from 0.5 to 1.5
- prev_state: float32 [4, 2, 16, 128, 128], P('rep', 'dom', 'ctx'), may hold values from -0.5 to 0.5
- ancestors: int32 [4, 2], P('rep', 'dom'), may hold values from 0 to 1
- suffix_start: int32 [4], P('rep'), may hold values from 128 to 511
- cotangent: bfloat16 [4, 2, 512, 2048], P('rep', 'dom', 'ctx'), may hold values from -6 to 6
Outputs:
- mixed: bfloat16 [4, 2, 512, 2048], P('rep', 'dom', 'ctx')
- grad_hidden: bfloat16 [4, 2, 512, 2048], P('rep', 'dom', 'ctx')
- grad_bmat: bfloat16 [4, 2, 512, 128], P('rep', 'dom', 'ctx')
- grad_cmat: bfloat16 [4, 2, 512, 128], P('rep', 'dom', 'ctx')
- grad_table: float32 [4, 128], replicated
- grad_skip: float32 [16], replicated
The draws below stay inside these ranges and needn't reach their ends.
All inputs are finite; a program needn't handle non-finite values.
Results may differ from the reference program's by a relative error of at most 0.008.
Values sent between devices are 32-bit elements; how exact they have to be, the bound alone decides.
No kernel may reach another device: no remote copies, remote signals or barrier semaphores. Data moves between devices by JAX's collectives and lax.ppermute only.
A program may use at most 192 MiB of HBM per device.

```python
import math
import jax
import jax.numpy as jnp
from jax import lax

HEADS = 16
HD = 128
N = 128
VOCAB = 4
CH = 128
CUE_QUERY_COUNT = 4
CUE_SAMPLE_COUNT = 2
STRAND_SPAN = 512
W = 2048
N_CTX = 4


def draw_log_decay(key, part):
    stochastic_seed_array = jax.random.split(key, 7)
    head_shape = (CUE_QUERY_COUNT, CUE_SAMPLE_COUNT, 1, HEADS)
    fast_share = 0.5
    picker = jax.random.uniform(stochastic_seed_array[0], head_shape, jnp.float32)
    fast_rate = jax.random.uniform(stochastic_seed_array[1], head_shape, jnp.float32, 1.0 / 50.0, 1.0 / 30.0)
    keeping = jax.random.uniform(stochastic_seed_array[2], head_shape, jnp.float32, 0.4, 0.8)
    slow_rate = -jnp.log(keeping) / STRAND_SPAN
    base_rate = jnp.where(picker < fast_share, fast_rate, slow_rate)
    rough = jax.random.uniform(stochastic_seed_array[3], (CUE_QUERY_COUNT, CUE_SAMPLE_COUNT, STRAND_SPAN, HEADS), jnp.float32, 0.4, 1.6)
    rates = base_rate * rough
    spike_occurrences = jax.random.randint(stochastic_seed_array[4], (CUE_QUERY_COUNT, CUE_SAMPLE_COUNT, 2), 0, STRAND_SPAN)
    symbol_site_indices = jnp.arange(STRAND_SPAN)
    foremost_hit_index = (symbol_site_indices[None, None, :] == spike_occurrences[:, :, 0:1]).astype(jnp.float32)
    subsequent_hit_index = (symbol_site_indices[None, None, :] == spike_occurrences[:, :, 1:2]).astype(jnp.float32)
    first_loss = -jnp.log(jax.random.uniform(stochastic_seed_array[5], head_shape, jnp.float32, 0.5, 0.8))
    second_loss = -jnp.log(jax.random.uniform(stochastic_seed_array[6], head_shape, jnp.float32, 0.5, 0.8))
    rates = rates + foremost_hit_index[:, :, :, None] * first_loss + subsequent_hit_index[:, :, :, None] * second_loss
    return rates.astype(jnp.float32)


def touch_ends(result, key, low, largest):
    index_at = [jax.random.randint(jax.random.fold_in(key, axis), (), 0, length) for axis, length in enumerate(result.shape)]
    widest = result.shape.index(max(result.shape))
    next_to = index_at[:widest] + [(index_at[widest] + 1) % result.shape[widest]] + index_at[widest + 1:]
    return result.at[tuple(index_at)].set(low).at[tuple(next_to)].set(largest)


def shard_levels(key, dims, cuts, low, high):
    loudness = 1.0
    for dim, blocks in cuts:
        heights = jax.random.uniform(jax.random.fold_in(jax.random.fold_in(key, 6), dim), (blocks,), jnp.float32, low / len(cuts), high / len(cuts))
        loudness = loudness * jnp.repeat(jnp.exp(heights), dims[dim] // blocks).reshape((-1,) + (1,) * (len(dims) - 1 - dim))
    return loudness


def noise(rng, extent, scale, limit, cuts=(), kind=jnp.bfloat16):
    gain = shard_levels(rng, extent, cuts, -0.22, 0.18) if cuts else 1.0
    entries = jax.random.normal(rng, extent, jnp.float32) * scale * gain
    return jnp.minimum(jnp.maximum(entries, -limit), limit).astype(kind)


def setup_inputs(seed: int = 0) -> dict:
    streams_of = jax.random.split(jax.random.key(seed), 13)
    return {
        "hidden": noise(streams_of[0], (CUE_QUERY_COUNT, CUE_SAMPLE_COUNT, STRAND_SPAN, W), 1.0, 6.0, ((0, 4), (1, 2), (2, 4))),
        "bmat": noise(streams_of[1], (CUE_QUERY_COUNT, CUE_SAMPLE_COUNT, STRAND_SPAN, N), N ** -0.5, 0.5, ((0, 4), (1, 2), (2, 4))),
        "cmat": noise(streams_of[2], (CUE_QUERY_COUNT, CUE_SAMPLE_COUNT, STRAND_SPAN, N), 1.0, 6.0, ((0, 4), (1, 2), (2, 4))),
        "tokens": touch_ends(jax.random.randint(streams_of[3], (CUE_QUERY_COUNT, CUE_SAMPLE_COUNT, STRAND_SPAN), 0, VOCAB), jax.random.fold_in(streams_of[3], 1), 0, VOCAB - 1).astype(jnp.int32),
        "table": noise(streams_of[4], (VOCAB, N), N ** -0.5, 0.5, (), jnp.float32),
        "step_size": jnp.clip(jnp.exp(math.log(0.05) - 2.3025851 * jax.random.uniform(streams_of[5], (CUE_QUERY_COUNT, CUE_SAMPLE_COUNT, STRAND_SPAN, HEADS), jnp.float32) ** shard_levels(streams_of[5], (CUE_QUERY_COUNT, CUE_SAMPLE_COUNT, STRAND_SPAN, HEADS), ((0, 4), (1, 2), (2, 4)), -0.2, 0.2)), 0.005, 0.05),
        "log_decay": draw_log_decay(jax.random.fold_in(streams_of[12], 71), 0),
        "skip_gain": jnp.clip(1.0 + 0.1 * jax.random.normal(streams_of[7], (HEADS,), jnp.float32), 0.5, 1.5),
        "prev_state": noise(streams_of[8], (CUE_QUERY_COUNT, CUE_SAMPLE_COUNT, HEADS, HD, N), N ** -0.5, 0.5, ((0, 4), (1, 2), (2, 4)), jnp.float32),
        "ancestors": touch_ends(jax.random.randint(streams_of[9], (CUE_QUERY_COUNT, CUE_SAMPLE_COUNT), 0, CUE_SAMPLE_COUNT), jax.random.fold_in(streams_of[9], 1), 0, CUE_SAMPLE_COUNT - 1).astype(jnp.int32),
        "suffix_start": touch_ends(jax.random.randint(streams_of[10], (CUE_QUERY_COUNT,), STRAND_SPAN // 4, STRAND_SPAN), jax.random.fold_in(streams_of[10], 1), STRAND_SPAN // 4, STRAND_SPAN - 1).astype(jnp.int32),
        "cotangent": noise(streams_of[11], (CUE_QUERY_COUNT, CUE_SAMPLE_COUNT, STRAND_SPAN, W), 1.0, 6.0, ((0, 4), (1, 2), (2, 4))),
    }


def rounded(value):
    return lax.optimization_barrier(value.astype(jnp.bfloat16))

def product(pattern, left, right):
    return jnp.einsum(pattern, left.astype(jnp.float32), right.astype(jnp.float32))

def weigh(factor, values):
    return rounded(factor[:, :, None] * values.astype(jnp.float32))

def block_terms(hidden_rows, writer, reader, step_rows, rate_rows, grad_rows):
    cumulative = jnp.cumsum(rate_rows, axis=0)
    totals = cumulative[-1]
    scaled = rounded(step_rows[:, :, None] * hidden_rows.astype(jnp.float32))
    inner_dot = product('tn,sn->ts', reader, writer)
    across = cumulative.T
    kernel = jnp.exp(-jnp.abs(across[:, :, None] - across[:, None, :]))
    weights = rounded(kernel * inner_dot[None])
    mixed_in = product('hts,shp->thp', weights, scaled)
    back_in = product('hts,thp->shp', weights, grad_rows)
    paired = product('thp,shp->hts', grad_rows, scaled)
    crossed = rounded(lax.optimization_barrier(jnp.sum(kernel * paired, axis=0)))
    reader_in = product('ts,sn->tn', crossed, writer)
    writer_in = product('ts,tn->sn', crossed, reader)
    rising = jnp.exp(-cumulative)
    falling = jnp.exp(-(totals[None] - cumulative))
    state_end = product('shp,sn->hpn', weigh(falling, scaled), writer)
    state_begin = product('shp,sn->hpn', weigh(rising, scaled), writer)
    grad_end = product('thp,tn->hpn', weigh(falling, grad_rows), reader)
    grad_begin = product('thp,tn->hpn', weigh(rising, grad_rows), reader)
    decays = jnp.exp(-totals)
    return (mixed_in, back_in, reader_in, writer_in, rising, falling, scaled, decays, state_end, state_begin, grad_end, grad_begin)

def finish(hidden_rows, writer, reader, step_rows, grad_rows, skip_gain, block_out, state_in, state_back, grad_in, grad_back):
    mixed_in, back_in, reader_in, writer_in, rising, falling, scaled = block_out
    state_in = rounded(state_in)
    state_back = rounded(state_back)
    grad_in = rounded(grad_in)
    grad_back = rounded(grad_back)
    rise = rising[:, :, None]
    fall = falling[:, :, None]
    mixed = mixed_in + rise * product('hpn,tn->thp', state_in, reader) + fall * product('hpn,tn->thp', state_back, reader) + skip_gain[None, :, None] * hidden_rows.astype(jnp.float32)
    back = back_in + rise * product('hpn,sn->shp', grad_in, writer) + fall * product('hpn,sn->shp', grad_back, writer)
    grad_hidden = step_rows[:, :, None] * back + skip_gain[None, :, None] * grad_rows.astype(jnp.float32)
    grad_reader = reader_in + lax.optimization_barrier(jnp.sum(rise * product('thp,hpn->thn', grad_rows, state_in) + fall * product('thp,hpn->thn', grad_rows, state_back), axis=1))
    grad_writer = writer_in + lax.optimization_barrier(jnp.sum(rise * product('shp,hpn->shn', scaled, grad_in) + fall * product('shp,hpn->shn', scaled, grad_back), axis=1))
    return (mixed.astype(jnp.bfloat16), grad_hidden.astype(jnp.bfloat16), grad_reader.astype(jnp.bfloat16), grad_writer)

def reference(hidden, bmat, cmat, tokens, table, step_size, log_decay, skip_gain, prev_state, ancestors, suffix_start, cotangent):
    pair_count = CUE_QUERY_COUNT * CUE_SAMPLE_COUNT
    feature_dim = HEADS * HD
    begin_state = prev_state[jnp.arange(CUE_QUERY_COUNT)[:, None], ancestors]
    writer_all = (bmat.astype(jnp.float32) + table[tokens]).astype(jnp.bfloat16)
    symbol_site_indices = jnp.arange(STRAND_SPAN)
    live_rows = symbol_site_indices[None, :] < suffix_start[:, None]
    grad_all = jnp.where(live_rows[:, None, :, None], cotangent, jnp.zeros_like(cotangent))

    def one_pair(inputs):
        hidden_rows, writer, reader, step_rows, rate_rows, grad_rows, start_state = inputs

        def blocks(value):
            return value.reshape((N_CTX, CH) + value.shape[1:])
        pieces = (blocks(hidden_rows.reshape(STRAND_SPAN, HEADS, HD)), blocks(writer), blocks(reader), blocks(step_rows), blocks(rate_rows), blocks(grad_rows.reshape(STRAND_SPAN, HEADS, HD)))

        def run_block(members):
            return block_terms(members[0], members[1], members[2], members[3], members[4], members[5])
        block_out = lax.map(run_block, pieces)
        decays, state_end, state_begin, grad_end, grad_begin = block_out[7:]

        def advance(running, member):
            factor, addend = member
            return (factor[:, None, None] * running + addend, running)
        zero_state = jnp.zeros_like(start_state)
        _, state_in = lax.scan(advance, start_state, (decays, state_end))
        _, state_back = lax.scan(advance, zero_state, (decays, state_begin), reverse=True)
        _, grad_in = lax.scan(advance, zero_state, (decays, grad_end))
        _, grad_back = lax.scan(advance, zero_state, (decays, grad_begin), reverse=True)

        def run_finish(members):
            return finish(members[0], members[1], members[2], members[3], members[4], skip_gain, members[5], members[6], members[7], members[8], members[9])
        results = lax.map(run_finish, (pieces[0], pieces[1], pieces[2], pieces[3], pieces[5], block_out[:7], state_in, state_back, grad_in, grad_back))
        return (results[0].reshape(STRAND_SPAN, feature_dim), results[1].reshape(STRAND_SPAN, feature_dim), results[2].reshape(STRAND_SPAN, N), results[3].reshape(STRAND_SPAN, N))
    flat = (hidden.reshape(pair_count, STRAND_SPAN, feature_dim), writer_all.reshape(pair_count, STRAND_SPAN, N), cmat.reshape(pair_count, STRAND_SPAN, N), step_size.reshape(pair_count, STRAND_SPAN, HEADS), log_decay.reshape(pair_count, STRAND_SPAN, HEADS), grad_all.reshape(pair_count, STRAND_SPAN, feature_dim), begin_state.reshape(pair_count, HEADS, HD, N))
    mixed, grad_hidden, grad_cmat, grad_writer = lax.map(one_pair, flat)
    writer_scale = 1.0 / math.sqrt(HEADS * HD)
    total_scale = 1.0 / math.sqrt(CUE_QUERY_COUNT * CUE_SAMPLE_COUNT * STRAND_SPAN)
    grad_bmat = (grad_writer * writer_scale).astype(jnp.bfloat16)
    onehot = (tokens.reshape(pair_count, STRAND_SPAN)[:, :, None] == jnp.arange(VOCAB)[None, None, :]).astype(jnp.float32)
    grad_table = jnp.einsum('clv,cln->vn', onehot, grad_writer, precision=lax.Precision.HIGHEST) * (writer_scale * total_scale)
    grad_skip = product('clhp,clhp->h', hidden.reshape(pair_count, STRAND_SPAN, HEADS, HD), grad_all.reshape(pair_count, STRAND_SPAN, HEADS, HD)) * (total_scale / math.sqrt(HD))
    return (mixed.reshape(CUE_QUERY_COUNT, CUE_SAMPLE_COUNT, STRAND_SPAN, feature_dim), grad_hidden.reshape(CUE_QUERY_COUNT, CUE_SAMPLE_COUNT, STRAND_SPAN, feature_dim), grad_bmat.reshape(CUE_QUERY_COUNT, CUE_SAMPLE_COUNT, STRAND_SPAN, N), grad_cmat.reshape(CUE_QUERY_COUNT, CUE_SAMPLE_COUNT, STRAND_SPAN, N), grad_table, grad_skip)
```

```python
import functools
import math

import jax
import jax.numpy as jnp
from jax import lax
from jax.experimental import pallas as pl
from jax.experimental.pallas import tpu as pltpu
from jax.sharding import PartitionSpec as P

F32 = jnp.float32
BF16 = jnp.bfloat16
EXACT = lax.Precision.HIGHEST
NN = (((1,), (0,)), ((), ()))
NT = (((1,), (1,)), ((), ()))
TN = (((0,), (0,)), ((), ()))
CHUNKS = 4
HBM, CHIP = pltpu.HBM, pltpu.VMEM


def dot(left, right, dims=NN, precision=None):
    return lax.dot_general(
        left, right, dims, precision=precision, preferred_element_type=F32
    )


def one_hot_rows(tokens_row, rows):
    kinds = lax.broadcasted_iota(jnp.int32, (rows, tokens_row.shape[1]), 0)
    return kinds == tokens_row


def live_rows(meta, shape):
    return meta[0] + lax.broadcasted_iota(jnp.int32, shape, 0) < meta[1]


def column(cols, kind, per_chunk, head):
    at = kind * per_chunk + head
    return cols[:, at : at + 1]


STEP, RISE, FALL, CUM = range(4)


def start_kernel(
    per_chunk, head_dim, vocab, chunks,
    meta, bmat, cmat, tokens, table, step_t, rate_t, hid_far, cot_far,
    up_first, down_first, up_small, down_small, cols, writer,
    hid, cot, sems,
):
    length = bmat.shape[0]
    state = bmat.shape[1]
    part = per_chunk * head_dim
    lines = up_small.shape[1]
    copies = []
    for chunk in range(chunks):
        span = slice(chunk * part, (chunk + 1) * part)
        pair = [
            pltpu.make_async_copy(far.at[:, span], near.at[:, span], sems.at[chunk, at])
            for at, (far, near) in enumerate(((hid_far, hid), (cot_far, cot)))
        ]
        for copy in pair:
            copy.start()
        copies.append(pair)

    row = lax.broadcasted_iota(jnp.int32, (length, length), 0)
    col = lax.broadcasted_iota(jnp.int32, (length, length), 1)
    lower = jnp.where(col <= row, 1.0, 0.0).astype(F32)
    cumulative = dot(lower, rate_t[...], NT, EXACT)
    totals = cumulative[length - 1 : length, :]
    rising = jnp.exp(-cumulative)
    falling = jnp.exp(-(totals - cumulative))
    step = step_t[...].T
    for at in range(chunks):
        lo = at * per_chunk
        for kind, values in enumerate((step, rising, falling, cumulative)):
            cols[at, :, kind * per_chunk : (kind + 1) * per_chunk] = values[:, lo : lo + per_chunk]
    hot = one_hot_rows(tokens[...], vocab)
    looked = dot(jnp.where(hot, 1.0, 0.0).astype(F32), table[...], TN, EXACT)
    rows = (bmat[...].astype(F32) + looked).astype(BF16)
    writer[...] = rows
    chosen = jnp.where(one_hot_rows(tokens[...], lines), 1.0, 0.0).astype(BF16)
    kinds = lax.broadcasted_iota(jnp.int32, (lines, part), 0)
    live = live_rows(meta, (length, head_dim))
    for chunk in range(chunks):
        for copy in copies[chunk]:
            copy.wait()
        fallen, risen, grad_fallen, grad_risen, gone, skips = [], [], [], [], [], []
        for head in range(per_chunk):
            number = chunk * per_chunk + head
            at = slice(number * head_dim, (number + 1) * head_dim)
            rise = rising[:, number : number + 1]
            fall = falling[:, number : number + 1]
            values = hid[:, at].astype(F32)
            scaled = (step[:, number : number + 1] * values).astype(BF16).astype(F32)
            grads = jnp.where(live, cot[:, at].astype(F32), 0.0)
            fallen.append((fall * scaled).astype(BF16))
            risen.append((rise * scaled).astype(BF16))
            if chunk == 0:
                grad_fallen.append((fall * grads).astype(BF16))
                grad_risen.append((rise * grads).astype(BF16))
            gone.append(jnp.broadcast_to(rise[length - 1 : length, :], (1, head_dim)))
            skips.append(jnp.sum(values * grads, axis=0, keepdims=True))
        fallen, risen, gone, skips = (
            jnp.concatenate(parts, axis=1) for parts in (fallen, risen, gone, skips)
        )
        up_lines = jnp.where(
            kinds == vocab, jnp.where(meta[2] == 0, gone, 0.0), dot(chosen, fallen)
        )
        down_lines = jnp.where(
            kinds == vocab, gone, jnp.where(kinds == vocab + 1, skips, dot(chosen, risen))
        )
        up_small[chunk] = up_lines
        down_small[chunk] = down_lines
        small_rows = slice(2 * state + chunk * lines, 2 * state + (chunk + 1) * lines)
        up_first[small_rows, :] = up_lines
        down_first[small_rows, :] = down_lines
        if chunk == 0:
            writer_t, reader_t = rows.T, cmat[...].T
            up_first[0:state, :] = dot(writer_t, fallen)
            down_first[0:state, :] = dot(writer_t, risen)
            up_first[state : 2 * state, :] = dot(reader_t, jnp.concatenate(grad_fallen, axis=1))
            down_first[state : 2 * state, :] = dot(reader_t, jnp.concatenate(grad_risen, axis=1))


def combine_kernel(vocab, has_small, land, source, waits, *refs):
    meta, received, own, small, decays = refs[:5]
    send, held, near, rounded, sems = refs[-5:]
    del waits
    state = own.shape[2]
    fetch = [
        pltpu.make_async_copy(own.at[meta[source], at], near.at[at], sems.at[at])
        for at in range(2)
    ]
    for copy in fetch:
        copy.start()
    rounded[...] = received[0 : 2 * state, :].astype(BF16)
    store = pltpu.make_async_copy(rounded, held.at[meta[land]], sems.at[2])
    store.start()
    decay = decays[meta[source], vocab : vocab + 1, :]
    if has_small:
        lines = small.shape[1]
        for at in range(small.shape[0]):
            rows = slice(2 * state + at * lines, 2 * state + (at + 1) * lines)
            send[rows, :] = decays[at, vocab : vocab + 1, :] * received[rows, :] + small[at]
    for at in range(2):
        fetch[at].wait()
        rows = slice(at * state, (at + 1) * state)
        send[rows, :] = decay * received[rows, :] + near[at]
    store.wait()


def inner_kernel(
    per_chunk, head_dim, vocab,
    meta, hid, cot, writer, cmat, tokens, cols,
    up, down, mixed_in, back_in, reader_in, writer_in, tab,
    inner, inner_t, cross, writer_t, reader_t,
):
    chunk = pl.program_id(0)
    length = hid.shape[0]

    @pl.when(chunk == 0)
    def _():
        inner[...] = dot(cmat[...], writer[...], NT)
        inner_t[...] = dot(writer[...], cmat[...], NT)
        cross[...] = jnp.zeros_like(cross)
        writer_t[...] = writer[...].T
        reader_t[...] = cmat[...].T

    mine = cols[0]
    across = mine.T
    live = live_rows(meta, (length, head_dim))
    fallen, risen, grad_fallen, grad_risen = [], [], [], []
    for head in range(per_chunk):
        at = slice(head * head_dim, (head + 1) * head_dim)
        row = CUM * per_chunk + head
        decay = jnp.exp(
            -jnp.abs(column(mine, CUM, per_chunk, head) - across[row : row + 1, :])
        )
        rise = column(mine, RISE, per_chunk, head)
        fall = column(mine, FALL, per_chunk, head)
        scaled = (column(mine, STEP, per_chunk, head) * hid[:, at].astype(F32)).astype(BF16)
        grads_wide = jnp.where(live, cot[:, at].astype(F32), 0.0)
        grads = grads_wide.astype(BF16)
        scaled_wide = scaled.astype(F32)
        fallen.append((fall * scaled_wide).astype(BF16))
        risen.append((rise * scaled_wide).astype(BF16))
        grad_fallen.append((fall * grads_wide).astype(BF16))
        grad_risen.append((rise * grads_wide).astype(BF16))
        mixed_in[:, at] = dot((decay * inner[...]).astype(BF16), scaled)
        back_in[:, at] = dot((decay * inner_t[...]).astype(BF16), grads)
        cross[...] += decay * dot(grads, scaled, NT)
    up[0, 0] = dot(writer_t[...], jnp.concatenate(fallen, axis=1))
    up[0, 1] = dot(reader_t[...], jnp.concatenate(grad_fallen, axis=1))
    down[0, 0] = dot(writer_t[...], jnp.concatenate(risen, axis=1))
    down[0, 1] = dot(reader_t[...], jnp.concatenate(grad_risen, axis=1))

    @pl.when(chunk == pl.num_programs(0) - 1)
    def _():
        crossed = cross[...].astype(BF16)
        reader_in[...] = dot(crossed, writer[...])
        into = dot(crossed.astype(F32).T.astype(BF16), cmat[...])
        writer_in[...] = into
        chosen = jnp.where(one_hot_rows(tokens[...], tab.shape[0]), 1.0, 0.0).astype(F32)
        tab[...] = dot(chosen, into, precision=EXACT)


def sums_kernel(
    per_chunk, head_dim, vocab, table_scale, skip_scale,
    meta, earlier, later, small, grad_up, grad_down, tab, total, acc,
):
    chunk = pl.program_id(0)
    lines, width = earlier.shape

    @pl.when(chunk == 0)
    def _():
        acc[...] = jnp.zeros_like(acc)

    def split(lhs, rhs):
        high = lhs.astype(BF16)
        low = (lhs - high.astype(F32)).astype(BF16)
        both = dot(jnp.concatenate([high, low], axis=0), rhs.astype(BF16), NT)
        return both[0:lines] + both[lines:]

    head_of = chunk * per_chunk + lax.broadcasted_iota(jnp.int32, (128, width), 1) // head_dim
    picks = jnp.where(
        head_of == lax.broadcasted_iota(jnp.int32, (128, width), 0), 1.0, 0.0
    ).astype(F32)
    kinds = lax.broadcasted_iota(jnp.int32, (lines, 128), 0)
    tables = split(later[...], grad_up[0, 0]) + split(earlier[...], grad_down[0, 0])
    skips = jnp.broadcast_to(small[0, vocab + 1 : vocab + 2, :], (lines, width))
    acc[...] += jnp.where(kinds < vocab, tables, split(skips, picks))

    @pl.when(chunk == pl.num_programs(0) - 1)
    def _():
        total[...] = jnp.where(
            kinds < vocab,
            (acc[...] + tab[...]) * table_scale,
            jnp.where(kinds == vocab, acc[...] * skip_scale, 0.0),
        )


def finish_chunk(
    per_chunk, head_dim, vocab, meta, chunk, gains, hid, cot, writer, cmat, mine,
    mixed_in, back_in, chain_in, chain_back, begin_here, begin_there, earlier,
    mixed, grad_hidden, acc_c, acc_w,
):
    length = hid.shape[0]
    state = chain_in.shape[0] // 2
    live = live_rows(meta, (length, head_dim))
    begins = jnp.concatenate(
        [
            jnp.where(meta[3] != 0, begin_here[at], begin_there[at]).T
            for at in range(per_chunk)
        ],
        axis=1,
    )
    passed = jnp.where(meta[2] == 0, 1.0, earlier[vocab : vocab + 1, :])
    state_in = (chain_in[0:state].astype(F32) + passed * begins).astype(BF16)
    grad_in = chain_in[state:]
    state_back = chain_back[0:state]
    grad_back = chain_back[state:]
    from_in = dot(cmat, state_in)
    from_back = dot(cmat, state_back)
    grad_from_in = dot(writer, grad_in)
    grad_from_back = dot(writer, grad_back)
    fallen, risen, grad_fallen, grad_risen = [], [], [], []
    for head in range(per_chunk):
        at = slice(head * head_dim, (head + 1) * head_dim)
        rise = column(mine, RISE, per_chunk, head)
        fall = column(mine, FALL, per_chunk, head)
        step = column(mine, STEP, per_chunk, head)
        gain = gains[chunk * per_chunk + head]
        values = hid[:, at].astype(F32)
        scaled = (step * values).astype(BF16).astype(F32)
        grads = jnp.where(live, cot[:, at].astype(F32), 0.0)
        mixed[:, at] = (
            mixed_in[:, at] + rise * from_in[:, at] + fall * from_back[:, at] + gain * values
        ).astype(BF16)
        back = back_in[:, at] + rise * grad_from_in[:, at] + fall * grad_from_back[:, at]
        grad_hidden[:, at] = (step * back + gain * grads).astype(BF16)
        fallen.append((fall * scaled).astype(BF16))
        risen.append((rise * scaled).astype(BF16))
        grad_fallen.append((fall * grads).astype(BF16))
        grad_risen.append((rise * grads).astype(BF16))
    fallen, risen, grad_fallen, grad_risen = (
        jnp.concatenate(parts, axis=1) for parts in (fallen, risen, grad_fallen, grad_risen)
    )
    acc_c[...] += dot(grad_risen, state_in, NT) + dot(grad_fallen, state_back, NT)
    acc_w[...] += dot(risen, grad_in, NT) + dot(fallen, grad_back, NT)


def early_kernel(
    per_chunk, head_dim, vocab,
    meta, gains, hid, cot, writer, cmat, cols, mixed_in, back_in, reader_in, writer_in,
    held_up, held_down, begin_here, begin_there, earlier, *refs,
):
    mixed, grad_hidden, acc_c, acc_w = refs[-4:]
    chunk = pl.program_id(0)

    @pl.when(chunk == 0)
    def _():
        acc_c[...] = reader_in[...]
        acc_w[...] = writer_in[...]

    finish_chunk(
        per_chunk, head_dim, vocab, meta, chunk, gains, hid, cot, writer[...], cmat[...],
        cols[0], mixed_in, back_in, held_up[0], held_down[0], begin_here, begin_there, earlier,
        mixed, grad_hidden, acc_c, acc_w,
    )


def last_kernel(
    per_chunk, head_dim, vocab, bmat_scale, up_land, down_land, chunk,
    meta, gains, hid, cot, writer, cmat, cols, mixed_in, back_in, sum_c, sum_w,
    held_up, held_down, begin_here, begin_there, earlier, got_up, got_down, mixed_old, hidden_old,
    mixed, grad_hidden, grad_cmat, grad_bmat, acc_c, acc_w,
):
    del mixed_old, hidden_old
    acc_c[...] = sum_c[...]
    acc_w[...] = sum_w[...]
    chain_in = jnp.where(meta[up_land] == chunk, got_up[...].astype(BF16), held_up[0])
    chain_back = jnp.where(meta[down_land] == chunk, got_down[...].astype(BF16), held_down[0])
    finish_chunk(
        per_chunk, head_dim, vocab, meta, chunk, gains, hid, cot, writer[...], cmat[...],
        cols[0], mixed_in, back_in, chain_in, chain_back, begin_here, begin_there, earlier,
        mixed, grad_hidden, acc_c, acc_w,
    )
    grad_cmat[...] = acc_c[...].astype(BF16)
    grad_bmat[...] = (acc_w[...] * bmat_scale).astype(BF16)


def whole(shape):
    return pl.BlockSpec(shape, lambda *_: (0,) * len(shape))


def call(body, scalars, grid, ins, outs, scratch=(), aliases=None, limit=16 << 20):
    results = pl.pallas_call(
        body,
        out_shape=[
            jax.ShapeDtypeStruct(shape, kind) if place is None else place(shape, kind)
            for shape, kind, _, place in outs
        ],
        grid_spec=pltpu.PrefetchScalarGridSpec(
            num_scalar_prefetch=len(scalars),
            grid=grid,
            in_specs=[spec for _, spec, _ in ins],
            out_specs=[spec for _, _, spec, _ in outs],
            scratch_shapes=list(scratch),
        ),
        input_output_aliases=aliases or {},
        compiler_params=pltpu.CompilerParams(vmem_limit_bytes=limit),
    )(
        *scalars,
        *[
            array if place is None else pltpu.with_memory_space_constraint(array, place)
            for array, _, place in ins
        ],
    )
    return results


def sum_steps(axes):
    steps = []
    for axis in axes:
        count = lax.axis_size(axis)
        if count & (count - 1):
            steps.append(lambda value, axis=axis: lax.psum(value, axis))
            continue
        hop = 1
        while hop < count:
            swap = [(at, at ^ hop) for at in range(count)]
            steps.append(
                lambda value, axis=axis, swap=swap: value + lax.ppermute(value, axis, swap)
            )
            hop *= 2
    return steps


def per_device(
    hidden, bmat, cmat, tokens, table, step_size, log_decay, skip_gain,
    prev_state, ancestors, suffix_start, cotangent,
):
    prompts, parts, length, width = hidden.shape
    assert prompts * parts == 1
    heads = skip_gain.shape[0]
    head_dim = width // heads
    state_dim = bmat.shape[3]
    vocab = table.shape[0]
    count = lax.axis_size("ctx")
    doms = lax.axis_size("dom")
    place = lax.axis_index("ctx")
    chunks = CHUNKS
    per_chunk = heads // chunks
    part = width // chunks
    total_rows = length * count * doms * lax.axis_size("rep")
    bmat_scale = 1.0 / math.sqrt(width)
    total_scale = 1.0 / math.sqrt(total_rows)
    lines = -(-(vocab + 2) // 8) * 8
    slots = chunks + count - 2

    hid = hidden.reshape(length, width)
    cot = cotangent.reshape(length, width)
    writes = bmat.reshape(length, state_dim)
    reads = cmat.reshape(length, state_dim)
    toks = tokens.reshape(1, length)
    steps_t = jnp.swapaxes(step_size, 2, 3).reshape(heads, length)
    rates_t = jnp.swapaxes(log_decay, 2, 3).reshape(heads, length)
    ancestor = ancestors[0, 0]
    here = ancestor == lax.axis_index("dom")

    times = jnp.arange(slots, dtype=jnp.int32)
    from_last = count - 1 - place
    table_of = []
    for far in (place, from_last):
        lands = times - jnp.maximum(far, 1) + 1
        table_of.append(jnp.where((lands >= 0) & (lands < chunks), lands, chunks))
        table_of.append(jnp.clip(times + 1 - far, 0, chunks - 1))
    base = jnp.stack([place * length, suffix_start[0], place, here]).astype(jnp.int32)
    meta = jnp.concatenate([base] + table_of)
    up_land, up_source, down_land, down_source = (4 + at * slots for at in range(4))

    own_state = prev_state[0, 0]
    if doms == 2:
        begin_here = lax.all_gather(own_state, "ctx", tiled=True)
    else:
        own_state = lax.dynamic_index_in_dim(
            lax.all_gather(own_state, "dom"), ancestor, 0, keepdims=False
        )
        begin_here = lax.all_gather(own_state, "ctx", tiled=True)

    anywhere = pl.BlockSpec(memory_space=pl.ANY)
    near = pl.BlockSpec(memory_space=pltpu.VMEM)
    by_chunk = pl.BlockSpec((length, part), lambda k, *_: (0, k))
    one_cols = pl.BlockSpec((1, length, 128), lambda k, *_: (k, 0, 0))
    pair = pl.BlockSpec((1, 2, state_dim, part), lambda k, *_: (k, 0, 0, 0))
    one_small = pl.BlockSpec((1, lines, part), lambda k, *_: (k, 0, 0))
    square = whole((length, state_dim))
    tok_spec = whole((1, length))
    full_rows = 2 * state_dim + chunks * lines
    small_shape = (chunks, lines, part)
    first = ((full_rows, part), F32, whole((full_rows, part)), CHIP)

    up_first, down_first, up_small, down_small, cols, writer = call(
        functools.partial(start_kernel, per_chunk, head_dim, vocab, chunks),
        (meta,), (1,),
        [
            (writes, square, HBM), (reads, square, HBM), (toks, tok_spec, HBM),
            (table, whole(table.shape), HBM), (steps_t, whole(steps_t.shape), HBM),
            (rates_t, whole(rates_t.shape), HBM), (hid, anywhere, HBM), (cot, anywhere, HBM),
        ],
        [
            first, first,
            (small_shape, F32, whole(small_shape), CHIP),
            (small_shape, F32, whole(small_shape), CHIP),
            ((chunks, length, 128), F32, whole((chunks, length, 128)), HBM),
            ((length, state_dim), BF16, square, HBM),
        ],
        [
            pltpu.VMEM((length, width), BF16), pltpu.VMEM((length, width), BF16),
            pltpu.SemaphoreType.DMA((chunks, 2)),
        ],
    )

    up, down, mixed_in, back_in, reader_in, writer_in, tab = call(
        functools.partial(inner_kernel, per_chunk, head_dim, vocab),
        (meta,), (chunks,),
        [
            (hid, by_chunk, HBM), (cot, by_chunk, HBM), (writer, square, HBM),
            (reads, square, HBM), (toks, tok_spec, HBM), (cols, one_cols, HBM),
        ],
        [
            ((chunks, 2, state_dim, part), F32, pair, HBM),
            ((chunks, 2, state_dim, part), F32, pair, HBM),
            ((length, width), F32, by_chunk, HBM),
            ((length, width), F32, by_chunk, HBM),
            ((length, state_dim), F32, square, HBM),
            ((length, state_dim), F32, square, HBM),
            ((lines, state_dim), F32, whole((lines, state_dim)), HBM),
        ],
        [pltpu.VMEM((length, length), F32)] * 3 + [pltpu.VMEM((state_dim, length), BF16)] * 2,
    )

    def step_chain(slot, received, own, small, land, source, held, waits):
        has_small = slot < count - 2
        rows = full_rows if has_small else 2 * state_dim
        held_shape = (chunks + 1, 2 * state_dim, part)
        ins = [
            (received, near, CHIP), (own, anywhere, HBM), (small, near, CHIP),
            (down_small, near, CHIP),
        ]
        aliases = {}
        if held is not None:
            aliases = {1 + len(ins): 1}
            ins.append((held, anywhere, HBM))
        ins += [(value, anywhere, None) for value in waits]
        return call(
            functools.partial(
                combine_kernel, vocab, has_small, land + slot, source + slot, len(waits)
            ),
            (meta,), (), ins,
            [((rows, part), F32, near, CHIP), (held_shape, BF16, anywhere, HBM)],
            [
                pltpu.VMEM((2, state_dim, part), F32), pltpu.VMEM((2 * state_dim, part), BF16),
                pltpu.SemaphoreType.DMA((3,)),
            ],
            aliases=aliases,
        )

    upward = [(at, at + 1) for at in range(count - 1)]
    downward = [(at + 1, at) for at in range(count - 1)]
    lines_at = 2 * state_dim // lines
    from_slot = pl.BlockSpec((lines, part), lambda k, *_: (lines_at + k, 0))
    grad_part = pl.BlockSpec((1, 1, state_dim, part), lambda k, *_: (k, 1, 0, 0))
    sums = sum_steps(("rep", "dom", "ctx"))
    send_up, send_down, held_up, held_down = up_first, down_first, None, None
    begin_there = begin_here
    total = None
    for slot in range(slots):
        got_up = lax.ppermute(send_up, "ctx", upward)
        got_down = lax.ppermute(send_down, "ctx", downward)
        waits = []
        if slot == count - 2:
            earlier, later = got_up, got_down
            waits.append(begin_here)
        if slot == count - 1:
            if doms == 2:
                begin_there = lax.ppermute(begin_here, "dom", [(0, 1), (1, 0)])
            (total,) = call(
                functools.partial(
                    sums_kernel, per_chunk, head_dim, vocab,
                    bmat_scale * total_scale, total_scale / math.sqrt(head_dim),
                ),
                (meta,), (chunks,),
                [
                    (earlier, from_slot, None), (later, from_slot, None),
                    (down_small, one_small, None), (up, grad_part, HBM),
                    (down, grad_part, HBM), (tab, whole(tab.shape), HBM),
                ],
                [((lines, state_dim), F32, whole((lines, state_dim)), None)],
                [pltpu.VMEM((lines, state_dim), F32)],
            )
            waits.append(total)
        if slot >= count:
            for step in sums[:2]:
                total = step(total)
            sums = sums[2:]
            waits.append(total)
            waits.append(begin_there)
        if slot == slots - 1:
            break
        send_up, held_up = step_chain(
            slot, got_up, up, up_small, up_land, up_source, held_up, waits
        )
        send_down, held_down = step_chain(
            slot, got_down, down, down_small, down_land, down_source, held_down, []
        )

    def chunk_specs(at):
        return (
            pl.BlockSpec((length, part), lambda k, *_: (0, k + at)),
            pl.BlockSpec((1, length, 128), lambda k, *_: (k + at, 0, 0)),
            pl.BlockSpec((1, 2 * state_dim, part), lambda k, *_: (k + at, 0, 0)),
            pl.BlockSpec((per_chunk, head_dim, state_dim), lambda k, *_: (k + at, 0, 0)),
            pl.BlockSpec((lines, part), lambda k, *_: (lines_at + k + at, 0)),
        )

    def finish_ins(at, sum_c, sum_w):
        slab, col, chain, states, small = chunk_specs(at)
        return [
            (hid, slab, HBM), (cot, slab, HBM), (writer, square, HBM), (reads, square, HBM),
            (cols, col, HBM), (mixed_in, slab, HBM), (back_in, slab, HBM),
            (sum_c, square, HBM), (sum_w, square, HBM),
            (held_up, chain, HBM), (held_down, chain, HBM),
            (begin_here, states, HBM), (begin_there, states, HBM), (earlier, small, None),
        ]

    slab = chunk_specs(0)[0]
    mixed, grad_hidden, sum_c, sum_w = call(
        functools.partial(early_kernel, per_chunk, head_dim, vocab),
        (meta, skip_gain), (chunks - 1,),
        finish_ins(0, reader_in, writer_in) + [(value, anywhere, None) for value in waits[:1]],
        [
            ((length, width), BF16, slab, HBM), ((length, width), BF16, slab, HBM),
            ((length, state_dim), F32, square, HBM), ((length, state_dim), F32, square, HBM),
        ],
    )
    for step in sums:
        total = step(total)
    ins = finish_ins(chunks - 1, sum_c, sum_w) + [
        (got_up, whole(got_up.shape), None), (got_down, whole(got_down.shape), None),
        (mixed, anywhere, HBM), (grad_hidden, anywhere, HBM),
    ]
    slab = chunk_specs(chunks - 1)[0]
    mixed, grad_hidden, grad_cmat, grad_bmat = call(
        functools.partial(
            last_kernel, per_chunk, head_dim, vocab, bmat_scale,
            up_land + slots - 1, down_land + slots - 1, chunks - 1,
        ),
        (meta, skip_gain), (1,), ins,
        [
            ((length, width), BF16, slab, HBM), ((length, width), BF16, slab, HBM),
            ((length, state_dim), BF16, square, HBM), ((length, state_dim), BF16, square, HBM),
        ],
        [pltpu.VMEM((length, state_dim), F32)] * 2,
        aliases={len(ins): 0, len(ins) + 1: 1},
    )
    return (
        mixed.reshape(hidden.shape),
        grad_hidden.reshape(hidden.shape),
        grad_bmat.reshape(bmat.shape),
        grad_cmat.reshape(cmat.shape),
        total[:vocab, :],
        total[vocab, :heads],
    )


def solution(mesh):
    rows = P("rep", "dom", "ctx", None)
    return jax.shard_map(
        per_device,
        mesh=mesh,
        in_specs=(
            rows, rows, rows, P("rep", "dom", "ctx"), P(), rows, rows, P(),
            P("rep", "dom", "ctx", None, None), P("rep", "dom"), P("rep"), rows,
        ),
        out_specs=(rows, rows, rows, rows, P(), P()),
        check_vma=False,
    )
```

```python
import functools
import math

import jax
import jax.numpy as jnp
from jax import lax
from jax.experimental import pallas as pl
from jax.experimental.pallas import tpu as pltpu
from jax.sharding import PartitionSpec as P

F32 = jnp.float32
BF16 = jnp.bfloat16
EXACT = lax.Precision.HIGHEST
NN = (((1,), (0,)), ((), ()))
NT = (((1,), (1,)), ((), ()))
TN = (((0,), (0,)), ((), ()))
CHUNKS = 4
HBM, CHIP = pltpu.HBM, pltpu.VMEM


def dot(left, right, dims=NN, precision=None):
    return lax.dot_general(
        left, right, dims, precision=precision, preferred_element_type=F32
    )


def one_hot_rows(tokens_row, rows):
    kinds = lax.broadcasted_iota(jnp.int32, (rows, tokens_row.shape[1]), 0)
    return kinds == tokens_row


def live_rows(meta, shape):
    return meta[0] + lax.broadcasted_iota(jnp.int32, shape, 0) < meta[1]


def column(cols, kind, per_chunk, head):
    at = kind * per_chunk + head
    return cols[:, at : at + 1]


STEP, RISE, FALL, CUM = range(4)


def start_kernel(
    per_chunk, head_dim, vocab, chunks,
    meta, bmat, cmat, tokens, table, step_t, rate_t, hid_far, cot_far,
    up_first, down_first, up_small, down_small, cols, writer,
    hid, cot, sems,
):
    length = bmat.shape[0]
    state = bmat.shape[1]
    part = per_chunk * head_dim
    lines = up_small.shape[1]
    copies = []
    for chunk in range(chunks):
        span = slice(chunk * part, (chunk + 1) * part)
        pair = [
            pltpu.make_async_copy(far.at[:, span], near.at[:, span], sems.at[chunk, at])
            for at, (far, near) in enumerate(((hid_far, hid), (cot_far, cot)))
        ]
        for copy in pair:
            copy.start()
        copies.append(pair)

    row = lax.broadcasted_iota(jnp.int32, (length, length), 0)
    col = lax.broadcasted_iota(jnp.int32, (length, length), 1)
    lower = jnp.where(col <= row, 1.0, 0.0).astype(F32)
    cumulative = dot(lower, rate_t[...], NT, EXACT)
    totals = cumulative[length - 1 : length, :]
    rising = jnp.exp(-cumulative)
    falling = jnp.exp(-(totals - cumulative))
    step = step_t[...].T
    for at in range(chunks):
        lo = at * per_chunk
        for kind, values in enumerate((step, rising, falling, cumulative)):
            cols[at, :, kind * per_chunk : (kind + 1) * per_chunk] = values[:, lo : lo + per_chunk]
    hot = one_hot_rows(tokens[...], vocab)
    looked = dot(jnp.where(hot, 1.0, 0.0).astype(F32), table[...], TN, EXACT)
    rows = (bmat[...].astype(F32) + looked).astype(BF16)
    writer[...] = rows
    chosen = jnp.where(one_hot_rows(tokens[...], lines), 1.0, 0.0).astype(BF16)
    kinds = lax.broadcasted_iota(jnp.int32, (lines, part), 0)
    live = live_rows(meta, (length, head_dim))
    for chunk in range(chunks):
        for copy in copies[chunk]:
            copy.wait()
        fallen, risen, grad_fallen, grad_risen, gone, skips = [], [], [], [], [], []
        for head in range(per_chunk):
            number = chunk * per_chunk + head
            at = slice(number * head_dim, (number + 1) * head_dim)
            rise = rising[:, number : number + 1]
            fall = falling[:, number : number + 1]
            values = hid[:, at].astype(F32)
            scaled = (step[:, number : number + 1] * values).astype(BF16).astype(F32)
            grads = jnp.where(live, cot[:, at].astype(F32), 0.0)
            fallen.append((fall * scaled).astype(BF16))
            risen.append((rise * scaled).astype(BF16))
            if chunk == 0:
                grad_fallen.append((fall * grads).astype(BF16))
                grad_risen.append((rise * grads).astype(BF16))
            gone.append(jnp.broadcast_to(rise[length - 1 : length, :], (1, head_dim)))
            skips.append(jnp.sum(values * grads, axis=0, keepdims=True))
        fallen, risen, gone, skips = (
            jnp.concatenate(parts, axis=1) for parts in (fallen, risen, gone, skips)
        )
        up_lines = jnp.where(
            kinds == vocab, jnp.where(meta[2] == 0, gone, 0.0), dot(chosen, fallen)
        )
        down_lines = jnp.where(
            kinds == vocab, gone, jnp.where(kinds == vocab + 1, skips, dot(chosen, risen))
        )
        up_small[chunk] = up_lines
        down_small[chunk] = down_lines
        small_rows = slice(2 * state + chunk * lines, 2 * state + (chunk + 1) * lines)
        up_first[small_rows, :] = up_lines
        down_first[small_rows, :] = down_lines
        if chunk == 0:
            writer_t, reader_t = rows.T, cmat[...].T
            up_first[0:state, :] = dot(writer_t, fallen)
            down_first[0:state, :] = dot(writer_t, risen)
            up_first[state : 2 * state, :] = dot(reader_t, jnp.concatenate(grad_fallen, axis=1))
            down_first[state : 2 * state, :] = dot(reader_t, jnp.concatenate(grad_risen, axis=1))


def head_copies(source, target, row, sems):
    heads, rows, width = source.shape
    return [
        pltpu.make_async_copy(
            source.at[head],
            target.at[pl.ds(row, rows), pl.ds(head * width, width)],
            sems.at[head],
        )
        for head in range(heads)
    ]


def relay_kernel(last, meta, from_before, from_after, up_old, down_old, up, down, sems):
    del up_old, down_old
    for at, (source, target) in enumerate(((from_before, up), (from_after, down))):
        copies = head_copies(source, target, 0, sems.at[at])

        @pl.when(meta[2] != (0, last)[at])
        def _():
            for copy in copies:
                copy.start()
            for copy in copies:
                copy.wait()


def gather_kernel(last, meta, own, from_before, from_after, begin, sems):
    place = meta[2]
    trash = last + 1
    copies = []
    for at, (source, row) in enumerate((
        (own, place),
        (from_before, jnp.where(place == 0, trash, place - 1)),
        (from_after, place + 1),
    )):
        copies += head_copies(source, begin.at[row], 0, sems.at[at])
    for copy in copies:
        copy.start()
    for copy in copies:
        copy.wait()


def combine_kernel(vocab, has_small, has_begin, slot, tables, waits, *refs):
    meta, received, own, small, decays = refs[:5]
    near, rounded, sems = refs[-3:]
    send, held = refs[-6:-4] if has_begin else refs[-5:-3]
    del waits
    state = own.shape[2]
    land, source, forward, piece = (at + slot for at in tables)
    fetch = [
        pltpu.make_async_copy(own.at[meta[source], at], near.at[at], sems.at[at])
        for at in range(2)
    ]
    for copy in fetch:
        copy.start()
    stores = []
    if has_begin:
        begin = refs[-4]
        stores.append(
            pltpu.make_async_copy(
                received.at[0:state, 0 : begin.shape[2]], begin.at[meta[piece]], sems.at[3]
            )
        )
        stores[-1].start()
    rounded[...] = received[0 : 2 * state, :].astype(BF16)
    stores.append(pltpu.make_async_copy(rounded, held.at[meta[land]], sems.at[2]))
    stores[-1].start()
    passing = meta[forward] != 0
    decay = jnp.where(passing, 1.0, decays[meta[source], vocab : vocab + 1, :])
    adding = jnp.where(passing, 0.0, 1.0)
    if has_small:
        lines = small.shape[1]
        for at in range(small.shape[0]):
            rows = slice(2 * state + at * lines, 2 * state + (at + 1) * lines)
            send[rows, :] = decays[at, vocab : vocab + 1, :] * received[rows, :] + small[at]
    for at in range(2):
        fetch[at].wait()
        rows = slice(at * state, (at + 1) * state)
        send[rows, :] = decay * received[rows, :] + adding * near[at]
    for store in stores:
        store.wait()


def inner_kernel(
    per_chunk, head_dim, vocab,
    meta, hid, cot, writer, cmat, tokens, cols,
    up, down, mixed_in, back_in, reader_in, writer_in, tab,
    inner, inner_t, cross, writer_t, reader_t,
):
    chunk = pl.program_id(0)
    length = hid.shape[0]

    @pl.when(chunk == 0)
    def _():
        inner[...] = dot(cmat[...], writer[...], NT)
        inner_t[...] = dot(writer[...], cmat[...], NT)
        cross[...] = jnp.zeros_like(cross)
        writer_t[...] = writer[...].T
        reader_t[...] = cmat[...].T

    mine = cols[0]
    across = mine.T
    live = live_rows(meta, (length, head_dim))
    fallen, risen, grad_fallen, grad_risen = [], [], [], []
    for head in range(per_chunk):
        at = slice(head * head_dim, (head + 1) * head_dim)
        row = CUM * per_chunk + head
        decay = jnp.exp(
            -jnp.abs(column(mine, CUM, per_chunk, head) - across[row : row + 1, :])
        )
        rise = column(mine, RISE, per_chunk, head)
        fall = column(mine, FALL, per_chunk, head)
        scaled = (column(mine, STEP, per_chunk, head) * hid[:, at].astype(F32)).astype(BF16)
        grads_wide = jnp.where(live, cot[:, at].astype(F32), 0.0)
        grads = grads_wide.astype(BF16)
        scaled_wide = scaled.astype(F32)
        fallen.append((fall * scaled_wide).astype(BF16))
        risen.append((rise * scaled_wide).astype(BF16))
        grad_fallen.append((fall * grads_wide).astype(BF16))
        grad_risen.append((rise * grads_wide).astype(BF16))
        mixed_in[:, at] = dot((decay * inner[...]).astype(BF16), scaled)
        back_in[:, at] = dot((decay * inner_t[...]).astype(BF16), grads)
        cross[...] += decay * dot(grads, scaled, NT)
    up[0, 0] = dot(writer_t[...], jnp.concatenate(fallen, axis=1))
    up[0, 1] = dot(reader_t[...], jnp.concatenate(grad_fallen, axis=1))
    down[0, 0] = dot(writer_t[...], jnp.concatenate(risen, axis=1))
    down[0, 1] = dot(reader_t[...], jnp.concatenate(grad_risen, axis=1))

    @pl.when(chunk == pl.num_programs(0) - 1)
    def _():
        crossed = cross[...].astype(BF16)
        reader_in[...] = dot(crossed, writer[...])
        into = dot(crossed.astype(F32).T.astype(BF16), cmat[...])
        writer_in[...] = into
        chosen = jnp.where(one_hot_rows(tokens[...], tab.shape[0]), 1.0, 0.0).astype(F32)
        tab[...] = dot(chosen, into, precision=EXACT)


def sums_kernel(
    per_chunk, head_dim, vocab, table_scale, skip_scale,
    meta, earlier, later, small, grad_up, grad_down, tab, total, acc,
):
    chunk = pl.program_id(0)
    lines, width = earlier.shape

    @pl.when(chunk == 0)
    def _():
        acc[...] = jnp.zeros_like(acc)

    def split(lhs, rhs):
        high = lhs.astype(BF16)
        low = (lhs - high.astype(F32)).astype(BF16)
        both = dot(jnp.concatenate([high, low], axis=0), rhs.astype(BF16), NT)
        return both[0:lines] + both[lines:]

    head_of = chunk * per_chunk + lax.broadcasted_iota(jnp.int32, (128, width), 1) // head_dim
    picks = jnp.where(
        head_of == lax.broadcasted_iota(jnp.int32, (128, width), 0), 1.0, 0.0
    ).astype(F32)
    kinds = lax.broadcasted_iota(jnp.int32, (lines, 128), 0)
    tables = split(later[...], grad_up[0, 0]) + split(earlier[...], grad_down[0, 0])
    skips = jnp.broadcast_to(small[0, vocab + 1 : vocab + 2, :], (lines, width))
    acc[...] += jnp.where(kinds < vocab, tables, split(skips, picks))

    @pl.when(chunk == pl.num_programs(0) - 1)
    def _():
        total[...] = jnp.where(
            kinds < vocab,
            (acc[...] + tab[...]) * table_scale,
            jnp.where(kinds == vocab, acc[...] * skip_scale, 0.0),
        )


def finish_chunk(
    per_chunk, head_dim, vocab, meta, chunk, gains, hid, cot, writer, cmat, mine,
    mixed_in, back_in, chain_in, chain_back, begin_here, begin_there, earlier,
    mixed, grad_hidden, acc_c, acc_w,
):
    length = hid.shape[0]
    state = chain_in.shape[0] // 2
    live = live_rows(meta, (length, head_dim))
    begins = []
    for at in range(begin_here.shape[0]):
        value = jnp.where(meta[3] != 0, begin_here[at], begin_there[at])
        for lane in range(0, value.shape[1], state):
            begins.append(value[:, lane : lane + state].T)
    begins = jnp.concatenate(begins, axis=1)
    passed = jnp.where(meta[2] == 0, 1.0, earlier[vocab : vocab + 1, :])
    state_in = (chain_in[0:state].astype(F32) + passed * begins).astype(BF16)
    grad_in = chain_in[state:]
    state_back = chain_back[0:state]
    grad_back = chain_back[state:]
    from_in = dot(cmat, state_in)
    from_back = dot(cmat, state_back)
    grad_from_in = dot(writer, grad_in)
    grad_from_back = dot(writer, grad_back)
    fallen, risen, grad_fallen, grad_risen = [], [], [], []
    for head in range(per_chunk):
        at = slice(head * head_dim, (head + 1) * head_dim)
        rise = column(mine, RISE, per_chunk, head)
        fall = column(mine, FALL, per_chunk, head)
        step = column(mine, STEP, per_chunk, head)
        gain = gains[chunk * per_chunk + head]
        values = hid[:, at].astype(F32)
        scaled = (step * values).astype(BF16).astype(F32)
        grads = jnp.where(live, cot[:, at].astype(F32), 0.0)
        mixed[:, at] = (
            mixed_in[:, at] + rise * from_in[:, at] + fall * from_back[:, at] + gain * values
        ).astype(BF16)
        back = back_in[:, at] + rise * grad_from_in[:, at] + fall * grad_from_back[:, at]
        grad_hidden[:, at] = (step * back + gain * grads).astype(BF16)
        fallen.append((fall * scaled).astype(BF16))
        risen.append((rise * scaled).astype(BF16))
        grad_fallen.append((fall * grads).astype(BF16))
        grad_risen.append((rise * grads).astype(BF16))
    fallen, risen, grad_fallen, grad_risen = (
        jnp.concatenate(parts, axis=1) for parts in (fallen, risen, grad_fallen, grad_risen)
    )
    acc_c[...] += dot(grad_risen, state_in, NT) + dot(grad_fallen, state_back, NT)
    acc_w[...] += dot(risen, grad_in, NT) + dot(fallen, grad_back, NT)


def early_kernel(
    per_chunk, head_dim, vocab,
    meta, gains, hid, cot, writer, cmat, cols, mixed_in, back_in, reader_in, writer_in,
    held_up, held_down, begin_here, begin_there, earlier, *refs,
):
    mixed, grad_hidden, acc_c, acc_w = refs[-5:-1]
    chunk = pl.program_id(0)

    @pl.when(chunk == 0)
    def _():
        acc_c[...] = reader_in[...]
        acc_w[...] = writer_in[...]

    finish_chunk(
        per_chunk, head_dim, vocab, meta, chunk, gains, hid, cot, writer[...], cmat[...],
        cols[0], mixed_in, back_in, held_up[0], held_down[0], begin_here, begin_there, earlier,
        mixed, grad_hidden, acc_c, acc_w,
    )


def last_kernel(
    per_chunk, head_dim, vocab, bmat_scale, up_land, down_land, chunk,
    meta, gains, hid, cot, writer, cmat, cols, mixed_in, back_in, sum_c, sum_w,
    held_up, held_down, begin_here, begin_there, earlier, got_up, got_down, *refs,
):
    sums = refs[2:-8]
    mixed, grad_hidden, grad_cmat, grad_bmat, grad_table, grad_skip, acc_c, acc_w = refs[-8:]
    total = sums[0][...]
    for value in sums[1:]:
        total = total + value[...]
    vocab_rows, heads = grad_table.shape[0], grad_skip.shape[1]
    grad_table[...] = total[0:vocab_rows, :]
    grad_skip[...] = total[vocab_rows : vocab_rows + 1, 0:heads]
    acc_c[...] = sum_c[...]
    acc_w[...] = sum_w[...]
    chain_in = jnp.where(meta[up_land] == chunk, got_up[...].astype(BF16), held_up[0])
    chain_back = jnp.where(meta[down_land] == chunk, got_down[...].astype(BF16), held_down[0])
    finish_chunk(
        per_chunk, head_dim, vocab, meta, chunk, gains, hid, cot, writer[...], cmat[...],
        cols[0], mixed_in, back_in, chain_in, chain_back, begin_here, begin_there, earlier,
        mixed, grad_hidden, acc_c, acc_w,
    )
    grad_cmat[...] = acc_c[...].astype(BF16)
    grad_bmat[...] = (acc_w[...] * bmat_scale).astype(BF16)


def whole(shape):
    return pl.BlockSpec(shape, lambda *_: (0,) * len(shape))


def call(body, scalars, grid, ins, outs, scratch=(), aliases=None, limit=16 << 20):
    results = pl.pallas_call(
        body,
        out_shape=[
            jax.ShapeDtypeStruct(shape, kind) if place is None else place(shape, kind)
            for shape, kind, _, place in outs
        ],
        grid_spec=pltpu.PrefetchScalarGridSpec(
            num_scalar_prefetch=len(scalars),
            grid=grid,
            in_specs=[spec for _, spec, _ in ins],
            out_specs=[spec for _, _, spec, _ in outs],
            scratch_shapes=list(scratch),
        ),
        input_output_aliases=aliases or {},
        compiler_params=pltpu.CompilerParams(vmem_limit_bytes=limit),
    )(
        *scalars,
        *[
            array if place is None else pltpu.with_memory_space_constraint(array, place)
            for array, _, place in ins
        ],
    )
    return results


def sum_steps(axes):
    steps, last = [], []
    for axis in axes:
        count = lax.axis_size(axis)
        if count & (count - 1):
            steps.append(functools.partial(lax.psum, axis_name=axis))
            continue
        hop = 1
        while hop < count:
            hops = [hop]
            if axis == axes[-1] and 4 * hop >= count:
                hops = range(hop, count, hop)
            group = [
                functools.partial(
                    lax.ppermute, axis_name=axis, perm=[(at, at ^ far) for at in range(count)]
                )
                for far in hops
            ]
            if axis == axes[-1] and 4 * hop >= count:
                last = group
                break
            steps.append(lambda value, group=group: value + group[0](value))
            hop *= 2
    return steps, last


def per_device(
    hidden, bmat, cmat, tokens, table, step_size, log_decay, skip_gain,
    prev_state, ancestors, suffix_start, cotangent,
):
    prompts, parts, length, width = hidden.shape
    assert prompts * parts == 1
    heads = skip_gain.shape[0]
    head_dim = width // heads
    state_dim = bmat.shape[3]
    vocab = table.shape[0]
    count = lax.axis_size("ctx")
    doms = lax.axis_size("dom")
    place = lax.axis_index("ctx")
    chunks = CHUNKS
    per_chunk = heads // chunks
    part = width // chunks
    total_rows = length * count * doms * lax.axis_size("rep")
    bmat_scale = 1.0 / math.sqrt(width)
    total_scale = 1.0 / math.sqrt(total_rows)
    lines = -(-(vocab + 2) // 8) * 8
    slots = chunks + count - 2

    hid = hidden.reshape(length, width)
    cot = cotangent.reshape(length, width)
    writes = bmat.reshape(length, state_dim)
    reads = cmat.reshape(length, state_dim)
    toks = tokens.reshape(1, length)
    steps_t = jnp.swapaxes(step_size, 2, 3).reshape(heads, length)
    rates_t = jnp.swapaxes(log_decay, 2, 3).reshape(heads, length)
    ancestor = ancestors[0, 0]
    here = ancestor == lax.axis_index("dom")

    times = jnp.arange(slots, dtype=jnp.int32)
    from_last = count - 1 - place
    table_of = []
    for far, toward in ((place, -1), (from_last, 1)):
        lands = times - jnp.maximum(far, 1) + 1
        pieces = place + toward * (times + 2)
        table_of.append(jnp.where((lands >= 0) & (lands < chunks), lands, chunks))
        table_of.append(jnp.clip(times + 1 - far, 0, chunks - 1))
        table_of.append((times + 1 < far).astype(jnp.int32))
        table_of.append(jnp.where((pieces >= 0) & (pieces < count), pieces, count))
    base = jnp.stack([place * length, suffix_start[0], place, here]).astype(jnp.int32)
    meta = jnp.concatenate([base] + table_of)
    up_tables = [4 + at * slots for at in range(4)]
    down_tables = [4 + at * slots for at in range(4, 8)]

    upward = [(at, at + 1) for at in range(count - 1)]
    downward = [(at + 1, at) for at in range(count - 1)]
    own_state = prev_state[0, 0]
    local_heads = own_state.shape[0]
    assert per_chunk % local_heads == 0
    if doms != 2:
        own_state = lax.dynamic_index_in_dim(
            lax.all_gather(own_state, "dom"), ancestor, 0, keepdims=False
        )
    from_before = lax.ppermute(own_state, "ctx", upward)
    from_after = lax.ppermute(own_state, "ctx", downward)

    anywhere = pl.BlockSpec(memory_space=pl.ANY)
    near = pl.BlockSpec(memory_space=pltpu.VMEM)
    by_chunk = pl.BlockSpec((length, part), lambda k, *_: (0, k))
    one_cols = pl.BlockSpec((1, length, 128), lambda k, *_: (k, 0, 0))
    pair = pl.BlockSpec((1, 2, state_dim, part), lambda k, *_: (k, 0, 0, 0))
    one_small = pl.BlockSpec((1, lines, part), lambda k, *_: (k, 0, 0))
    square = whole((length, state_dim))
    tok_spec = whole((1, length))
    full_rows = 2 * state_dim + chunks * lines
    small_shape = (chunks, lines, part)
    first = ((full_rows, part), F32, whole((full_rows, part)), CHIP)

    up_first, down_first, up_small, down_small, cols, writer = call(
        functools.partial(start_kernel, per_chunk, head_dim, vocab, chunks),
        (meta,), (1,),
        [
            (writes, square, HBM), (reads, square, HBM), (toks, tok_spec, HBM),
            (table, whole(table.shape), HBM), (steps_t, whole(steps_t.shape), HBM),
            (rates_t, whole(rates_t.shape), HBM), (hid, anywhere, HBM), (cot, anywhere, HBM),
        ],
        [
            first, first,
            (small_shape, F32, whole(small_shape), CHIP),
            (small_shape, F32, whole(small_shape), CHIP),
            ((chunks, length, 128), F32, whole((chunks, length, 128)), HBM),
            ((length, state_dim), BF16, square, HBM),
        ],
        [
            pltpu.VMEM((length, width), BF16), pltpu.VMEM((length, width), BF16),
            pltpu.SemaphoreType.DMA((chunks, 2)),
        ],
    )

    up_first, down_first = call(
        functools.partial(relay_kernel, count - 1),
        (meta,), (),
        [
            (from_before, anywhere, None), (from_after, anywhere, None),
            (up_first, near, CHIP), (down_first, near, CHIP),
        ],
        [
            ((full_rows, part), F32, near, CHIP), ((full_rows, part), F32, near, CHIP),
        ],
        [pltpu.SemaphoreType.DMA((2, local_heads))],
        aliases={3: 0, 4: 1},
    )
    begin_shape = (count + 1, head_dim, local_heads * state_dim)
    (begin_here,) = call(
        functools.partial(gather_kernel, count - 1),
        (meta,), (),
        [
            (own_state, anywhere, None), (from_before, anywhere, None),
            (from_after, anywhere, None),
        ],
        [(begin_shape, F32, anywhere, HBM)],
        [pltpu.SemaphoreType.DMA((3, local_heads))],
    )

    up, down, mixed_in, back_in, reader_in, writer_in, tab = call(
        functools.partial(inner_kernel, per_chunk, head_dim, vocab),
        (meta,), (chunks,),
        [
            (hid, by_chunk, HBM), (cot, by_chunk, HBM), (writer, square, HBM),
            (reads, square, HBM), (toks, tok_spec, HBM), (cols, one_cols, HBM),
        ],
        [
            ((chunks, 2, state_dim, part), F32, pair, HBM),
            ((chunks, 2, state_dim, part), F32, pair, HBM),
            ((length, width), F32, by_chunk, HBM),
            ((length, width), F32, by_chunk, HBM),
            ((length, state_dim), F32, square, HBM),
            ((length, state_dim), F32, square, HBM),
            ((lines, state_dim), F32, whole((lines, state_dim)), HBM),
        ],
        [pltpu.VMEM((length, length), F32)] * 3 + [pltpu.VMEM((state_dim, length), BF16)] * 2,
    )

    def step_chain(slot, received, own, small, tables, held, begin, waits):
        has_small = slot < count - 2
        has_begin = slot < count - 2
        rows = full_rows if has_small else 2 * state_dim
        held_shape = (chunks + 1, 2 * state_dim, part)
        ins = [
            (received, near, CHIP), (own, anywhere, HBM), (small, near, CHIP),
            (down_small, near, CHIP),
        ]
        outs = [((rows, part), F32, near, CHIP), (held_shape, BF16, anywhere, HBM)]
        aliases = {}
        if held is not None:
            aliases[1 + len(ins)] = 1
            ins.append((held, anywhere, HBM))
        if has_begin:
            aliases[1 + len(ins)] = 2
            ins.append((begin, anywhere, HBM))
            outs.append((begin_shape, F32, anywhere, HBM))
        ins += [(value, anywhere, None) for value in waits]
        results = call(
            functools.partial(
                combine_kernel, vocab, has_small, has_begin, slot, tables, len(waits)
            ),
            (meta,), (), ins, outs,
            [
                pltpu.VMEM((2, state_dim, part), F32), pltpu.VMEM((2 * state_dim, part), BF16),
                pltpu.SemaphoreType.DMA((4,)),
            ],
            aliases=aliases,
        )
        return results if has_begin else (*results, begin)

    lines_at = 2 * state_dim // lines
    from_slot = pl.BlockSpec((lines, part), lambda k, *_: (lines_at + k, 0))
    grad_part = pl.BlockSpec((1, 1, state_dim, part), lambda k, *_: (k, 1, 0, 0))
    sums, exchanges = sum_steps(("rep", "dom", "ctx"))
    send_up, send_down, held_up, held_down = up_first, down_first, None, None
    for slot in range(slots):
        first_place = max(0, slot - chunks + 1)
        got_down = lax.ppermute(
            send_down, "ctx", [(count - 1 - at, count - 2 - at) for at in range(first_place, count - 1)]
        )
        got_up = lax.ppermute(send_up, "ctx", upward[first_place:])
        waits_up, waits_down = [], []
        if slot == count - 2:
            earlier, later = got_up, got_down
        if slot == count - 1:
            begin_there = begin_here
            if doms == 2:
                begin_there = lax.ppermute(begin_here, "dom", [(0, 1), (1, 0)])
            (total,) = call(
                functools.partial(
                    sums_kernel, per_chunk, head_dim, vocab,
                    bmat_scale * total_scale, total_scale / math.sqrt(head_dim),
                ),
                (meta,), (chunks,),
                [
                    (earlier, from_slot, None), (later, from_slot, None),
                    (down_small, one_small, None), (up, grad_part, HBM),
                    (down, grad_part, HBM), (tab, whole(tab.shape), HBM),
                ],
                [((lines, state_dim), F32, whole((lines, state_dim)), None)],
                [pltpu.VMEM((lines, state_dim), F32)],
            )
        if slot == slots - 1:
            break
        if slot >= count - 1:
            if slot > count - 1:
                waits_down.append(begin_there)
                for step in sums[:1]:
                    total = step(total)
                sums = sums[1:]
            waits_down.append(total)
        send_down, held_down, begin_here = step_chain(
            slot, got_down, down, down_small, down_tables, held_down, begin_here, waits_down
        )
        if slot >= count - 1:
            for step in sums[:1]:
                total = step(total)
            sums = sums[1:]
            waits_up.append(total)
        send_up, held_up, begin_here = step_chain(
            slot, got_up, up, up_small, up_tables, held_up, begin_here, waits_up
        )

    def chunk_specs(at):
        return (
            pl.BlockSpec((length, part), lambda k, *_: (0, k + at)),
            pl.BlockSpec((1, length, 128), lambda k, *_: (k + at, 0, 0)),
            pl.BlockSpec((1, 2 * state_dim, part), lambda k, *_: (k + at, 0, 0)),
            pl.BlockSpec(
                (per_chunk // local_heads, head_dim, local_heads * state_dim),
                lambda k, *_: (k + at, 0, 0),
            ),
            pl.BlockSpec((lines, part), lambda k, *_: (lines_at + k + at, 0)),
        )

    def finish_ins(at, sum_c, sum_w):
        slab, col, chain, states, small = chunk_specs(at)
        return [
            (hid, slab, HBM), (cot, slab, HBM), (writer, square, HBM), (reads, square, HBM),
            (cols, col, HBM), (mixed_in, slab, HBM), (back_in, slab, HBM),
            (sum_c, square, HBM), (sum_w, square, HBM),
            (held_up, chain, HBM), (held_down, chain, HBM),
            (begin_here, states, HBM), (begin_there, states, HBM), (earlier, small, None),
        ]

    for step in sums:
        total = step(total)
    slab = chunk_specs(0)[0]
    mixed, grad_hidden, sum_c, sum_w, total = call(
        functools.partial(early_kernel, per_chunk, head_dim, vocab),
        (meta, skip_gain), (chunks - 1,),
        finish_ins(0, reader_in, writer_in) + [(total, anywhere, None)],
        [
            ((length, width), BF16, slab, HBM), ((length, width), BF16, slab, HBM),
            ((length, state_dim), F32, square, HBM), ((length, state_dim), F32, square, HBM),
            (total.shape, F32, anywhere, None),
        ],
        aliases={16: 4},
    )
    exchanged = [exchange(total) for exchange in exchanges]
    ins = finish_ins(chunks - 1, sum_c, sum_w) + [
        (got_up, whole(got_up.shape), None), (got_down, whole(got_down.shape), None),
        (mixed, anywhere, HBM), (grad_hidden, anywhere, HBM),
    ] + [(value, whole(value.shape), None) for value in [total] + exchanged]
    slab = chunk_specs(chunks - 1)[0]
    mixed, grad_hidden, grad_cmat, grad_bmat, grad_table, grad_skip = call(
        functools.partial(
            last_kernel, per_chunk, head_dim, vocab, bmat_scale,
            up_tables[0] + slots - 1, down_tables[0] + slots - 1, chunks - 1,
        ),
        (meta, skip_gain), (1,), ins,
        [
            ((length, width), BF16, slab, HBM), ((length, width), BF16, slab, HBM),
            ((length, state_dim), BF16, square, HBM), ((length, state_dim), BF16, square, HBM),
            (table.shape, F32, whole(table.shape), HBM),
            ((1, heads), F32, whole((1, heads)), HBM),
        ],
        [pltpu.VMEM((length, state_dim), F32)] * 2,
        aliases={18: 0, 19: 1},
    )
    return (
        mixed.reshape(hidden.shape),
        grad_hidden.reshape(hidden.shape),
        grad_bmat.reshape(bmat.shape),
        grad_cmat.reshape(cmat.shape),
        grad_table,
        grad_skip.reshape(heads),
    )


def solution(mesh):
    rows = P("rep", "dom", "ctx", None)
    return jax.shard_map(
        per_device,
        mesh=mesh,
        in_specs=(
            rows, rows, rows, P("rep", "dom", "ctx"), P(), rows, rows, P(),
            P("rep", "dom", "ctx", None, None), P("rep", "dom"), P("rep"), rows,
        ),
        out_specs=(rows, rows, rows, rows, P(), P()),
        check_vma=False,
    )
```

```python
import functools
import math

import jax
import jax.numpy as jnp
from jax import lax
from jax.experimental import pallas as pl
from jax.experimental.pallas import tpu as pltpu
from jax.sharding import PartitionSpec as P

F32 = jnp.float32
BF16 = jnp.bfloat16
EXACT = lax.Precision.HIGHEST
NN = (((1,), (0,)), ((), ()))
NT = (((1,), (1,)), ((), ()))
TN = (((0,), (0,)), ((), ()))
CHUNKS = 4
HBM, CHIP = pltpu.HBM, pltpu.VMEM


def dot(left, right, dims=NN, precision=None):
    return lax.dot_general(
        left, right, dims, precision=precision, preferred_element_type=F32
    )


def one_hot_rows(tokens_row, rows):
    kinds = lax.broadcasted_iota(jnp.int32, (rows, tokens_row.shape[1]), 0)
    return kinds == tokens_row


def live_rows(meta, shape):
    return meta[0] + lax.broadcasted_iota(jnp.int32, shape, 0) < meta[1]


def column(cols, kind, per_chunk, head):
    at = kind * per_chunk + head
    return cols[:, at : at + 1]


STEP, RISE, FALL, CUM = range(4)


def start_kernel(
    per_chunk, head_dim, vocab, chunks,
    meta, bmat, cmat, tokens, table, step_t, rate_t, hid_far, cot_far,
    up_first, down_first, up_small, down_small, cols, writer, hid, cot, sems,
):
    length = bmat.shape[0]
    state = bmat.shape[1]
    part = per_chunk * head_dim
    lines = up_small.shape[1]
    copies = []
    for chunk in range(chunks):
        span = slice(chunk * part, (chunk + 1) * part)
        pair = [
            pltpu.make_async_copy(far.at[:, span], near.at[:, span], sems.at[chunk, at])
            for at, (far, near) in enumerate(((hid_far, hid), (cot_far, cot)))
        ]
        for copy in pair:
            copy.start()
        copies.append(pair)

    row = lax.broadcasted_iota(jnp.int32, (length, length), 0)
    col = lax.broadcasted_iota(jnp.int32, (length, length), 1)
    lower = jnp.where(col <= row, 1.0, 0.0).astype(F32)
    cumulative = dot(lower, rate_t[...], NT, EXACT)
    totals = cumulative[length - 1 : length, :]
    rising = jnp.exp(-cumulative)
    falling = jnp.exp(-(totals - cumulative))
    step = step_t[...].T
    for at in range(chunks):
        lo = at * per_chunk
        for kind, values in enumerate((step, rising, falling, cumulative)):
            cols[at, :, kind * per_chunk : (kind + 1) * per_chunk] = values[:, lo : lo + per_chunk]
    hot = one_hot_rows(tokens[...], vocab)
    looked = dot(jnp.where(hot, 1.0, 0.0).astype(F32), table[...], TN, EXACT)
    rows = (bmat[...].astype(F32) + looked).astype(BF16)
    writer[...] = rows
    chosen = jnp.where(one_hot_rows(tokens[...], lines), 1.0, 0.0).astype(BF16)
    kinds = lax.broadcasted_iota(jnp.int32, (lines, part), 0)
    live = live_rows(meta, (length, head_dim))
    for chunk in range(chunks):
        for copy in copies[chunk]:
            copy.wait()
        fallen, risen, grad_fallen, grad_risen, gone, skips = [], [], [], [], [], []
        for head in range(per_chunk):
            number = chunk * per_chunk + head
            at = slice(number * head_dim, (number + 1) * head_dim)
            rise = rising[:, number : number + 1]
            fall = falling[:, number : number + 1]
            values = hid[:, at].astype(F32)
            scaled = (step[:, number : number + 1] * values).astype(BF16).astype(F32)
            grads = jnp.where(live, cot[:, at].astype(F32), 0.0)
            fallen.append((fall * scaled).astype(BF16))
            risen.append((rise * scaled).astype(BF16))
            if chunk == 0:
                grad_fallen.append((fall * grads).astype(BF16))
                grad_risen.append((rise * grads).astype(BF16))
            gone.append(jnp.broadcast_to(rise[length - 1 : length, :], (1, head_dim)))
            skips.append(jnp.sum(values * grads, axis=0, keepdims=True))
        fallen, risen, gone, skips = (
            jnp.concatenate(parts, axis=1) for parts in (fallen, risen, gone, skips)
        )
        up_lines = jnp.where(
            kinds == vocab, jnp.where(meta[2] == 0, gone, 0.0), dot(chosen, fallen)
        )
        down_lines = jnp.where(
            kinds == vocab, gone, jnp.where(kinds == vocab + 1, skips, dot(chosen, risen))
        )
        up_small[chunk] = up_lines
        down_small[chunk] = down_lines
        small_rows = slice(2 * state + chunk * lines, 2 * state + (chunk + 1) * lines)
        up_first[small_rows, :] = up_lines
        down_first[small_rows, :] = down_lines
        if chunk == 0:
            writer_t, reader_t = rows.T, cmat[...].T
            up_first[0:state, :] = dot(writer_t, fallen)
            down_first[0:state, :] = dot(writer_t, risen)
            up_first[state : 2 * state, :] = dot(reader_t, jnp.concatenate(grad_fallen, axis=1))
            down_first[state : 2 * state, :] = dot(reader_t, jnp.concatenate(grad_risen, axis=1))


def head_copies(source, target, row, sems):
    heads, rows, width = source.shape
    return [
        pltpu.make_async_copy(
            source.at[head],
            target.at[pl.ds(row, rows), pl.ds(head * width, width)],
            sems.at[head],
        )
        for head in range(heads)
    ]


def relay_kernel(last, meta, from_before, from_after, up_old, down_old, up, down, sems):
    del up_old, down_old
    for at, (source, target) in enumerate(((from_before, up), (from_after, down))):
        copies = head_copies(source, target, 0, sems.at[at])

        @pl.when(meta[2] != (0, last)[at])
        def _():
            for copy in copies:
                copy.start()
            for copy in copies:
                copy.wait()


def gather_kernel(last, meta, own, from_before, from_after, begin, sems):
    place = meta[2]
    trash = last + 1
    copies = []
    for at, (source, row) in enumerate((
        (own, place),
        (from_before, jnp.where(place == 0, trash, place - 1)),
        (from_after, place + 1),
    )):
        copies += head_copies(source, begin.at[row], 0, sems.at[at])
    for copy in copies:
        copy.start()
    for copy in copies:
        copy.wait()


def combine_kernel(vocab, has_small, has_begin, slot, tables, waits, *refs):
    meta, received, own, small, decays = refs[:5]
    send, held = refs[-3:-1] if has_begin else refs[-2:]
    del waits
    state = own.shape[2]
    land, source, forward, piece = (at + slot for at in tables)
    if has_begin:
        begin = refs[-1]
        begin[meta[piece]] = received[0:state, 0 : begin.shape[2]]
    held[meta[land]] = received[0 : 2 * state, :].astype(BF16)
    passing = meta[forward] != 0
    decay = jnp.where(passing, 1.0, decays[meta[source], vocab : vocab + 1, :])
    adding = jnp.where(passing, 0.0, 1.0)
    if has_small:
        lines = small.shape[1]
        for at in range(small.shape[0]):
            rows = slice(2 * state + at * lines, 2 * state + (at + 1) * lines)
            send[rows, :] = decays[at, vocab : vocab + 1, :] * received[rows, :] + small[at]
    for at in range(2):
        rows = slice(at * state, (at + 1) * state)
        send[rows, :] = decay * received[rows, :] + adding * own[meta[source], at]


def inner_kernel(
    per_chunk, head_dim, vocab,
    meta, hid, cot, writer, cmat, tokens, cols,
    up, down, mixed_in, back_in, reader_in, writer_in, tab,
    inner, inner_t, cross, writer_t, reader_t,
):
    chunk = pl.program_id(0)
    length = hid.shape[0]

    @pl.when(chunk == 0)
    def _():
        inner[...] = dot(cmat[...], writer[...], NT)
        inner_t[...] = dot(writer[...], cmat[...], NT)
        cross[...] = jnp.zeros_like(cross)
        writer_t[...] = writer[...].T
        reader_t[...] = cmat[...].T

    mine = cols[0]
    across = mine.T
    live = live_rows(meta, (length, head_dim))
    fallen, risen, grad_fallen, grad_risen = [], [], [], []
    for head in range(per_chunk):
        at = slice(head * head_dim, (head + 1) * head_dim)
        row = CUM * per_chunk + head
        decay = jnp.exp(
            -jnp.abs(column(mine, CUM, per_chunk, head) - across[row : row + 1, :])
        )
        rise = column(mine, RISE, per_chunk, head)
        fall = column(mine, FALL, per_chunk, head)
        scaled = (column(mine, STEP, per_chunk, head) * hid[:, at].astype(F32)).astype(BF16)
        grads_wide = jnp.where(live, cot[:, at].astype(F32), 0.0)
        grads = grads_wide.astype(BF16)
        scaled_wide = scaled.astype(F32)
        fallen.append((fall * scaled_wide).astype(BF16))
        risen.append((rise * scaled_wide).astype(BF16))
        grad_fallen.append((fall * grads_wide).astype(BF16))
        grad_risen.append((rise * grads_wide).astype(BF16))
        mixed_in[:, at] = dot((decay * inner[...]).astype(BF16), scaled)
        back_in[:, at] = dot((decay * inner_t[...]).astype(BF16), grads)
        cross[...] += decay * dot(grads, scaled, NT)
    up[0, 0] = dot(writer_t[...], jnp.concatenate(fallen, axis=1))
    up[0, 1] = dot(reader_t[...], jnp.concatenate(grad_fallen, axis=1))
    down[0, 0] = dot(writer_t[...], jnp.concatenate(risen, axis=1))
    down[0, 1] = dot(reader_t[...], jnp.concatenate(grad_risen, axis=1))

    @pl.when(chunk == pl.num_programs(0) - 1)
    def _():
        crossed = cross[...].astype(BF16)
        reader_in[...] = dot(crossed, writer[...])
        into = dot(crossed.astype(F32).T.astype(BF16), cmat[...])
        writer_in[...] = into
        chosen = jnp.where(one_hot_rows(tokens[...], tab.shape[0]), 1.0, 0.0).astype(F32)
        tab[...] = dot(chosen, into, precision=EXACT)


def sums_kernel(
    per_chunk, head_dim, vocab, table_scale, skip_scale,
    meta, earlier, later, small, grad_up, grad_down, tab, total, acc,
):
    chunk = pl.program_id(0)
    lines, width = earlier.shape

    @pl.when(chunk == 0)
    def _():
        acc[...] = jnp.zeros_like(acc)

    def split(lhs, rhs):
        high = lhs.astype(BF16)
        low = (lhs - high.astype(F32)).astype(BF16)
        both = dot(jnp.concatenate([high, low], axis=0), rhs.astype(BF16), NT)
        return both[0:lines] + both[lines:]

    head_of = chunk * per_chunk + lax.broadcasted_iota(jnp.int32, (128, width), 1) // head_dim
    picks = jnp.where(
        head_of == lax.broadcasted_iota(jnp.int32, (128, width), 0), 1.0, 0.0
    ).astype(F32)
    kinds = lax.broadcasted_iota(jnp.int32, (lines, 128), 0)
    tables = split(later[...], grad_up[0, 0]) + split(earlier[...], grad_down[0, 0])
    skips = jnp.broadcast_to(small[0, vocab + 1 : vocab + 2, :], (lines, width))
    acc[...] += jnp.where(kinds < vocab, tables, split(skips, picks))

    @pl.when(chunk == pl.num_programs(0) - 1)
    def _():
        total[...] = jnp.where(
            kinds < vocab,
            (acc[...] + tab[...]) * table_scale,
            jnp.where(kinds == vocab, acc[...] * skip_scale, 0.0),
        )


def finish_chunk(
    per_chunk, head_dim, vocab, meta, chunk, gains, hid, cot, writer, cmat, mine,
    mixed_in, back_in, chain_in, chain_back, begin_here, begin_there, earlier,
    mixed, grad_hidden, acc_c, acc_w,
):
    length = hid.shape[0]
    state = chain_in.shape[0] // 2
    live = live_rows(meta, (length, head_dim))
    begins = []
    for at in range(begin_here.shape[0]):
        value = jnp.where(meta[3] != 0, begin_here[at], begin_there[at])
        for lane in range(0, value.shape[1], state):
            begins.append(value[:, lane : lane + state].T)
    begins = jnp.concatenate(begins, axis=1)
    passed = jnp.where(meta[2] == 0, 1.0, earlier[vocab : vocab + 1, :])
    state_in = (chain_in[0:state].astype(F32) + passed * begins).astype(BF16)
    grad_in = chain_in[state:]
    state_back = chain_back[0:state]
    grad_back = chain_back[state:]
    from_in = dot(cmat, state_in)
    from_back = dot(cmat, state_back)
    grad_from_in = dot(writer, grad_in)
    grad_from_back = dot(writer, grad_back)
    fallen, risen, grad_fallen, grad_risen = [], [], [], []
    for head in range(per_chunk):
        at = slice(head * head_dim, (head + 1) * head_dim)
        rise = column(mine, RISE, per_chunk, head)
        fall = column(mine, FALL, per_chunk, head)
        step = column(mine, STEP, per_chunk, head)
        gain = gains[chunk * per_chunk + head]
        values = hid[:, at].astype(F32)
        scaled = (step * values).astype(BF16).astype(F32)
        grads = jnp.where(live, cot[:, at].astype(F32), 0.0)
        mixed[:, at] = (
            mixed_in[:, at] + rise * from_in[:, at] + fall * from_back[:, at] + gain * values
        ).astype(BF16)
        back = back_in[:, at] + rise * grad_from_in[:, at] + fall * grad_from_back[:, at]
        grad_hidden[:, at] = (step * back + gain * grads).astype(BF16)
        fallen.append((fall * scaled).astype(BF16))
        risen.append((rise * scaled).astype(BF16))
        grad_fallen.append((fall * grads).astype(BF16))
        grad_risen.append((rise * grads).astype(BF16))
    fallen, risen, grad_fallen, grad_risen = (
        jnp.concatenate(parts, axis=1) for parts in (fallen, risen, grad_fallen, grad_risen)
    )
    acc_c[...] += dot(grad_risen, state_in, NT) + dot(grad_fallen, state_back, NT)
    acc_w[...] += dot(risen, grad_in, NT) + dot(fallen, grad_back, NT)


def early_kernel(
    per_chunk, head_dim, vocab,
    meta, gains, hid, cot, writer, cmat, cols, mixed_in, back_in, reader_in, writer_in,
    held_up, held_down, begin_here, begin_there, earlier, *refs,
):
    mixed, grad_hidden, acc_c, acc_w = refs[-5:-1]
    chunk = pl.program_id(0)

    @pl.when(chunk == 0)
    def _():
        acc_c[...] = reader_in[...]
        acc_w[...] = writer_in[...]

    finish_chunk(
        per_chunk, head_dim, vocab, meta, chunk, gains, hid, cot, writer[...], cmat[...],
        cols[0], mixed_in, back_in, held_up[0], held_down[0], begin_here, begin_there, earlier,
        mixed, grad_hidden, acc_c, acc_w,
    )


def last_kernel(
    per_chunk, head_dim, vocab, bmat_scale, up_land, down_land, chunk,
    meta, gains, hid, cot, writer, cmat, cols, mixed_in, back_in, sum_c, sum_w,
    held_up, held_down, begin_here, begin_there, earlier, got_up, got_down, *refs,
):
    sums = refs[2:-8]
    mixed, grad_hidden, grad_cmat, grad_bmat, grad_table, grad_skip, acc_c, acc_w = refs[-8:]
    total = sums[0][...]
    for value in sums[1:]:
        total = total + value[...]
    vocab_rows, heads = grad_table.shape[0], grad_skip.shape[1]
    grad_table[...] = total[0:vocab_rows, :]
    grad_skip[...] = total[vocab_rows : vocab_rows + 1, 0:heads]
    acc_c[...] = sum_c[...]
    acc_w[...] = sum_w[...]
    chain_in = jnp.where(meta[up_land] == chunk, got_up[...].astype(BF16), held_up[0])
    chain_back = jnp.where(meta[down_land] == chunk, got_down[...].astype(BF16), held_down[0])
    finish_chunk(
        per_chunk, head_dim, vocab, meta, chunk, gains, hid, cot, writer[...], cmat[...],
        cols[0], mixed_in, back_in, chain_in, chain_back, begin_here, begin_there, earlier,
        mixed, grad_hidden, acc_c, acc_w,
    )
    grad_cmat[...] = acc_c[...].astype(BF16)
    grad_bmat[...] = (acc_w[...] * bmat_scale).astype(BF16)


def whole(shape):
    return pl.BlockSpec(shape, lambda *_: (0,) * len(shape))


def call(body, scalars, grid, ins, outs, scratch=(), aliases=None, limit=16 << 20):
    results = pl.pallas_call(
        body,
        out_shape=[
            jax.ShapeDtypeStruct(shape, kind) if place is None else place(shape, kind)
            for shape, kind, _, place in outs
        ],
        grid_spec=pltpu.PrefetchScalarGridSpec(
            num_scalar_prefetch=len(scalars),
            grid=grid,
            in_specs=[spec for _, spec, _ in ins],
            out_specs=[spec for _, _, spec, _ in outs],
            scratch_shapes=list(scratch),
        ),
        input_output_aliases=aliases or {},
        compiler_params=pltpu.CompilerParams(vmem_limit_bytes=limit),
    )(
        *scalars,
        *[
            array if place is None else pltpu.with_memory_space_constraint(array, place)
            for array, _, place in ins
        ],
    )
    return results


def sum_steps(axes):
    steps, last = [], []
    for axis in axes:
        count = lax.axis_size(axis)
        if count & (count - 1):
            steps.append(functools.partial(lax.psum, axis_name=axis))
            continue
        hop = 1
        while hop < count:
            hops = [hop]
            if axis == axes[-1] and 4 * hop >= count:
                hops = range(hop, count, hop)
            group = [
                functools.partial(
                    lax.ppermute, axis_name=axis, perm=[(at, at ^ far) for at in range(count)]
                )
                for far in hops
            ]
            if axis == axes[-1] and 4 * hop >= count:
                last = group
                break
            steps.append(lambda value, group=group: value + group[0](value))
            hop *= 2
    return steps, last


def per_device(
    hidden, bmat, cmat, tokens, table, step_size, log_decay, skip_gain,
    prev_state, ancestors, suffix_start, cotangent,
):
    prompts, parts, length, width = hidden.shape
    assert prompts * parts == 1
    heads = skip_gain.shape[0]
    head_dim = width // heads
    state_dim = bmat.shape[3]
    vocab = table.shape[0]
    count = lax.axis_size("ctx")
    doms = lax.axis_size("dom")
    place = lax.axis_index("ctx")
    chunks = CHUNKS
    per_chunk = heads // chunks
    part = width // chunks
    total_rows = length * count * doms * lax.axis_size("rep")
    bmat_scale = 1.0 / math.sqrt(width)
    total_scale = 1.0 / math.sqrt(total_rows)
    lines = -(-(vocab + 2) // 8) * 8
    slots = chunks + count - 2

    hid = hidden.reshape(length, width)
    cot = cotangent.reshape(length, width)
    writes = bmat.reshape(length, state_dim)
    reads = cmat.reshape(length, state_dim)
    toks = tokens.reshape(1, length)
    steps_t = jnp.swapaxes(step_size, 2, 3).reshape(heads, length)
    rates_t = jnp.swapaxes(log_decay, 2, 3).reshape(heads, length)
    ancestor = ancestors[0, 0]
    here = ancestor == lax.axis_index("dom")

    times = jnp.arange(slots, dtype=jnp.int32)
    from_last = count - 1 - place
    table_of = []
    for far, toward in ((place, -1), (from_last, 1)):
        lands = times - jnp.maximum(far, 1) + 1
        pieces = place + toward * (times + 2)
        table_of.append(jnp.where((lands >= 0) & (lands < chunks), lands, chunks))
        table_of.append(jnp.clip(times + 1 - far, 0, chunks - 1))
        table_of.append((times + 1 < far).astype(jnp.int32))
        table_of.append(jnp.where((pieces >= 0) & (pieces < count), pieces, count))
    base = jnp.stack([place * length, suffix_start[0], place, here]).astype(jnp.int32)
    meta = jnp.concatenate([base] + table_of)
    up_tables = [4 + at * slots for at in range(4)]
    down_tables = [4 + at * slots for at in range(4, 8)]

    upward = [(at, at + 1) for at in range(count - 1)]
    downward = [(at + 1, at) for at in range(count - 1)]
    own_state = prev_state[0, 0]
    local_heads = own_state.shape[0]
    assert per_chunk % local_heads == 0
    if doms != 2:
        own_state = lax.dynamic_index_in_dim(
            lax.all_gather(own_state, "dom"), ancestor, 0, keepdims=False
        )
    from_before = lax.ppermute(own_state, "ctx", upward)
    from_after = lax.ppermute(own_state, "ctx", downward)

    anywhere = pl.BlockSpec(memory_space=pl.ANY)
    near = pl.BlockSpec(memory_space=pltpu.VMEM)
    by_chunk = pl.BlockSpec((length, part), lambda k, *_: (0, k))
    one_cols = pl.BlockSpec((1, length, 128), lambda k, *_: (k, 0, 0))
    pair = pl.BlockSpec((1, 2, state_dim, part), lambda k, *_: (k, 0, 0, 0))
    one_small = pl.BlockSpec((1, lines, part), lambda k, *_: (k, 0, 0))
    square = whole((length, state_dim))
    tok_spec = whole((1, length))
    full_rows = 2 * state_dim + chunks * lines
    small_shape = (chunks, lines, part)
    first = ((full_rows, part), F32, near, CHIP)

    up_first, down_first, up_small, down_small, cols, writer, hid, cot = call(
        functools.partial(start_kernel, per_chunk, head_dim, vocab, chunks),
        (meta,), (1,),
        [
            (writes, square, HBM), (reads, square, HBM), (toks, tok_spec, HBM),
            (table, whole(table.shape), HBM), (steps_t, whole(steps_t.shape), HBM),
            (rates_t, whole(rates_t.shape), HBM), (hid, anywhere, HBM), (cot, anywhere, HBM),
        ],
        [
            first, first,
            (small_shape, F32, near, CHIP), (small_shape, F32, near, CHIP),
            ((chunks, length, 128), F32, near, CHIP), ((length, state_dim), BF16, near, CHIP),
            ((length, width), BF16, near, CHIP), ((length, width), BF16, near, CHIP),
        ],
        [pltpu.SemaphoreType.DMA((chunks, 2))],
    )

    up_first, down_first = call(
        functools.partial(relay_kernel, count - 1),
        (meta,), (),
        [
            (from_before, anywhere, None), (from_after, anywhere, None),
            (up_first, near, CHIP), (down_first, near, CHIP),
        ],
        [
            ((full_rows, part), F32, near, CHIP), ((full_rows, part), F32, near, CHIP),
        ],
        [pltpu.SemaphoreType.DMA((2, local_heads))],
        aliases={3: 0, 4: 1},
    )
    begin_shape = (count + 1, head_dim, local_heads * state_dim)
    (begin_here,) = call(
        functools.partial(gather_kernel, count - 1),
        (meta,), (),
        [
            (own_state, anywhere, None), (from_before, anywhere, None),
            (from_after, anywhere, None),
        ],
        [(begin_shape, F32, near, CHIP)],
        [pltpu.SemaphoreType.DMA((3, local_heads))],
    )

    up, down, mixed_in, back_in, reader_in, writer_in, tab = call(
        functools.partial(inner_kernel, per_chunk, head_dim, vocab),
        (meta,), (chunks,),
        [
            (hid, by_chunk, CHIP), (cot, by_chunk, CHIP), (writer, square, CHIP),
            (reads, square, HBM), (toks, tok_spec, HBM), (cols, one_cols, CHIP),
        ],
        [
            ((chunks, 2, state_dim, part), F32, pair, CHIP),
            ((chunks, 2, state_dim, part), F32, pair, CHIP),
            ((length, width), F32, by_chunk, CHIP),
            ((length, width), F32, by_chunk, CHIP),
            ((length, state_dim), F32, square, CHIP),
            ((length, state_dim), F32, square, CHIP),
            ((lines, state_dim), F32, whole((lines, state_dim)), CHIP),
        ],
        [pltpu.VMEM((length, length), F32)] * 3 + [pltpu.VMEM((state_dim, length), BF16)] * 2,
    )

    def step_chain(slot, received, own, small, tables, held, begin, waits):
        has_small = slot < count - 2
        has_begin = slot < count - 2
        rows = full_rows if has_small else 2 * state_dim
        held_shape = (chunks + 1, 2 * state_dim, part)
        ins = [
            (received, near, CHIP), (own, near, CHIP), (small, near, CHIP),
            (down_small, near, CHIP),
        ]
        outs = [((rows, part), F32, near, CHIP), (held_shape, BF16, near, CHIP)]
        aliases = {}
        if held is not None:
            aliases[1 + len(ins)] = 1
            ins.append((held, near, CHIP))
        if has_begin:
            aliases[1 + len(ins)] = 2
            ins.append((begin, near, CHIP))
            outs.append((begin_shape, F32, near, CHIP))
        ins += [(value, anywhere, None) for value in waits]
        results = call(
            functools.partial(
                combine_kernel, vocab, has_small, has_begin, slot, tables, len(waits)
            ),
            (meta,), (), ins, outs,
            aliases=aliases,
        )
        return results if has_begin else (*results, begin)

    lines_at = 2 * state_dim // lines
    from_slot = pl.BlockSpec((lines, part), lambda k, *_: (lines_at + k, 0))
    grad_part = pl.BlockSpec((1, 1, state_dim, part), lambda k, *_: (k, 1, 0, 0))
    sums, exchanges = sum_steps(("rep", "dom", "ctx"))
    send_up, send_down, held_up, held_down = up_first, down_first, None, None
    for slot in range(slots):
        first_place = max(0, slot - chunks + 1)
        got_down = lax.ppermute(
            send_down, "ctx", [(count - 1 - at, count - 2 - at) for at in range(first_place, count - 1)]
        )
        got_up = lax.ppermute(send_up, "ctx", upward[first_place:])
        waits_up, waits_down = [], []
        if slot == count - 2:
            earlier, later = got_up, got_down
        if slot == count - 1:
            begin_there = begin_here
            if doms == 2:
                begin_there = lax.ppermute(begin_here, "dom", [(0, 1), (1, 0)])
            (total,) = call(
                functools.partial(
                    sums_kernel, per_chunk, head_dim, vocab,
                    bmat_scale * total_scale, total_scale / math.sqrt(head_dim),
                ),
                (meta,), (chunks,),
                [
                    (earlier, from_slot, None), (later, from_slot, None),
                    (down_small, one_small, None), (up, grad_part, CHIP),
                    (down, grad_part, CHIP), (tab, whole(tab.shape), CHIP),
                ],
                [((lines, state_dim), F32, whole((lines, state_dim)), None)],
                [pltpu.VMEM((lines, state_dim), F32)],
            )
        if slot == slots - 1:
            break
        if slot >= count - 1:
            if slot > count - 1:
                waits_down.append(begin_there)
                for step in sums[:1]:
                    total = step(total)
                sums = sums[1:]
            waits_down.append(total)
        send_down, held_down, begin_here = step_chain(
            slot, got_down, down, down_small, down_tables, held_down, begin_here, waits_down
        )
        if slot >= count - 1:
            for step in sums[:1]:
                total = step(total)
            sums = sums[1:]
            waits_up.append(total)
        send_up, held_up, begin_here = step_chain(
            slot, got_up, up, up_small, up_tables, held_up, begin_here, waits_up
        )

    def chunk_specs(at):
        return (
            pl.BlockSpec((length, part), lambda k, *_: (0, k + at)),
            pl.BlockSpec((1, length, 128), lambda k, *_: (k + at, 0, 0)),
            pl.BlockSpec((1, 2 * state_dim, part), lambda k, *_: (k + at, 0, 0)),
            pl.BlockSpec(
                (per_chunk // local_heads, head_dim, local_heads * state_dim),
                lambda k, *_: (k + at, 0, 0),
            ),
            pl.BlockSpec((lines, part), lambda k, *_: (lines_at + k + at, 0)),
        )

    def finish_ins(at, sum_c, sum_w):
        slab, col, chain, states, small = chunk_specs(at)
        return [
            (hid, slab, CHIP), (cot, slab, CHIP), (writer, square, CHIP), (reads, square, HBM),
            (cols, col, CHIP), (mixed_in, slab, CHIP), (back_in, slab, CHIP),
            (sum_c, square, CHIP), (sum_w, square, CHIP),
            (held_up, chain, CHIP), (held_down, chain, CHIP),
            (begin_here, states, CHIP), (begin_there, states, CHIP), (earlier, small, None),
        ]

    for step in sums:
        total = step(total)
    slab = chunk_specs(0)[0]
    mixed, grad_hidden, sum_c, sum_w, total = call(
        functools.partial(early_kernel, per_chunk, head_dim, vocab),
        (meta, skip_gain), (chunks - 1,),
        finish_ins(0, reader_in, writer_in) + [(total, anywhere, None)],
        [
            ((length, width), BF16, slab, HBM), ((length, width), BF16, slab, HBM),
            ((length, state_dim), F32, square, CHIP), ((length, state_dim), F32, square, CHIP),
            (total.shape, F32, anywhere, None),
        ],
        aliases={16: 4},
    )
    exchanged = [exchange(total) for exchange in exchanges]
    ins = finish_ins(chunks - 1, sum_c, sum_w) + [
        (got_up, whole(got_up.shape), None), (got_down, whole(got_down.shape), None),
        (mixed, anywhere, HBM), (grad_hidden, anywhere, HBM),
    ] + [(value, whole(value.shape), None) for value in [total] + exchanged]
    slab = chunk_specs(chunks - 1)[0]
    mixed, grad_hidden, grad_cmat, grad_bmat, grad_table, grad_skip = call(
        functools.partial(
            last_kernel, per_chunk, head_dim, vocab, bmat_scale,
            up_tables[0] + slots - 1, down_tables[0] + slots - 1, chunks - 1,
        ),
        (meta, skip_gain), (1,), ins,
        [
            ((length, width), BF16, slab, HBM), ((length, width), BF16, slab, HBM),
            ((length, state_dim), BF16, square, HBM), ((length, state_dim), BF16, square, HBM),
            (table.shape, F32, whole(table.shape), HBM),
            ((1, heads), F32, whole((1, heads)), HBM),
        ],
        [pltpu.VMEM((length, state_dim), F32)] * 2,
        aliases={18: 0, 19: 1},
    )
    return (
        mixed.reshape(hidden.shape),
        grad_hidden.reshape(hidden.shape),
        grad_bmat.reshape(bmat.shape),
        grad_cmat.reshape(cmat.shape),
        grad_table,
        grad_skip.reshape(heads),
    )


def solution(mesh):
    rows = P("rep", "dom", "ctx", None)
    return jax.shard_map(
        per_device,
        mesh=mesh,
        in_specs=(
            rows, rows, rows, P("rep", "dom", "ctx"), P(), rows, rows, P(),
            P("rep", "dom", "ctx", None, None), P("rep", "dom"), P("rep"), rows,
        ),
        out_specs=(rows, rows, rows, rows, P(), P()),
        check_vma=False,
    )
```

```python
import functools
import math

import jax
import jax.numpy as jnp
from jax import lax
from jax.experimental import pallas as pl
from jax.experimental.pallas import tpu as pltpu
from jax.sharding import PartitionSpec as P

F32 = jnp.float32
BF16 = jnp.bfloat16
EXACT = lax.Precision.HIGHEST
NN = (((1,), (0,)), ((), ()))
NT = (((1,), (1,)), ((), ()))
TN = (((0,), (0,)), ((), ()))
CHUNKS = 4
HBM, CHIP = pltpu.HBM, pltpu.VMEM


def dot(left, right, dims=NN, precision=None):
    return lax.dot_general(
        left, right, dims, precision=precision, preferred_element_type=F32
    )


def one_hot_rows(tokens_row, rows):
    kinds = lax.broadcasted_iota(jnp.int32, (rows, tokens_row.shape[1]), 0)
    return kinds == tokens_row


def live_rows(meta, shape):
    return meta[0] + lax.broadcasted_iota(jnp.int32, shape, 0) < meta[1]


def column(cols, kind, per_chunk, head):
    at = kind * per_chunk + head
    return cols[:, at : at + 1]


STEP, RISE, FALL, CUM = range(4)


def start_kernel(
    per_chunk, head_dim, vocab, chunks,
    meta, bmat, cmat, tokens, table, step_t, rate_t, hid_far, cot_far,
    up_first, down_first, up_small, down_small, cols, writer, hid, cot, sems,
):
    length = bmat.shape[0]
    state = bmat.shape[1]
    part = per_chunk * head_dim
    lines = up_small.shape[1]
    copies = []
    for chunk in range(chunks):
        span = slice(chunk * part, (chunk + 1) * part)
        pair = [
            pltpu.make_async_copy(far.at[:, span], near.at[:, span], sems.at[chunk, at])
            for at, (far, near) in enumerate(((hid_far, hid), (cot_far, cot)))
        ]
        for copy in pair:
            copy.start()
        copies.append(pair)

    row = lax.broadcasted_iota(jnp.int32, (length, length), 0)
    col = lax.broadcasted_iota(jnp.int32, (length, length), 1)
    lower = jnp.where(col <= row, 1.0, 0.0).astype(F32)
    cumulative = dot(lower, rate_t[...], NT, EXACT)
    totals = cumulative[length - 1 : length, :]
    rising = jnp.exp(-cumulative)
    falling = jnp.exp(-(totals - cumulative))
    step = step_t[...].T
    for at in range(chunks):
        lo = at * per_chunk
        for kind, values in enumerate((step, rising, falling, cumulative)):
            cols[at, :, kind * per_chunk : (kind + 1) * per_chunk] = values[:, lo : lo + per_chunk]
    hot = one_hot_rows(tokens[...], vocab)
    looked = dot(jnp.where(hot, 1.0, 0.0).astype(F32), table[...], TN, EXACT)
    rows = (bmat[...].astype(F32) + looked).astype(BF16)
    writer[...] = rows
    chosen = jnp.where(one_hot_rows(tokens[...], lines), 1.0, 0.0).astype(BF16)
    kinds = lax.broadcasted_iota(jnp.int32, (lines, part), 0)
    live = live_rows(meta, (length, head_dim))
    for chunk in range(chunks):
        for copy in copies[chunk]:
            copy.wait()
        fallen, risen, grad_fallen, grad_risen, gone, skips = [], [], [], [], [], []
        for head in range(per_chunk):
            number = chunk * per_chunk + head
            at = slice(number * head_dim, (number + 1) * head_dim)
            rise = rising[:, number : number + 1]
            fall = falling[:, number : number + 1]
            values = hid[:, at].astype(F32)
            scaled = (step[:, number : number + 1] * values).astype(BF16).astype(F32)
            grads = jnp.where(live, cot[:, at].astype(F32), 0.0)
            fallen.append((fall * scaled).astype(BF16))
            risen.append((rise * scaled).astype(BF16))
            if chunk == 0:
                grad_fallen.append((fall * grads).astype(BF16))
                grad_risen.append((rise * grads).astype(BF16))
            gone.append(jnp.broadcast_to(rise[length - 1 : length, :], (1, head_dim)))
            skips.append(jnp.sum(values * grads, axis=0, keepdims=True))
        fallen, risen, gone, skips = (
            jnp.concatenate(parts, axis=1) for parts in (fallen, risen, gone, skips)
        )
        up_lines = jnp.where(
            kinds == vocab, jnp.where(meta[2] == 0, gone, 0.0), dot(chosen, fallen)
        )
        down_lines = jnp.where(
            kinds == vocab, gone, jnp.where(kinds == vocab + 1, skips, dot(chosen, risen))
        )
        up_small[chunk] = up_lines
        down_small[chunk] = down_lines
        small_rows = slice(2 * state + chunk * lines, 2 * state + (chunk + 1) * lines)
        up_first[small_rows, :] = up_lines
        down_first[small_rows, :] = down_lines
        if chunk == 0:
            writer_t, reader_t = rows.T, cmat[...].T
            up_first[0:state, :] = dot(writer_t, fallen)
            down_first[0:state, :] = dot(writer_t, risen)
            up_first[state : 2 * state, :] = dot(reader_t, jnp.concatenate(grad_fallen, axis=1))
            down_first[state : 2 * state, :] = dot(reader_t, jnp.concatenate(grad_risen, axis=1))


def head_copies(source, target, row, sems):
    heads, rows, width = source.shape
    return [
        pltpu.make_async_copy(
            source.at[head],
            target.at[pl.ds(row, rows), pl.ds(head * width, width)],
            sems.at[head],
        )
        for head in range(heads)
    ]


def relay_kernel(last, paired, meta, *refs):
    sources, (up, down, sems) = refs[:-5], refs[-3:]
    if paired:
        plans = [
            (meta[2] == target, message, pieces)
            for target, message, pieces in ((1, up, sources), (2, down, sources))
        ]
    else:
        plans = [
            (meta[2] != (0, last)[at], message, sources[at : at + 1])
            for at, message in enumerate((up, down))
        ]
    for at, (wanted, message, pieces) in enumerate(plans):
        copies = []
        for half, source in enumerate(pieces):
            copies += head_copies(source, message, half * source.shape[1], sems.at[at, half])

        @pl.when(wanted)
        def _():
            for copy in copies:
                copy.start()
            for copy in copies:
                copy.wait()


def gather_kernel(last, paired, meta, *refs):
    sources, begin, sems = refs[:-2], refs[-2], refs[-1]
    place = meta[2]
    if paired:
        rows = (lax.bitwise_xor(place, 1), place)
    else:
        rows = (jnp.where(place == 0, last + 1, place - 1), place + 1, place)
    copies = []
    for at, (source, row) in enumerate(zip(sources, rows, strict=True)):
        copies += head_copies(source, begin.at[row], 0, sems.at[at])
    for copy in copies:
        copy.start()
    for copy in copies:
        copy.wait()


def combine_kernel(vocab, has_small, has_begin, slot, tables, waits, *refs):
    meta, received, own, small, decays = refs[:5]
    send, held = refs[-3:-1] if has_begin else refs[-2:]
    del waits
    state = own.shape[2]
    land, source, forward, piece, other = (at + slot for at in tables)
    if has_begin:
        begin = refs[-1]
        begin[meta[piece]] = received[0:state, 0 : begin.shape[2]]
        begin[meta[other]] = received[state : 2 * state, 0 : begin.shape[2]]
    held[meta[land]] = received[0 : 2 * state, :].astype(BF16)
    passing = meta[forward] != 0
    decay = jnp.where(passing, 1.0, decays[meta[source], vocab : vocab + 1, :])
    adding = jnp.where(passing, 0.0, 1.0)
    if has_small:
        lines = small.shape[1]
        for at in range(small.shape[0]):
            rows = slice(2 * state + at * lines, 2 * state + (at + 1) * lines)
            send[rows, :] = decays[at, vocab : vocab + 1, :] * received[rows, :] + small[at]
    for at in range(2):
        rows = slice(at * state, (at + 1) * state)
        send[rows, :] = decay * received[rows, :] + adding * own[meta[source], at]


def inner_kernel(
    per_chunk, head_dim, vocab,
    meta, hid, cot, writer, cmat, tokens, cols,
    up, down, mixed_in, back_in, reader_in, writer_in, tab,
    inner, inner_t, cross, writer_t, reader_t,
):
    chunk = pl.program_id(0)
    length = hid.shape[0]

    @pl.when(chunk == 0)
    def _():
        inner[...] = dot(cmat[...], writer[...], NT)
        inner_t[...] = dot(writer[...], cmat[...], NT)
        cross[...] = jnp.zeros_like(cross)
        writer_t[...] = writer[...].T
        reader_t[...] = cmat[...].T

    mine = cols[0]
    across = mine.T
    live = live_rows(meta, (length, head_dim))
    fallen, risen, grad_fallen, grad_risen = [], [], [], []
    for head in range(per_chunk):
        at = slice(head * head_dim, (head + 1) * head_dim)
        row = CUM * per_chunk + head
        decay = jnp.exp(
            -jnp.abs(column(mine, CUM, per_chunk, head) - across[row : row + 1, :])
        )
        rise = column(mine, RISE, per_chunk, head)
        fall = column(mine, FALL, per_chunk, head)
        scaled = (column(mine, STEP, per_chunk, head) * hid[:, at].astype(F32)).astype(BF16)
        grads_wide = jnp.where(live, cot[:, at].astype(F32), 0.0)
        grads = grads_wide.astype(BF16)
        scaled_wide = scaled.astype(F32)
        fallen.append((fall * scaled_wide).astype(BF16))
        risen.append((rise * scaled_wide).astype(BF16))
        grad_fallen.append((fall * grads_wide).astype(BF16))
        grad_risen.append((rise * grads_wide).astype(BF16))
        mixed_in[:, at] = dot((decay * inner[...]).astype(BF16), scaled)
        back_in[:, at] = dot((decay * inner_t[...]).astype(BF16), grads)
        cross[...] += decay * dot(grads, scaled, NT)
    up[0, 0] = dot(writer_t[...], jnp.concatenate(fallen, axis=1))
    up[0, 1] = dot(reader_t[...], jnp.concatenate(grad_fallen, axis=1))
    down[0, 0] = dot(writer_t[...], jnp.concatenate(risen, axis=1))
    down[0, 1] = dot(reader_t[...], jnp.concatenate(grad_risen, axis=1))

    @pl.when(chunk == pl.num_programs(0) - 1)
    def _():
        crossed = cross[...].astype(BF16)
        reader_in[...] = dot(crossed, writer[...])
        into = dot(crossed.astype(F32).T.astype(BF16), cmat[...])
        writer_in[...] = into
        chosen = jnp.where(one_hot_rows(tokens[...], tab.shape[0]), 1.0, 0.0).astype(F32)
        tab[...] = dot(chosen, into, precision=EXACT)


def sums_kernel(
    per_chunk, head_dim, vocab, table_scale, skip_scale,
    meta, earlier, later, small, grad_up, grad_down, tab, total, acc,
):
    chunk = pl.program_id(0)
    lines, width = earlier.shape

    @pl.when(chunk == 0)
    def _():
        acc[...] = jnp.zeros_like(acc)

    def split(lhs, rhs):
        high = lhs.astype(BF16)
        low = (lhs - high.astype(F32)).astype(BF16)
        both = dot(jnp.concatenate([high, low], axis=0), rhs.astype(BF16), NT)
        return both[0:lines] + both[lines:]

    head_of = chunk * per_chunk + lax.broadcasted_iota(jnp.int32, (128, width), 1) // head_dim
    picks = jnp.where(
        head_of == lax.broadcasted_iota(jnp.int32, (128, width), 0), 1.0, 0.0
    ).astype(F32)
    kinds = lax.broadcasted_iota(jnp.int32, (lines, 128), 0)
    tables = split(later[...], grad_up[0, 0]) + split(earlier[...], grad_down[0, 0])
    skips = jnp.broadcast_to(small[0, vocab + 1 : vocab + 2, :], (lines, width))
    acc[...] += jnp.where(kinds < vocab, tables, split(skips, picks))

    @pl.when(chunk == pl.num_programs(0) - 1)
    def _():
        total[...] = jnp.where(
            kinds < vocab,
            (acc[...] + tab[...]) * table_scale,
            jnp.where(kinds == vocab, acc[...] * skip_scale, 0.0),
        )


def finish_chunk(
    per_chunk, head_dim, vocab, meta, chunk, gains, hid, cot, writer, cmat, mine,
    mixed_in, back_in, chain_in, chain_back, begin_here, begin_there, earlier,
    mixed, grad_hidden, acc_c, acc_w,
):
    length = hid.shape[0]
    state = chain_in.shape[0] // 2
    live = live_rows(meta, (length, head_dim))
    begins = []
    for at in range(begin_here.shape[0]):
        value = jnp.where(meta[3] != 0, begin_here[at], begin_there[at])
        for lane in range(0, value.shape[1], state):
            begins.append(value[:, lane : lane + state].T)
    begins = jnp.concatenate(begins, axis=1)
    passed = jnp.where(meta[2] == 0, 1.0, earlier[vocab : vocab + 1, :])
    state_in = (chain_in[0:state].astype(F32) + passed * begins).astype(BF16)
    grad_in = chain_in[state:]
    state_back = chain_back[0:state]
    grad_back = chain_back[state:]
    from_in = dot(cmat, state_in)
    from_back = dot(cmat, state_back)
    grad_from_in = dot(writer, grad_in)
    grad_from_back = dot(writer, grad_back)
    fallen, risen, grad_fallen, grad_risen = [], [], [], []
    for head in range(per_chunk):
        at = slice(head * head_dim, (head + 1) * head_dim)
        rise = column(mine, RISE, per_chunk, head)
        fall = column(mine, FALL, per_chunk, head)
        step = column(mine, STEP, per_chunk, head)
        gain = gains[chunk * per_chunk + head]
        values = hid[:, at].astype(F32)
        scaled = (step * values).astype(BF16).astype(F32)
        grads = jnp.where(live, cot[:, at].astype(F32), 0.0)
        mixed[:, at] = (
            mixed_in[:, at] + rise * from_in[:, at] + fall * from_back[:, at] + gain * values
        ).astype(BF16)
        back = back_in[:, at] + rise * grad_from_in[:, at] + fall * grad_from_back[:, at]
        grad_hidden[:, at] = (step * back + gain * grads).astype(BF16)
        fallen.append((fall * scaled).astype(BF16))
        risen.append((rise * scaled).astype(BF16))
        grad_fallen.append((fall * grads).astype(BF16))
        grad_risen.append((rise * grads).astype(BF16))
    fallen, risen, grad_fallen, grad_risen = (
        jnp.concatenate(parts, axis=1) for parts in (fallen, risen, grad_fallen, grad_risen)
    )
    acc_c[...] += dot(grad_risen, state_in, NT) + dot(grad_fallen, state_back, NT)
    acc_w[...] += dot(risen, grad_in, NT) + dot(fallen, grad_back, NT)


def early_kernel(
    per_chunk, head_dim, vocab,
    meta, gains, hid, cot, writer, cmat, cols, mixed_in, back_in, reader_in, writer_in,
    held_up, held_down, begin_here, begin_there, earlier, *refs,
):
    mixed, grad_hidden, acc_c, acc_w = refs[-5:-1]
    chunk = pl.program_id(0)

    @pl.when(chunk == 0)
    def _():
        acc_c[...] = reader_in[...]
        acc_w[...] = writer_in[...]

    finish_chunk(
        per_chunk, head_dim, vocab, meta, chunk, gains, hid, cot, writer[...], cmat[...],
        cols[0], mixed_in, back_in, held_up[0], held_down[0], begin_here, begin_there, earlier,
        mixed, grad_hidden, acc_c, acc_w,
    )


def last_kernel(
    per_chunk, head_dim, vocab, bmat_scale, up_land, down_land, chunk,
    meta, gains, hid, cot, writer, cmat, cols, mixed_in, back_in, sum_c, sum_w,
    held_up, held_down, begin_here, begin_there, earlier, got_up, got_down, *refs,
):
    sums = refs[2:-8]
    mixed, grad_hidden, grad_cmat, grad_bmat, grad_table, grad_skip, acc_c, acc_w = refs[-8:]
    total = sums[0][...]
    for value in sums[1:]:
        total = total + value[...]
    vocab_rows, heads = grad_table.shape[0], grad_skip.shape[1]
    grad_table[...] = total[0:vocab_rows, :]
    grad_skip[...] = total[vocab_rows : vocab_rows + 1, 0:heads]
    acc_c[...] = sum_c[...]
    acc_w[...] = sum_w[...]
    chain_in = jnp.where(meta[up_land] == chunk, got_up[...].astype(BF16), held_up[0])
    chain_back = jnp.where(meta[down_land] == chunk, got_down[...].astype(BF16), held_down[0])
    finish_chunk(
        per_chunk, head_dim, vocab, meta, chunk, gains, hid, cot, writer[...], cmat[...],
        cols[0], mixed_in, back_in, chain_in, chain_back, begin_here, begin_there, earlier,
        mixed, grad_hidden, acc_c, acc_w,
    )
    grad_cmat[...] = acc_c[...].astype(BF16)
    grad_bmat[...] = (acc_w[...] * bmat_scale).astype(BF16)


def whole(shape):
    return pl.BlockSpec(shape, lambda *_: (0,) * len(shape))


def call(body, scalars, grid, ins, outs, scratch=(), aliases=None, limit=16 << 20):
    results = pl.pallas_call(
        body,
        out_shape=[
            jax.ShapeDtypeStruct(shape, kind) if place is None else place(shape, kind)
            for shape, kind, _, place in outs
        ],
        grid_spec=pltpu.PrefetchScalarGridSpec(
            num_scalar_prefetch=len(scalars),
            grid=grid,
            in_specs=[spec for _, spec, _ in ins],
            out_specs=[spec for _, _, spec, _ in outs],
            scratch_shapes=list(scratch),
        ),
        input_output_aliases=aliases or {},
        compiler_params=pltpu.CompilerParams(vmem_limit_bytes=limit),
    )(
        *scalars,
        *[
            array if place is None else pltpu.with_memory_space_constraint(array, place)
            for array, _, place in ins
        ],
    )
    return results


def sum_steps(axes):
    steps, last = [], []
    for axis in axes:
        count = lax.axis_size(axis)
        if count & (count - 1):
            steps.append(functools.partial(lax.psum, axis_name=axis))
            continue
        hop = 1
        while hop < count:
            hops = [hop]
            if axis == axes[-1] and 4 * hop >= count:
                hops = range(hop, count, hop)
            group = [
                functools.partial(
                    lax.ppermute, axis_name=axis, perm=[(at, at ^ far) for at in range(count)]
                )
                for far in hops
            ]
            if axis == axes[-1] and 4 * hop >= count:
                last = group
                break
            steps.append(lambda value, group=group: value + group[0](value))
            hop *= 2
    return steps, last


def per_device(
    hidden, bmat, cmat, tokens, table, step_size, log_decay, skip_gain,
    prev_state, ancestors, suffix_start, cotangent,
):
    prompts, parts, length, width = hidden.shape
    assert prompts * parts == 1
    heads = skip_gain.shape[0]
    head_dim = width // heads
    state_dim = bmat.shape[3]
    vocab = table.shape[0]
    count = lax.axis_size("ctx")
    doms = lax.axis_size("dom")
    place = lax.axis_index("ctx")
    chunks = CHUNKS
    per_chunk = heads // chunks
    part = width // chunks
    total_rows = length * count * doms * lax.axis_size("rep")
    bmat_scale = 1.0 / math.sqrt(width)
    total_scale = 1.0 / math.sqrt(total_rows)
    lines = -(-(vocab + 2) // 8) * 8
    slots = chunks + count - 2
    paired = count == 4

    hid = hidden.reshape(length, width)
    cot = cotangent.reshape(length, width)
    writes = bmat.reshape(length, state_dim)
    reads = cmat.reshape(length, state_dim)
    toks = tokens.reshape(1, length)
    steps_t = jnp.swapaxes(step_size, 2, 3).reshape(heads, length)
    rates_t = jnp.swapaxes(log_decay, 2, 3).reshape(heads, length)
    ancestor = ancestors[0, 0]
    here = ancestor == lax.axis_index("dom")

    times = jnp.arange(slots, dtype=jnp.int32)
    from_last = count - 1 - place
    table_of = []
    for far, toward in ((place, -1), (from_last, 1)):
        lands = times - jnp.maximum(far, 1) + 1
        pieces = place + toward * (times + 2)
        others = jnp.full_like(times, count)
        if paired:
            arrives = times + 2 == far
            pieces = jnp.where(arrives, 0 if toward < 0 else 3, count)
            others = jnp.where(arrives, 1 if toward < 0 else 2, count)
        table_of.append(jnp.where((lands >= 0) & (lands < chunks), lands, chunks))
        table_of.append(jnp.clip(times + 1 - far, 0, chunks - 1))
        table_of.append((times + 1 < far).astype(jnp.int32))
        table_of.append(jnp.where((pieces >= 0) & (pieces < count), pieces, count))
        table_of.append(others)
    base = [place * length, suffix_start[0], place, here]
    meta = jnp.concatenate([jnp.stack(base).astype(jnp.int32)] + table_of)
    up_tables = [4 + at * slots for at in range(5)]
    down_tables = [4 + at * slots for at in range(5, 10)]

    upward = [(at, at + 1) for at in range(count - 1)]
    downward = [(at + 1, at) for at in range(count - 1)]
    own_state = prev_state[0, 0]
    local_heads = own_state.shape[0]
    assert per_chunk % local_heads == 0
    if doms != 2:
        own_state = lax.dynamic_index_in_dim(
            lax.all_gather(own_state, "dom"), ancestor, 0, keepdims=False
        )
    if paired:
        swap = [(at, at ^ 1) for at in range(count)]
        pieces = [lax.ppermute(own_state, "ctx", swap), own_state]
    else:
        pieces = [lax.ppermute(own_state, "ctx", way) for way in (upward, downward)]

    anywhere = pl.BlockSpec(memory_space=pl.ANY)
    near = pl.BlockSpec(memory_space=pltpu.VMEM)
    by_chunk = pl.BlockSpec((length, part), lambda k, *_: (0, k))
    one_cols = pl.BlockSpec((1, length, 128), lambda k, *_: (k, 0, 0))
    pair = pl.BlockSpec((1, 2, state_dim, part), lambda k, *_: (k, 0, 0, 0))
    one_small = pl.BlockSpec((1, lines, part), lambda k, *_: (k, 0, 0))
    square = whole((length, state_dim))
    tok_spec = whole((1, length))
    full_rows = 2 * state_dim + chunks * lines
    small_shape = (chunks, lines, part)
    first = ((full_rows, part), F32, near, CHIP)

    up_first, down_first, up_small, down_small, cols, writer, hid, cot = call(
        functools.partial(start_kernel, per_chunk, head_dim, vocab, chunks),
        (meta,), (1,),
        [
            (writes, square, HBM), (reads, square, HBM), (toks, tok_spec, HBM),
            (table, whole(table.shape), HBM), (steps_t, whole(steps_t.shape), HBM),
            (rates_t, whole(rates_t.shape), HBM), (hid, anywhere, HBM), (cot, anywhere, HBM),
        ],
        [
            first, first,
            (small_shape, F32, near, CHIP), (small_shape, F32, near, CHIP),
            ((chunks, length, 128), F32, near, CHIP), ((length, state_dim), BF16, near, CHIP),
            ((length, width), BF16, near, CHIP), ((length, width), BF16, near, CHIP),
        ],
        [pltpu.SemaphoreType.DMA((chunks, 2))],
    )

    up_first, down_first = call(
        functools.partial(relay_kernel, count - 1, paired),
        (meta,), (),
        [(piece, anywhere, None) for piece in pieces]
        + [(up_first, near, CHIP), (down_first, near, CHIP)],
        [
            ((full_rows, part), F32, near, CHIP), ((full_rows, part), F32, near, CHIP),
        ],
        [pltpu.SemaphoreType.DMA((2, 2, local_heads))],
        aliases={3: 0, 4: 1},
    )
    begin_shape = (count + 1, head_dim, local_heads * state_dim)
    (begin_here,) = call(
        functools.partial(gather_kernel, count - 1, paired),
        (meta,), (),
        [
            (piece, anywhere, None) for piece in (pieces if paired else pieces + [own_state])
        ],
        [(begin_shape, F32, near, CHIP)],
        [pltpu.SemaphoreType.DMA((3, local_heads))],
    )

    up, down, mixed_in, back_in, reader_in, writer_in, tab = call(
        functools.partial(inner_kernel, per_chunk, head_dim, vocab),
        (meta,), (chunks,),
        [
            (hid, by_chunk, CHIP), (cot, by_chunk, CHIP), (writer, square, CHIP),
            (reads, square, HBM), (toks, tok_spec, HBM), (cols, one_cols, CHIP),
        ],
        [
            ((chunks, 2, state_dim, part), F32, pair, CHIP),
            ((chunks, 2, state_dim, part), F32, pair, CHIP),
            ((length, width), F32, by_chunk, CHIP),
            ((length, width), F32, by_chunk, CHIP),
            ((length, state_dim), F32, square, CHIP),
            ((length, state_dim), F32, square, CHIP),
            ((lines, state_dim), F32, whole((lines, state_dim)), CHIP),
        ],
        [pltpu.VMEM((length, length), F32)] * 3 + [pltpu.VMEM((state_dim, length), BF16)] * 2,
    )

    def step_chain(slot, received, own, small, tables, held, begin, waits):
        has_small = slot < count - 2
        has_begin = slot < count - 2
        rows = full_rows if has_small else 2 * state_dim
        held_shape = (chunks + 1, 2 * state_dim, part)
        ins = [
            (received, near, CHIP), (own, near, CHIP), (small, near, CHIP),
            (down_small, near, CHIP),
        ]
        outs = [((rows, part), F32, near, CHIP), (held_shape, BF16, near, CHIP)]
        aliases = {}
        if held is not None:
            aliases[1 + len(ins)] = 1
            ins.append((held, near, CHIP))
        if has_begin:
            aliases[1 + len(ins)] = 2
            ins.append((begin, near, CHIP))
            outs.append((begin_shape, F32, near, CHIP))
        ins += [(value, anywhere, None) for value in waits]
        results = call(
            functools.partial(
                combine_kernel, vocab, has_small, has_begin, slot, tables, len(waits)
            ),
            (meta,), (), ins, outs,
            aliases=aliases,
        )
        return results if has_begin else (*results, begin)

    lines_at = 2 * state_dim // lines
    from_slot = pl.BlockSpec((lines, part), lambda k, *_: (lines_at + k, 0))
    grad_part = pl.BlockSpec((1, 1, state_dim, part), lambda k, *_: (k, 1, 0, 0))
    sums, exchanges = sum_steps(("rep", "dom", "ctx"))
    send_up, send_down, held_up, held_down = up_first, down_first, None, None
    for slot in range(slots):
        first_place = max(0, slot - chunks + 1)
        got_down = lax.ppermute(
            send_down, "ctx", [(count - 1 - at, count - 2 - at) for at in range(first_place, count - 1)]
        )
        got_up = lax.ppermute(send_up, "ctx", upward[first_place:])
        waits_up, waits_down = [], []
        if slot == count - 2:
            earlier, later = got_up, got_down
        if slot == count - 1:
            begin_there = begin_here
            if doms == 2:
                begin_there = lax.ppermute(begin_here, "dom", [(0, 1), (1, 0)])
            (total,) = call(
                functools.partial(
                    sums_kernel, per_chunk, head_dim, vocab,
                    bmat_scale * total_scale, total_scale / math.sqrt(head_dim),
                ),
                (meta,), (chunks,),
                [
                    (earlier, from_slot, None), (later, from_slot, None),
                    (down_small, one_small, None), (up, grad_part, CHIP),
                    (down, grad_part, CHIP), (tab, whole(tab.shape), CHIP),
                ],
                [((lines, state_dim), F32, whole((lines, state_dim)), None)],
                [pltpu.VMEM((lines, state_dim), F32)],
            )
        if slot == slots - 1:
            break
        if slot >= count - 1:
            if slot > count - 1:
                waits_down.append(begin_there)
                for step in sums[:1]:
                    total = step(total)
                sums = sums[1:]
            waits_down.append(total)
        send_down, held_down, begin_here = step_chain(
            slot, got_down, down, down_small, down_tables, held_down, begin_here, waits_down
        )
        if slot >= count - 1:
            for step in sums[:1]:
                total = step(total)
            sums = sums[1:]
            waits_up.append(total)
        send_up, held_up, begin_here = step_chain(
            slot, got_up, up, up_small, up_tables, held_up, begin_here, waits_up
        )

    def chunk_specs(at):
        return (
            pl.BlockSpec((length, part), lambda k, *_: (0, k + at)),
            pl.BlockSpec((1, length, 128), lambda k, *_: (k + at, 0, 0)),
            pl.BlockSpec((1, 2 * state_dim, part), lambda k, *_: (k + at, 0, 0)),
            pl.BlockSpec(
                (per_chunk // local_heads, head_dim, local_heads * state_dim),
                lambda k, *_: (k + at, 0, 0),
            ),
            pl.BlockSpec((lines, part), lambda k, *_: (lines_at + k + at, 0)),
        )

    def finish_ins(at, sum_c, sum_w):
        slab, col, chain, states, small = chunk_specs(at)
        return [
            (hid, slab, CHIP), (cot, slab, CHIP), (writer, square, CHIP), (reads, square, HBM),
            (cols, col, CHIP), (mixed_in, slab, CHIP), (back_in, slab, CHIP),
            (sum_c, square, CHIP), (sum_w, square, CHIP),
            (held_up, chain, CHIP), (held_down, chain, CHIP),
            (begin_here, states, CHIP), (begin_there, states, CHIP), (earlier, small, None),
        ]

    for step in sums:
        total = step(total)
    slab = chunk_specs(0)[0]
    mixed, grad_hidden, sum_c, sum_w, total = call(
        functools.partial(early_kernel, per_chunk, head_dim, vocab),
        (meta, skip_gain), (chunks - 1,),
        finish_ins(0, reader_in, writer_in) + [(total, anywhere, None)],
        [
            ((length, width), BF16, slab, HBM), ((length, width), BF16, slab, HBM),
            ((length, state_dim), F32, square, CHIP), ((length, state_dim), F32, square, CHIP),
            (total.shape, F32, anywhere, None),
        ],
        aliases={16: 4},
    )
    exchanged = [exchange(total) for exchange in exchanges]
    ins = finish_ins(chunks - 1, sum_c, sum_w) + [
        (got_up, whole(got_up.shape), None), (got_down, whole(got_down.shape), None),
        (mixed, anywhere, HBM), (grad_hidden, anywhere, HBM),
    ] + [(value, whole(value.shape), None) for value in [total] + exchanged]
    slab = chunk_specs(chunks - 1)[0]
    mixed, grad_hidden, grad_cmat, grad_bmat, grad_table, grad_skip = call(
        functools.partial(
            last_kernel, per_chunk, head_dim, vocab, bmat_scale,
            up_tables[0] + slots - 1, down_tables[0] + slots - 1, chunks - 1,
        ),
        (meta, skip_gain), (1,), ins,
        [
            ((length, width), BF16, slab, HBM), ((length, width), BF16, slab, HBM),
            ((length, state_dim), BF16, square, HBM), ((length, state_dim), BF16, square, HBM),
            (table.shape, F32, whole(table.shape), HBM),
            ((1, heads), F32, whole((1, heads)), HBM),
        ],
        [pltpu.VMEM((length, state_dim), F32)] * 2,
        aliases={18: 0, 19: 1},
    )
    return (
        mixed.reshape(hidden.shape),
        grad_hidden.reshape(hidden.shape),
        grad_bmat.reshape(bmat.shape),
        grad_cmat.reshape(cmat.shape),
        grad_table,
        grad_skip.reshape(heads),
    )


def solution(mesh):
    rows = P("rep", "dom", "ctx", None)
    return jax.shard_map(
        per_device,
        mesh=mesh,
        in_specs=(
            rows, rows, rows, P("rep", "dom", "ctx"), P(), rows, rows, P(),
            P("rep", "dom", "ctx", None, None), P("rep", "dom"), P("rep"), rows,
        ),
        out_specs=(rows, rows, rows, rows, P(), P()),
        check_vma=False,
    )
```

```python
import functools
import math

import jax
import jax.numpy as jnp
from jax import lax
from jax.experimental import pallas as pl
from jax.experimental.pallas import tpu as pltpu
from jax.sharding import PartitionSpec as P

F32 = jnp.float32
BF16 = jnp.bfloat16
EXACT = lax.Precision.HIGHEST
NN = (((1,), (0,)), ((), ()))
NT = (((1,), (1,)), ((), ()))
TN = (((0,), (0,)), ((), ()))
CHUNKS = 4
HBM, CHIP = pltpu.HBM, pltpu.VMEM


def dot(left, right, dims=NN, precision=None):
    return lax.dot_general(
        left, right, dims, precision=precision, preferred_element_type=F32
    )


def one_hot_rows(tokens_row, rows):
    kinds = lax.broadcasted_iota(jnp.int32, (rows, tokens_row.shape[1]), 0)
    return kinds == tokens_row


def live_rows(meta, shape):
    return meta[0] + lax.broadcasted_iota(jnp.int32, shape, 0) < meta[1]


def column(cols, kind, per_chunk, head):
    at = kind * per_chunk + head
    return cols[:, at : at + 1]


STEP, RISE, FALL, CUM = range(4)


def start_kernel(
    per_chunk, head_dim, vocab, chunks,
    meta, bmat, cmat, tokens, table, step_t, rate_t, hid_far, cot_far,
    x_first, y_first, small, cols, writer, hid, cot, sems,
):
    length = bmat.shape[0]
    state = bmat.shape[1]
    part = per_chunk * head_dim
    lines = small.shape[2]
    odd = meta[4] != 0
    copies = []
    for chunk in range(chunks):
        span = slice(chunk * part, (chunk + 1) * part)
        pair = [
            pltpu.make_async_copy(far.at[:, span], near.at[:, span], sems.at[chunk, at])
            for at, (far, near) in enumerate(((hid_far, hid), (cot_far, cot)))
        ]
        for copy in pair:
            copy.start()
        copies.append(pair)

    row = lax.broadcasted_iota(jnp.int32, (length, length), 0)
    col = lax.broadcasted_iota(jnp.int32, (length, length), 1)
    lower = jnp.where(col <= row, 1.0, 0.0).astype(F32)
    cumulative = dot(lower, rate_t[...], NT, EXACT)
    totals = cumulative[length - 1 : length, :]
    rising = jnp.exp(-cumulative)
    falling = jnp.exp(-(totals - cumulative))
    step = step_t[...].T
    for at in range(chunks):
        lo = at * per_chunk
        for kind, values in enumerate((step, rising, falling, cumulative)):
            cols[at, :, kind * per_chunk : (kind + 1) * per_chunk] = values[:, lo : lo + per_chunk]
    hot = one_hot_rows(tokens[...], vocab)
    looked = dot(jnp.where(hot, 1.0, 0.0).astype(F32), table[...], TN, EXACT)
    rows = (bmat[...].astype(F32) + looked).astype(BF16)
    writer[...] = rows
    chosen = jnp.where(one_hot_rows(tokens[...], lines), 1.0, 0.0).astype(BF16)
    kinds = lax.broadcasted_iota(jnp.int32, (lines, part), 0)
    live = live_rows(meta, (length, head_dim))
    for chunk in range(chunks):
        for copy in copies[chunk]:
            copy.wait()
        fallen, risen, grad_fallen, grad_risen, gone, skips = [], [], [], [], [], []
        for head in range(per_chunk):
            number = chunk * per_chunk + head
            at = slice(number * head_dim, (number + 1) * head_dim)
            rise = rising[:, number : number + 1]
            fall = falling[:, number : number + 1]
            values = hid[:, at].astype(F32)
            scaled = (step[:, number : number + 1] * values).astype(BF16).astype(F32)
            grads = jnp.where(live, cot[:, at].astype(F32), 0.0)
            fallen.append((fall * scaled).astype(BF16))
            risen.append((rise * scaled).astype(BF16))
            if chunk == 0:
                grad_fallen.append((fall * grads).astype(BF16))
                grad_risen.append((rise * grads).astype(BF16))
            gone.append(jnp.broadcast_to(rise[length - 1 : length, :], (1, head_dim)))
            skips.append(jnp.sum(values * grads, axis=0, keepdims=True))
        fallen, risen, gone, skips = (
            jnp.concatenate(parts, axis=1) for parts in (fallen, risen, gone, skips)
        )
        up_lines = jnp.where(
            kinds == vocab, jnp.where(meta[2] == 0, gone, 0.0), dot(chosen, fallen)
        )
        down_lines = jnp.where(
            kinds == vocab, gone, jnp.where(kinds == vocab + 1, skips, dot(chosen, risen))
        )
        small[0, chunk] = up_lines
        small[1, chunk] = down_lines
        small_rows = slice(2 * state + chunk * lines, 2 * state + (chunk + 1) * lines)
        x_first[small_rows, :] = jnp.where(odd, down_lines, up_lines)
        y_first[small_rows, :] = jnp.where(odd, up_lines, down_lines)
        if chunk == 0:
            ends = jnp.where(odd, risen, fallen)
            grad_ends = jnp.where(
                odd, jnp.concatenate(grad_risen, axis=1), jnp.concatenate(grad_fallen, axis=1)
            )
            x_first[0:state, :] = dot(rows.T, ends)
            x_first[state : 2 * state, :] = dot(cmat[...].T, grad_ends)
            y_first[0 : 2 * state, :] = jnp.zeros((2 * state, part), F32)


def head_copies(source, target, row, sems):
    heads, rows, width = source.shape
    return [
        pltpu.make_async_copy(
            source.at[head],
            target.at[pl.ds(row, rows), pl.ds(head * width, width)],
            sems.at[head],
        )
        for head in range(heads)
    ]


def relay_kernel(last, paired, meta, *refs):
    sources, (x, y, sems) = refs[:-5], refs[-3:]
    place, odd = meta[2], meta[4] != 0
    if paired:
        plans = [((place == 1) | (place == 2), y, sources)]
    else:
        before, after = sources
        inside, ahead = place > 0, place < last
        plans = [
            (inside & jnp.logical_not(odd), x, [before]), (inside & odd, y, [before]),
            (ahead & odd, x, [after]), (ahead & jnp.logical_not(odd), y, [after]),
        ]
    for at, (wanted, message, pieces) in enumerate(plans):
        copies = []
        for half, source in enumerate(pieces):
            copies += head_copies(source, message, half * source.shape[1], sems.at[at, half])

        @pl.when(wanted)
        def _():
            for copy in copies:
                copy.start()
            for copy in copies:
                copy.wait()


def gather_kernel(last, paired, meta, *refs):
    sources, begin, sems = refs[:-2], refs[-2], refs[-1]
    place = meta[2]
    if paired:
        rows = (lax.bitwise_xor(place, 1), place)
    else:
        rows = (jnp.where(place == 0, last + 1, place - 1), place + 1, place)
    copies = []
    for at, (source, row) in enumerate(zip(sources, rows, strict=True)):
        copies += head_copies(source, begin.at[row], 0, sems.at[at])
    for copy in copies:
        copy.start()
    for copy in copies:
        copy.wait()


def combine_kernel(vocab, has_small, has_begin, sends, slot, side, tables, *refs):
    meta, received, own, small = refs[:4]
    held = refs[-1 - has_begin]
    way = meta[4] if side else 1 - meta[4]
    state = own.shape[3]
    land, source, forward, piece, other = (at + slot for at in tables)
    if has_begin:
        begin = refs[-1]
        begin[meta[piece]] = received[0:state, 0 : begin.shape[2]]
        begin[meta[other]] = received[state : 2 * state, 0 : begin.shape[2]]
    held[way, meta[land]] = received[0 : 2 * state, :].astype(BF16)
    if not sends:
        return
    send = refs[-2 - has_begin]
    passing = meta[forward] != 0
    decay = jnp.where(passing, 1.0, small[1, meta[source], vocab : vocab + 1, :])
    adding = jnp.where(passing, 0.0, 1.0)
    if has_small:
        lines = small.shape[2]
        for at in range(small.shape[1]):
            rows = slice(2 * state + at * lines, 2 * state + (at + 1) * lines)
            send[rows, :] = (
                small[1, at, vocab : vocab + 1, :] * received[rows, :] + small[way, at]
            )
    for at in range(2):
        rows = slice(at * state, (at + 1) * state)
        send[rows, :] = decay * received[rows, :] + adding * own[way, meta[source], at]


def inner_kernel(
    per_chunk, head_dim, vocab,
    meta, hid, cot, writer, cmat, tokens, cols,
    ends, mixed_in, back_in, reader_in, writer_in, tab,
    inner, inner_t, cross, writer_t, reader_t,
):
    chunk = pl.program_id(0)
    length = hid.shape[0]

    @pl.when(chunk == 0)
    def _():
        inner[...] = dot(cmat[...], writer[...], NT)
        inner_t[...] = dot(writer[...], cmat[...], NT)
        cross[...] = jnp.zeros_like(cross)
        writer_t[...] = writer[...].T
        reader_t[...] = cmat[...].T

    mine = cols[0]
    across = mine.T
    live = live_rows(meta, (length, head_dim))
    fallen, risen, grad_fallen, grad_risen = [], [], [], []
    for head in range(per_chunk):
        at = slice(head * head_dim, (head + 1) * head_dim)
        row = CUM * per_chunk + head
        decay = jnp.exp(
            -jnp.abs(column(mine, CUM, per_chunk, head) - across[row : row + 1, :])
        )
        rise = column(mine, RISE, per_chunk, head)
        fall = column(mine, FALL, per_chunk, head)
        scaled = (column(mine, STEP, per_chunk, head) * hid[:, at].astype(F32)).astype(BF16)
        grads_wide = jnp.where(live, cot[:, at].astype(F32), 0.0)
        grads = grads_wide.astype(BF16)
        scaled_wide = scaled.astype(F32)
        fallen.append((fall * scaled_wide).astype(BF16))
        risen.append((rise * scaled_wide).astype(BF16))
        grad_fallen.append((fall * grads_wide).astype(BF16))
        grad_risen.append((rise * grads_wide).astype(BF16))
        mixed_in[:, at] = dot((decay * inner[...]).astype(BF16), scaled)
        back_in[:, at] = dot((decay * inner_t[...]).astype(BF16), grads)
        cross[...] += decay * dot(grads, scaled, NT)
    ends[0, 0, 0] = dot(writer_t[...], jnp.concatenate(fallen, axis=1))
    ends[0, 0, 1] = dot(reader_t[...], jnp.concatenate(grad_fallen, axis=1))
    ends[1, 0, 0] = dot(writer_t[...], jnp.concatenate(risen, axis=1))
    ends[1, 0, 1] = dot(reader_t[...], jnp.concatenate(grad_risen, axis=1))

    @pl.when(chunk == pl.num_programs(0) - 1)
    def _():
        crossed = cross[...].astype(BF16)
        reader_in[...] = dot(crossed, writer[...])
        into = dot(crossed.astype(F32).T.astype(BF16), cmat[...])
        writer_in[...] = into
        chosen = jnp.where(one_hot_rows(tokens[...], tab.shape[0]), 1.0, 0.0).astype(F32)
        tab[...] = dot(chosen, into, precision=EXACT)


def sums_kernel(
    per_chunk, head_dim, vocab, table_scale, skip_scale,
    meta, from_x, from_y, small, grad_up, grad_down, tab, total, acc,
):
    chunk = pl.program_id(0)
    lines, width = from_x.shape
    odd = meta[4] != 0
    earlier = jnp.where(odd, from_x[...], from_y[...])
    later = jnp.where(odd, from_y[...], from_x[...])

    @pl.when(chunk == 0)
    def _():
        acc[...] = jnp.zeros_like(acc)

    def split(lhs, rhs):
        high = lhs.astype(BF16)
        low = (lhs - high.astype(F32)).astype(BF16)
        both = dot(jnp.concatenate([high, low], axis=0), rhs.astype(BF16), NT)
        return both[0:lines] + both[lines:]

    head_of = chunk * per_chunk + lax.broadcasted_iota(jnp.int32, (128, width), 1) // head_dim
    picks = jnp.where(
        head_of == lax.broadcasted_iota(jnp.int32, (128, width), 0), 1.0, 0.0
    ).astype(F32)
    kinds = lax.broadcasted_iota(jnp.int32, (lines, 128), 0)
    tables = split(later, grad_up[0, 0, 0]) + split(earlier, grad_down[0, 0, 0])
    skips = jnp.broadcast_to(small[0, 0, vocab + 1 : vocab + 2, :], (lines, width))
    acc[...] += jnp.where(kinds < vocab, tables, split(skips, picks))

    @pl.when(chunk == pl.num_programs(0) - 1)
    def _():
        total[...] = jnp.where(
            kinds < vocab,
            (acc[...] + tab[...]) * table_scale,
            jnp.where(kinds == vocab, acc[...] * skip_scale, 0.0),
        )


def finish_chunk(
    per_chunk, head_dim, vocab, meta, chunk, gains, hid, cot, writer, cmat, mine,
    mixed_in, back_in, chain_in, chain_back, begin_here, begin_there, from_x, from_y,
    mixed, grad_hidden, acc_c, acc_w,
):
    length = hid.shape[0]
    state = chain_in.shape[0] // 2
    live = live_rows(meta, (length, head_dim))
    begins = []
    for at in range(begin_here.shape[0]):
        value = jnp.where(meta[3] != 0, begin_here[at], begin_there[at])
        for lane in range(0, value.shape[1], state):
            begins.append(value[:, lane : lane + state].T)
    begins = jnp.concatenate(begins, axis=1)
    row = slice(vocab, vocab + 1)
    passed = jnp.where(meta[4] != 0, from_x[row, :], from_y[row, :])
    passed = jnp.where(meta[2] == 0, 1.0, passed)
    state_in = (chain_in[0:state].astype(F32) + passed * begins).astype(BF16)
    grad_in = chain_in[state:]
    state_back = chain_back[0:state]
    grad_back = chain_back[state:]
    from_in = dot(cmat, state_in)
    from_back = dot(cmat, state_back)
    grad_from_in = dot(writer, grad_in)
    grad_from_back = dot(writer, grad_back)
    fallen, risen, grad_fallen, grad_risen = [], [], [], []
    for head in range(per_chunk):
        at = slice(head * head_dim, (head + 1) * head_dim)
        rise = column(mine, RISE, per_chunk, head)
        fall = column(mine, FALL, per_chunk, head)
        step = column(mine, STEP, per_chunk, head)
        gain = gains[chunk * per_chunk + head]
        values = hid[:, at].astype(F32)
        scaled = (step * values).astype(BF16).astype(F32)
        grads = jnp.where(live, cot[:, at].astype(F32), 0.0)
        mixed[:, at] = (
            mixed_in[:, at] + rise * from_in[:, at] + fall * from_back[:, at] + gain * values
        ).astype(BF16)
        back = back_in[:, at] + rise * grad_from_in[:, at] + fall * grad_from_back[:, at]
        grad_hidden[:, at] = (step * back + gain * grads).astype(BF16)
        fallen.append((fall * scaled).astype(BF16))
        risen.append((rise * scaled).astype(BF16))
        grad_fallen.append((fall * grads).astype(BF16))
        grad_risen.append((rise * grads).astype(BF16))
    fallen, risen, grad_fallen, grad_risen = (
        jnp.concatenate(parts, axis=1) for parts in (fallen, risen, grad_fallen, grad_risen)
    )
    acc_c[...] += dot(grad_risen, state_in, NT) + dot(grad_fallen, state_back, NT)
    acc_w[...] += dot(risen, grad_in, NT) + dot(fallen, grad_back, NT)


def early_kernel(
    per_chunk, head_dim, vocab,
    meta, gains, hid, cot, writer, cmat, cols, mixed_in, back_in, reader_in, writer_in,
    held_up, held_down, begin_here, begin_there, from_x, from_y, *refs,
):
    mixed, grad_hidden, acc_c, acc_w = refs[-5:-1]
    chunk = pl.program_id(0)

    @pl.when(chunk == 0)
    def _():
        acc_c[...] = reader_in[...]
        acc_w[...] = writer_in[...]

    finish_chunk(
        per_chunk, head_dim, vocab, meta, chunk, gains, hid, cot, writer[...], cmat[...],
        cols[0], mixed_in, back_in, held_up[0, 0], held_down[0, 0], begin_here, begin_there, from_x, from_y,
        mixed, grad_hidden, acc_c, acc_w,
    )


def last_kernel(
    per_chunk, head_dim, vocab, bmat_scale, land, chunk,
    meta, gains, hid, cot, writer, cmat, cols, mixed_in, back_in, sum_c, sum_w,
    held_up, held_down, begin_here, begin_there, from_x, from_y, got, *refs,
):
    sums = refs[2:-8]
    mixed, grad_hidden, grad_cmat, grad_bmat, grad_table, grad_skip, acc_c, acc_w = refs[-8:]
    total = sums[0][...]
    for value in sums[1:]:
        total = total + value[...]
    vocab_rows, heads = grad_table.shape[0], grad_skip.shape[1]
    grad_table[...] = total[0:vocab_rows, :]
    grad_skip[...] = total[vocab_rows : vocab_rows + 1, 0:heads]
    acc_c[...] = sum_c[...]
    acc_w[...] = sum_w[...]
    fresh, odd = meta[land] == chunk, meta[4] != 0
    arrived = got[...].astype(BF16)
    chain_in = jnp.where(fresh & odd, arrived, held_up[0, 0])
    chain_back = jnp.where(fresh & jnp.logical_not(odd), arrived, held_down[0, 0])
    finish_chunk(
        per_chunk, head_dim, vocab, meta, chunk, gains, hid, cot, writer[...], cmat[...],
        cols[0], mixed_in, back_in, chain_in, chain_back, begin_here, begin_there, from_x, from_y,
        mixed, grad_hidden, acc_c, acc_w,
    )
    grad_cmat[...] = acc_c[...].astype(BF16)
    grad_bmat[...] = (acc_w[...] * bmat_scale).astype(BF16)


def whole(shape):
    return pl.BlockSpec(shape, lambda *_: (0,) * len(shape))


def call(body, scalars, grid, ins, outs, scratch=(), aliases=None, limit=16 << 20):
    results = pl.pallas_call(
        body,
        out_shape=[
            jax.ShapeDtypeStruct(shape, kind) if place is None else place(shape, kind)
            for shape, kind, _, place in outs
        ],
        grid_spec=pltpu.PrefetchScalarGridSpec(
            num_scalar_prefetch=len(scalars),
            grid=grid,
            in_specs=[spec for _, spec, _ in ins],
            out_specs=[spec for _, _, spec, _ in outs],
            scratch_shapes=list(scratch),
        ),
        input_output_aliases=aliases or {},
        compiler_params=pltpu.CompilerParams(vmem_limit_bytes=limit),
    )(
        *scalars,
        *[
            array if place is None else pltpu.with_memory_space_constraint(array, place)
            for array, _, place in ins
        ],
    )
    return results


def sum_steps(axes):
    steps, last = [], []
    for axis in axes:
        count = lax.axis_size(axis)
        if count & (count - 1):
            steps.append(functools.partial(lax.psum, axis_name=axis))
            continue
        hop = 1
        while hop < count:
            hops = [hop]
            if axis == axes[-1] and 4 * hop >= count:
                hops = range(hop, count, hop)
            group = [
                functools.partial(
                    lax.ppermute, axis_name=axis, perm=[(at, at ^ far) for at in range(count)]
                )
                for far in hops
            ]
            if axis == axes[-1] and 4 * hop >= count:
                last = group
                break
            steps.append(lambda value, group=group: value + group[0](value))
            hop *= 2
    return steps, last


def per_device(
    hidden, bmat, cmat, tokens, table, step_size, log_decay, skip_gain,
    prev_state, ancestors, suffix_start, cotangent,
):
    prompts, parts, length, width = hidden.shape
    assert prompts * parts == 1
    heads = skip_gain.shape[0]
    head_dim = width // heads
    state_dim = bmat.shape[3]
    vocab = table.shape[0]
    count = lax.axis_size("ctx")
    doms = lax.axis_size("dom")
    place = lax.axis_index("ctx")
    chunks = CHUNKS
    per_chunk = heads // chunks
    part = width // chunks
    total_rows = length * count * doms * lax.axis_size("rep")
    bmat_scale = 1.0 / math.sqrt(width)
    total_scale = 1.0 / math.sqrt(total_rows)
    lines = -(-(vocab + 2) // 8) * 8
    slots = chunks + count - 2
    paired = count == 4

    hid = hidden.reshape(length, width)
    cot = cotangent.reshape(length, width)
    writes = bmat.reshape(length, state_dim)
    reads = cmat.reshape(length, state_dim)
    toks = tokens.reshape(1, length)
    steps_t = jnp.swapaxes(step_size, 2, 3).reshape(heads, length)
    rates_t = jnp.swapaxes(log_decay, 2, 3).reshape(heads, length)
    ancestor = ancestors[0, 0]
    here = ancestor == lax.axis_index("dom")

    times = jnp.arange(slots, dtype=jnp.int32)
    from_last = count - 1 - place
    odd = place % 2
    table_of = []
    for upward_here in (odd == 1, odd == 0):
        far = jnp.where(upward_here, place, from_last)
        lands = times - jnp.maximum(far, 1) + 1
        if paired:
            arrives = times + 2 == far
            pieces = jnp.where(arrives, jnp.where(upward_here, 0, 3), count)
            others = jnp.where(arrives, jnp.where(upward_here, 1, 2), count)
        else:
            pieces = place + jnp.where(upward_here, -1, 1) * (times + 2)
            pieces = jnp.where((pieces >= 0) & (pieces < count), pieces, count)
            others = jnp.full_like(times, count)
        table_of += [
            jnp.where((lands >= 0) & (lands < chunks), lands, chunks),
            jnp.clip(times + 1 - far, 0, chunks - 1),
            (times + 1 < far).astype(jnp.int32),
            pieces, others,
        ]
    base = [place * length, suffix_start[0], place, here, odd]
    base = jnp.stack([jnp.asarray(value, jnp.int32) for value in base])
    meta = jnp.concatenate([base] + [value.astype(jnp.int32) for value in table_of])
    tables = [[5 + (5 * side + at) * slots for at in range(5)] for side in range(2)]

    upward = [(at, at + 1) for at in range(count - 1)]
    downward = [(at + 1, at) for at in range(count - 1)]
    own_state = prev_state[0, 0]
    local_heads = own_state.shape[0]
    assert per_chunk % local_heads == 0
    if doms != 2:
        own_state = lax.dynamic_index_in_dim(
            lax.all_gather(own_state, "dom"), ancestor, 0, keepdims=False
        )
    if paired:
        swap = [(at, at ^ 1) for at in range(count)]
        pieces = [lax.ppermute(own_state, "ctx", swap), own_state]
    else:
        pieces = [lax.ppermute(own_state, "ctx", way) for way in (upward, downward)]

    anywhere = pl.BlockSpec(memory_space=pl.ANY)
    near = pl.BlockSpec(memory_space=pltpu.VMEM)
    by_chunk = pl.BlockSpec((length, part), lambda k, *_: (0, k))
    one_cols = pl.BlockSpec((1, length, 128), lambda k, *_: (k, 0, 0))
    pair = pl.BlockSpec((2, 1, 2, state_dim, part), lambda k, *_: (0, k, 0, 0, 0))
    one_small = pl.BlockSpec((1, 1, lines, part), lambda k, *_: (1, k, 0, 0))
    square = whole((length, state_dim))
    tok_spec = whole((1, length))
    full_rows = 2 * state_dim + chunks * lines
    small_shape = (2, chunks, lines, part)
    first = ((full_rows, part), F32, near, CHIP)

    x_first, y_first, small, cols, writer, hid, cot = call(
        functools.partial(start_kernel, per_chunk, head_dim, vocab, chunks),
        (meta,), (1,),
        [
            (writes, square, HBM), (reads, square, HBM), (toks, tok_spec, HBM),
            (table, whole(table.shape), HBM), (steps_t, whole(steps_t.shape), HBM),
            (rates_t, whole(rates_t.shape), HBM), (hid, anywhere, HBM), (cot, anywhere, HBM),
        ],
        [
            first, first,
            (small_shape, F32, near, CHIP),
            ((chunks, length, 128), F32, near, CHIP), ((length, state_dim), BF16, near, CHIP),
            ((length, width), BF16, near, CHIP), ((length, width), BF16, near, CHIP),
        ],
        [pltpu.SemaphoreType.DMA((chunks, 2))],
    )

    x_first, y_first = call(
        functools.partial(relay_kernel, count - 1, paired),
        (meta,), (),
        [(piece, anywhere, None) for piece in pieces]
        + [(x_first, near, CHIP), (y_first, near, CHIP)],
        [
            ((full_rows, part), F32, near, CHIP), ((full_rows, part), F32, near, CHIP),
        ],
        [pltpu.SemaphoreType.DMA((4, 2, local_heads))],
        aliases={3: 0, 4: 1},
    )
    begin_shape = (count + 1, head_dim, local_heads * state_dim)
    (begin_here,) = call(
        functools.partial(gather_kernel, count - 1, paired),
        (meta,), (),
        [
            (piece, anywhere, None) for piece in (pieces if paired else pieces + [own_state])
        ],
        [(begin_shape, F32, near, CHIP)],
        [pltpu.SemaphoreType.DMA((3, local_heads))],
    )

    ends, mixed_in, back_in, reader_in, writer_in, tab = call(
        functools.partial(inner_kernel, per_chunk, head_dim, vocab),
        (meta,), (chunks,),
        [
            (hid, by_chunk, CHIP), (cot, by_chunk, CHIP), (writer, square, CHIP),
            (reads, square, HBM), (toks, tok_spec, HBM), (cols, one_cols, CHIP),
        ],
        [
            ((2, chunks, 2, state_dim, part), F32, pair, CHIP),
            ((length, width), F32, by_chunk, CHIP),
            ((length, width), F32, by_chunk, CHIP),
            ((length, state_dim), F32, square, CHIP),
            ((length, state_dim), F32, square, CHIP),
            ((lines, state_dim), F32, whole((lines, state_dim)), CHIP),
        ],
        [pltpu.VMEM((length, length), F32)] * 3 + [pltpu.VMEM((state_dim, length), BF16)] * 2,
    )

    def step_chain(slot, side, received, held, begin, waits):
        has_small = slot < count - 2
        has_begin = slot < count - 2
        sends = side == 1 or slot + 1 < slots - 1
        rows = full_rows if has_small else 2 * state_dim
        held_shape = (2, chunks + 1, 2 * state_dim, part)
        ins = [(received, near, CHIP), (ends, near, CHIP), (small, near, CHIP)]
        outs = [((rows, part), F32, near, CHIP)] if sends else []
        outs.append((held_shape, BF16, near, CHIP))
        aliases = {}
        if held is not None:
            aliases[1 + len(ins)] = len(outs) - 1
            ins.append((held, near, CHIP))
        if has_begin:
            aliases[1 + len(ins)] = len(outs)
            ins.append((begin, near, CHIP))
            outs.append((begin_shape, F32, near, CHIP))
        ins += [(value, anywhere, None) for value in waits]
        results = call(
            functools.partial(
                combine_kernel, vocab, has_small, has_begin, sends, slot, side, tables[side]
            ),
            (meta,), (), ins, outs,
            aliases=aliases,
        )
        results = list(results) if has_begin else [*results, begin]
        return results if sends else [None, *results]

    lines_at = 2 * state_dim // lines
    from_slot = pl.BlockSpec((lines, part), lambda k, *_: (lines_at + k, 0))
    grad_parts = [
        pl.BlockSpec((1, 1, 1, state_dim, part), lambda k, *_, way=way: (way, k, 1, 0, 0))
        for way in range(2)
    ]
    sums, exchanges = sum_steps(("rep", "dom", "ctx"))
    assert count % 2 == 0
    even_links = [(at, at ^ 1) for at in range(count)]
    odd_links = [(at, (at - 1 ^ 1) + 1) for at in range(1, count - 1)]
    send_x, send_y, held = x_first, y_first, None
    for slot in range(slots):
        got_x = lax.ppermute(send_x, "ctx", even_links)
        if slot < slots - 1:
            got_y = lax.ppermute(send_y, "ctx", odd_links)
        waits_up, waits_down = [], []
        if slot == count - 2:
            from_x, from_y = got_x, got_y
        if slot == count - 1:
            begin_there = begin_here
            if doms == 2:
                begin_there = lax.ppermute(begin_here, "dom", [(0, 1), (1, 0)])
            (total,) = call(
                functools.partial(
                    sums_kernel, per_chunk, head_dim, vocab,
                    bmat_scale * total_scale, total_scale / math.sqrt(head_dim),
                ),
                (meta,), (chunks,),
                [
                    (from_x, from_slot, None), (from_y, from_slot, None),
                    (small, one_small, CHIP), (ends, grad_parts[0], CHIP),
                    (ends, grad_parts[1], CHIP), (tab, whole(tab.shape), CHIP),
                ],
                [((lines, state_dim), F32, whole((lines, state_dim)), None)],
                [pltpu.VMEM((lines, state_dim), F32)],
            )
        if slot == slots - 1:
            break
        if slot >= count - 1:
            if slot > count - 1:
                waits_down.append(begin_there)
                for step in sums[:1]:
                    total = step(total)
                sums = sums[1:]
            waits_down.append(total)
        send_y, held, begin_here = step_chain(slot, 0, got_x, held, begin_here, waits_down)
        if slot >= count - 1:
            for step in sums[:1]:
                total = step(total)
            sums = sums[1:]
            waits_up.append(total)
        send_x, held, begin_here = step_chain(slot, 1, got_y, held, begin_here, waits_up)

    def chunk_specs(at):
        return (
            pl.BlockSpec((length, part), lambda k, *_: (0, k + at)),
            pl.BlockSpec((1, length, 128), lambda k, *_: (k + at, 0, 0)),
            [
                pl.BlockSpec(
                    (1, 1, 2 * state_dim, part), lambda k, *_, way=way: (way, k + at, 0, 0)
                )
                for way in range(2)
            ],
            pl.BlockSpec(
                (per_chunk // local_heads, head_dim, local_heads * state_dim),
                lambda k, *_: (k + at, 0, 0),
            ),
            pl.BlockSpec((lines, part), lambda k, *_: (lines_at + k + at, 0)),
        )

    def finish_ins(at, sum_c, sum_w):
        slab, col, chain, states, rows = chunk_specs(at)
        return [
            (hid, slab, CHIP), (cot, slab, CHIP), (writer, square, CHIP), (reads, square, HBM),
            (cols, col, CHIP), (mixed_in, slab, CHIP), (back_in, slab, CHIP),
            (sum_c, square, CHIP), (sum_w, square, CHIP),
            (held, chain[0], CHIP), (held, chain[1], CHIP),
            (begin_here, states, CHIP), (begin_there, states, CHIP), (from_x, rows, None), (from_y, rows, None),
        ]

    for step in sums:
        total = step(total)
    slab = chunk_specs(0)[0]
    mixed, grad_hidden, sum_c, sum_w, total = call(
        functools.partial(early_kernel, per_chunk, head_dim, vocab),
        (meta, skip_gain), (chunks - 1,),
        finish_ins(0, reader_in, writer_in) + [(total, anywhere, None)],
        [
            ((length, width), BF16, slab, HBM), ((length, width), BF16, slab, HBM),
            ((length, state_dim), F32, square, CHIP), ((length, state_dim), F32, square, CHIP),
            (total.shape, F32, anywhere, None),
        ],
        aliases={17: 4},
    )
    exchanged = [exchange(total) for exchange in exchanges]
    ins = finish_ins(chunks - 1, sum_c, sum_w) + [
        (got_x, whole(got_x.shape), None),
        (mixed, anywhere, HBM), (grad_hidden, anywhere, HBM),
    ] + [(value, whole(value.shape), None) for value in [total] + exchanged]
    slab = chunk_specs(chunks - 1)[0]
    mixed, grad_hidden, grad_cmat, grad_bmat, grad_table, grad_skip = call(
        functools.partial(
            last_kernel, per_chunk, head_dim, vocab, bmat_scale,
            tables[0][0] + slots - 1, chunks - 1,
        ),
        (meta, skip_gain), (1,), ins,
        [
            ((length, width), BF16, slab, HBM), ((length, width), BF16, slab, HBM),
            ((length, state_dim), BF16, square, HBM), ((length, state_dim), BF16, square, HBM),
            (table.shape, F32, whole(table.shape), HBM),
            ((1, heads), F32, whole((1, heads)), HBM),
        ],
        [pltpu.VMEM((length, state_dim), F32)] * 2,
        aliases={18: 0, 19: 1},
    )
    return (
        mixed.reshape(hidden.shape),
        grad_hidden.reshape(hidden.shape),
        grad_bmat.reshape(bmat.shape),
        grad_cmat.reshape(cmat.shape),
        grad_table,
        grad_skip.reshape(heads),
    )


def solution(mesh):
    rows = P("rep", "dom", "ctx", None)
    return jax.shard_map(
        per_device,
        mesh=mesh,
        in_specs=(
            rows, rows, rows, P("rep", "dom", "ctx"), P(), rows, rows, P(),
            P("rep", "dom", "ctx", None, None), P("rep", "dom"), P("rep"), rows,
        ),
        out_specs=(rows, rows, rows, rows, P(), P()),
        check_vma=False,
    )
```

```python
import functools
import math

import jax
import jax.numpy as jnp
from jax import lax
from jax.experimental import pallas as pl
from jax.experimental.pallas import tpu as pltpu
from jax.sharding import PartitionSpec as P

F32 = jnp.float32
BF16 = jnp.bfloat16
EXACT = lax.Precision.HIGHEST
NN = (((1,), (0,)), ((), ()))
NT = (((1,), (1,)), ((), ()))
TN = (((0,), (0,)), ((), ()))
CHUNKS = 4
HBM, CHIP = pltpu.HBM, pltpu.VMEM


def dot(left, right, dims=NN, precision=None):
    return lax.dot_general(
        left, right, dims, precision=precision, preferred_element_type=F32
    )


def one_hot_rows(tokens_row, rows):
    kinds = lax.broadcasted_iota(jnp.int32, (rows, tokens_row.shape[1]), 0)
    return kinds == tokens_row


def live_rows(meta, shape):
    return meta[0] + lax.broadcasted_iota(jnp.int32, shape, 0) < meta[1]


def column(cols, kind, per_chunk, head):
    at = kind * per_chunk + head
    return cols[:, at : at + 1]


STEP, RISE, FALL, CUM = range(4)


def start_kernel(
    per_chunk, head_dim, vocab, chunks,
    meta, bmat, cmat, tokens, table, step_t, rate_t, hid_far, cot_far, state_far,
    x_first, y_first, small, cols, writer, hid, cot, state_near, sems,
):
    length = bmat.shape[0]
    state = bmat.shape[1]
    part = per_chunk * head_dim
    lines = small.shape[2]
    odd = meta[4] != 0
    copies = []
    for chunk in range(chunks):
        span = slice(chunk * part, (chunk + 1) * part)
        pair = [
            pltpu.make_async_copy(far.at[:, span], near.at[:, span], sems.at[chunk, at])
            for at, (far, near) in enumerate(((hid_far, hid), (cot_far, cot)))
        ]
        for copy in pair:
            copy.start()
        copies.append(pair)
    keep = pltpu.make_async_copy(state_far, state_near, sems.at[chunks, 0])
    keep.start()

    row = lax.broadcasted_iota(jnp.int32, (length, length), 0)
    col = lax.broadcasted_iota(jnp.int32, (length, length), 1)
    lower = jnp.where(col <= row, 1.0, 0.0).astype(F32)
    cumulative = dot(lower, rate_t[...], NT, EXACT)
    totals = cumulative[length - 1 : length, :]
    rising = jnp.exp(-cumulative)
    falling = jnp.exp(-(totals - cumulative))
    step = step_t[...].T
    for at in range(chunks):
        lo = at * per_chunk
        for kind, values in enumerate((step, rising, falling, cumulative)):
            cols[at, :, kind * per_chunk : (kind + 1) * per_chunk] = values[:, lo : lo + per_chunk]
    hot = one_hot_rows(tokens[...], vocab)
    looked = dot(jnp.where(hot, 1.0, 0.0).astype(F32), table[...], TN, EXACT)
    rows = (bmat[...].astype(F32) + looked).astype(BF16)
    writer[...] = rows
    chosen = jnp.where(one_hot_rows(tokens[...], lines), 1.0, 0.0).astype(BF16)
    kinds = lax.broadcasted_iota(jnp.int32, (lines, part), 0)
    live = live_rows(meta, (length, head_dim))
    for chunk in range(chunks):
        for copy in copies[chunk]:
            copy.wait()
        fallen, risen, grad_fallen, grad_risen, gone, skips = [], [], [], [], [], []
        for head in range(per_chunk):
            number = chunk * per_chunk + head
            at = slice(number * head_dim, (number + 1) * head_dim)
            rise = rising[:, number : number + 1]
            fall = falling[:, number : number + 1]
            values = hid[:, at].astype(F32)
            scaled = (step[:, number : number + 1] * values).astype(BF16).astype(F32)
            grads = jnp.where(live, cot[:, at].astype(F32), 0.0)
            fallen.append((fall * scaled).astype(BF16))
            risen.append((rise * scaled).astype(BF16))
            if chunk == 0:
                grad_fallen.append((fall * grads).astype(BF16))
                grad_risen.append((rise * grads).astype(BF16))
            gone.append(jnp.broadcast_to(rise[length - 1 : length, :], (1, head_dim)))
            skips.append(jnp.sum(values * grads, axis=0, keepdims=True))
        fallen, risen, gone, skips = (
            jnp.concatenate(parts, axis=1) for parts in (fallen, risen, gone, skips)
        )
        up_lines = jnp.where(
            kinds == vocab, jnp.where(meta[2] == 0, gone, 0.0), dot(chosen, fallen)
        )
        down_lines = jnp.where(
            kinds == vocab, gone, jnp.where(kinds == vocab + 1, skips, dot(chosen, risen))
        )
        small[0, chunk] = up_lines
        small[1, chunk] = down_lines
        small_rows = slice(2 * state + chunk * lines, 2 * state + (chunk + 1) * lines)
        x_first[small_rows, :] = jnp.where(odd, down_lines, up_lines)
        y_first[small_rows, :] = jnp.where(odd, up_lines, down_lines)
        if chunk == 0:
            ends = jnp.where(odd, risen, fallen)
            grad_ends = jnp.where(
                odd, jnp.concatenate(grad_risen, axis=1), jnp.concatenate(grad_fallen, axis=1)
            )
            x_first[0:state, :] = dot(rows.T, ends)
            x_first[state : 2 * state, :] = dot(cmat[...].T, grad_ends)
            y_first[0 : 2 * state, :] = jnp.zeros((2 * state, part), F32)
    keep.wait()


def head_copies(source, target, row, sems):
    heads, rows, width = source.shape
    return [
        pltpu.make_async_copy(
            source.at[head],
            target.at[pl.ds(row, rows), pl.ds(head * width, width)],
            sems.at[head],
        )
        for head in range(heads)
    ]


def relay_kernel(last, paired, meta, *refs):
    sources, (x, y, sems) = refs[:-5], refs[-3:]
    place, odd = meta[2], meta[4] != 0
    if paired:
        plans = [((place == 1) | (place == 2), y, sources)]
    else:
        before, after = sources
        inside, ahead = place > 0, place < last
        plans = [
            (inside & jnp.logical_not(odd), x, [before]), (inside & odd, y, [before]),
            (ahead & odd, x, [after]), (ahead & jnp.logical_not(odd), y, [after]),
        ]
    for at, (wanted, message, pieces) in enumerate(plans):
        copies = []
        for half, source in enumerate(pieces):
            copies += head_copies(source, message, half * source.shape[1], sems.at[at, half])

        @pl.when(wanted)
        def _():
            for copy in copies:
                copy.start()
            for copy in copies:
                copy.wait()


def gather_kernel(last, paired, meta, *refs):
    sources, begin, sems = refs[:-2], refs[-2], refs[-1]
    place = meta[2]
    if paired:
        rows = (lax.bitwise_xor(place, 1), place)
    else:
        rows = (jnp.where(place == 0, last + 1, place - 1), place + 1, place)
    copies = []
    for at, (source, row) in enumerate(zip(sources, rows, strict=True)):
        copies += head_copies(source, begin.at[row], 0, sems.at[at])
    for copy in copies:
        copy.start()
    for copy in copies:
        copy.wait()


def combine_kernel(vocab, has_small, has_begin, sends, slot, side, tables, *refs):
    meta, received, own, small = refs[:4]
    held = refs[-1 - has_begin]
    way = meta[4] if side else 1 - meta[4]
    state = own.shape[3]
    land, source, forward, piece, other = (at + slot for at in tables)
    if has_begin:
        begin = refs[-1]
        begin[meta[piece]] = received[0:state, 0 : begin.shape[2]]
        begin[meta[other]] = received[state : 2 * state, 0 : begin.shape[2]]
    held[way, meta[land]] = received[0 : 2 * state, :].astype(BF16)
    if not sends:
        return
    send = refs[-2 - has_begin]
    passing = meta[forward] != 0
    decay = jnp.where(passing, 1.0, small[1, meta[source], vocab : vocab + 1, :])
    adding = jnp.where(passing, 0.0, 1.0)
    if has_small:
        lines = small.shape[2]
        for at in range(small.shape[1]):
            rows = slice(2 * state + at * lines, 2 * state + (at + 1) * lines)
            send[rows, :] = (
                small[1, at, vocab : vocab + 1, :] * received[rows, :] + small[way, at]
            )
    for at in range(2):
        rows = slice(at * state, (at + 1) * state)
        send[rows, :] = decay * received[rows, :] + adding * own[way, meta[source], at]


def inner_kernel(
    per_chunk, head_dim, vocab,
    meta, hid, cot, writer, cmat, tokens, cols,
    ends, mixed_in, back_in, reader_in, writer_in, tab,
    inner, inner_t, cross, writer_t, reader_t,
):
    chunk = pl.program_id(0)
    length = hid.shape[0]

    @pl.when(chunk == 0)
    def _():
        inner[...] = dot(cmat[...], writer[...], NT)
        inner_t[...] = dot(writer[...], cmat[...], NT)
        cross[...] = jnp.zeros_like(cross)
        writer_t[...] = writer[...].T
        reader_t[...] = cmat[...].T

    mine = cols[0]
    across = mine.T
    live = live_rows(meta, (length, head_dim))
    fallen, risen, grad_fallen, grad_risen = [], [], [], []
    for head in range(per_chunk):
        at = slice(head * head_dim, (head + 1) * head_dim)
        row = CUM * per_chunk + head
        decay = jnp.exp(
            -jnp.abs(column(mine, CUM, per_chunk, head) - across[row : row + 1, :])
        )
        rise = column(mine, RISE, per_chunk, head)
        fall = column(mine, FALL, per_chunk, head)
        scaled = (column(mine, STEP, per_chunk, head) * hid[:, at].astype(F32)).astype(BF16)
        grads_wide = jnp.where(live, cot[:, at].astype(F32), 0.0)
        grads = grads_wide.astype(BF16)
        scaled_wide = scaled.astype(F32)
        fallen.append((fall * scaled_wide).astype(BF16))
        risen.append((rise * scaled_wide).astype(BF16))
        grad_fallen.append((fall * grads_wide).astype(BF16))
        grad_risen.append((rise * grads_wide).astype(BF16))
        mixed_in[:, at] = dot((decay * inner[...]).astype(BF16), scaled)
        back_in[:, at] = dot((decay * inner_t[...]).astype(BF16), grads)
        cross[...] += decay * dot(grads, scaled, NT)
    ends[0, 0, 0] = dot(writer_t[...], jnp.concatenate(fallen, axis=1))
    ends[0, 0, 1] = dot(reader_t[...], jnp.concatenate(grad_fallen, axis=1))
    ends[1, 0, 0] = dot(writer_t[...], jnp.concatenate(risen, axis=1))
    ends[1, 0, 1] = dot(reader_t[...], jnp.concatenate(grad_risen, axis=1))

    @pl.when(chunk == pl.num_programs(0) - 1)
    def _():
        crossed = cross[...].astype(BF16)
        reader_in[...] = dot(crossed, writer[...])
        into = dot(crossed.astype(F32).T.astype(BF16), cmat[...])
        writer_in[...] = into
        chosen = jnp.where(one_hot_rows(tokens[...], tab.shape[0]), 1.0, 0.0).astype(F32)
        tab[...] = dot(chosen, into, precision=EXACT)


def sums_kernel(
    per_chunk, head_dim, vocab, table_scale, skip_scale,
    meta, from_x, from_y, small, grad_up, grad_down, tab, total, acc,
):
    chunk = pl.program_id(0)
    lines, width = from_x.shape
    odd = meta[4] != 0
    earlier = jnp.where(odd, from_x[...], from_y[...])
    later = jnp.where(odd, from_y[...], from_x[...])

    @pl.when(chunk == 0)
    def _():
        acc[...] = jnp.zeros_like(acc)

    def split(lhs, rhs):
        high = lhs.astype(BF16)
        low = (lhs - high.astype(F32)).astype(BF16)
        both = dot(jnp.concatenate([high, low], axis=0), rhs.astype(BF16), NT)
        return both[0:lines] + both[lines:]

    head_of = chunk * per_chunk + lax.broadcasted_iota(jnp.int32, (128, width), 1) // head_dim
    picks = jnp.where(
        head_of == lax.broadcasted_iota(jnp.int32, (128, width), 0), 1.0, 0.0
    ).astype(F32)
    kinds = lax.broadcasted_iota(jnp.int32, (lines, 128), 0)
    tables = split(later, grad_up[0, 0, 0]) + split(earlier, grad_down[0, 0, 0])
    skips = jnp.broadcast_to(small[0, 0, vocab + 1 : vocab + 2, :], (lines, width))
    acc[...] += jnp.where(kinds < vocab, tables, split(skips, picks))

    @pl.when(chunk == pl.num_programs(0) - 1)
    def _():
        total[...] = jnp.where(
            kinds < vocab,
            (acc[...] + tab[...]) * table_scale,
            jnp.where(kinds == vocab, acc[...] * skip_scale, 0.0),
        )


def finish_chunk(
    per_chunk, head_dim, vocab, meta, chunk, gains, hid, cot, writer, cmat, mine,
    mixed_in, back_in, chain_in, chain_back, begin_here, begin_there, from_x, from_y,
    mixed, grad_hidden, acc_c, acc_w,
):
    length = hid.shape[0]
    state = chain_in.shape[0] // 2
    live = live_rows(meta, (length, head_dim))
    begins = []
    for at in range(begin_here.shape[0]):
        value = jnp.where(meta[3] != 0, begin_here[at], begin_there[at])
        for lane in range(0, value.shape[1], state):
            begins.append(value[:, lane : lane + state].T)
    begins = jnp.concatenate(begins, axis=1)
    row = slice(vocab, vocab + 1)
    passed = jnp.where(meta[4] != 0, from_x[row, :], from_y[row, :])
    passed = jnp.where(meta[2] == 0, 1.0, passed)
    state_in = (chain_in[0:state].astype(F32) + passed * begins).astype(BF16)
    grad_in = chain_in[state:]
    state_back = chain_back[0:state]
    grad_back = chain_back[state:]
    from_in = dot(cmat, state_in)
    from_back = dot(cmat, state_back)
    grad_from_in = dot(writer, grad_in)
    grad_from_back = dot(writer, grad_back)
    fallen, risen, grad_fallen, grad_risen = [], [], [], []
    for head in range(per_chunk):
        at = slice(head * head_dim, (head + 1) * head_dim)
        rise = column(mine, RISE, per_chunk, head)
        fall = column(mine, FALL, per_chunk, head)
        step = column(mine, STEP, per_chunk, head)
        gain = gains[chunk * per_chunk + head]
        values = hid[:, at].astype(F32)
        scaled = (step * values).astype(BF16).astype(F32)
        grads = jnp.where(live, cot[:, at].astype(F32), 0.0)
        mixed[:, at] = (
            mixed_in[:, at] + rise * from_in[:, at] + fall * from_back[:, at] + gain * values
        ).astype(BF16)
        back = back_in[:, at] + rise * grad_from_in[:, at] + fall * grad_from_back[:, at]
        grad_hidden[:, at] = (step * back + gain * grads).astype(BF16)
        fallen.append((fall * scaled).astype(BF16))
        risen.append((rise * scaled).astype(BF16))
        grad_fallen.append((fall * grads).astype(BF16))
        grad_risen.append((rise * grads).astype(BF16))
    fallen, risen, grad_fallen, grad_risen = (
        jnp.concatenate(parts, axis=1) for parts in (fallen, risen, grad_fallen, grad_risen)
    )
    acc_c[...] += dot(grad_risen, state_in, NT) + dot(grad_fallen, state_back, NT)
    acc_w[...] += dot(risen, grad_in, NT) + dot(fallen, grad_back, NT)


def early_kernel(
    per_chunk, head_dim, vocab,
    meta, gains, hid, cot, writer, cmat, cols, mixed_in, back_in, reader_in, writer_in,
    held_up, held_down, begin_here, begin_there, from_x, from_y, *refs,
):
    mixed, grad_hidden, acc_c, acc_w = refs[-5:-1]
    chunk = pl.program_id(0)

    @pl.when(chunk == 0)
    def _():
        acc_c[...] = reader_in[...]
        acc_w[...] = writer_in[...]

    finish_chunk(
        per_chunk, head_dim, vocab, meta, chunk, gains, hid, cot, writer[...], cmat[...],
        cols[0], mixed_in, back_in, held_up[0, 0], held_down[0, 0], begin_here, begin_there, from_x, from_y,
        mixed, grad_hidden, acc_c, acc_w,
    )


def last_kernel(
    per_chunk, head_dim, vocab, bmat_scale, land, chunk,
    meta, gains, hid, cot, writer, cmat, cols, mixed_in, back_in, sum_c, sum_w,
    held_up, held_down, begin_here, begin_there, from_x, from_y, got, *refs,
):
    sums = refs[2:-8]
    mixed, grad_hidden, grad_cmat, grad_bmat, grad_table, grad_skip, acc_c, acc_w = refs[-8:]
    total = sums[0][...]
    for value in sums[1:]:
        total = total + value[...]
    vocab_rows, heads = grad_table.shape[0], grad_skip.shape[1]
    grad_table[...] = total[0:vocab_rows, :]
    grad_skip[...] = total[vocab_rows : vocab_rows + 1, 0:heads]
    acc_c[...] = sum_c[...]
    acc_w[...] = sum_w[...]
    fresh, odd = meta[land] == chunk, meta[4] != 0
    arrived = got[...].astype(BF16)
    chain_in = jnp.where(fresh & odd, arrived, held_up[0, 0])
    chain_back = jnp.where(fresh & jnp.logical_not(odd), arrived, held_down[0, 0])
    finish_chunk(
        per_chunk, head_dim, vocab, meta, chunk, gains, hid, cot, writer[...], cmat[...],
        cols[0], mixed_in, back_in, chain_in, chain_back, begin_here, begin_there, from_x, from_y,
        mixed, grad_hidden, acc_c, acc_w,
    )
    grad_cmat[...] = acc_c[...].astype(BF16)
    grad_bmat[...] = (acc_w[...] * bmat_scale).astype(BF16)


def whole(shape):
    return pl.BlockSpec(shape, lambda *_: (0,) * len(shape))


def call(body, scalars, grid, ins, outs, scratch=(), aliases=None, limit=16 << 20):
    results = pl.pallas_call(
        body,
        out_shape=[
            jax.ShapeDtypeStruct(shape, kind) if place is None else place(shape, kind)
            for shape, kind, _, place in outs
        ],
        grid_spec=pltpu.PrefetchScalarGridSpec(
            num_scalar_prefetch=len(scalars),
            grid=grid,
            in_specs=[spec for _, spec, _ in ins],
            out_specs=[spec for _, _, spec, _ in outs],
            scratch_shapes=list(scratch),
        ),
        input_output_aliases=aliases or {},
        compiler_params=pltpu.CompilerParams(vmem_limit_bytes=limit),
    )(
        *scalars,
        *[
            array if place is None else pltpu.with_memory_space_constraint(array, place)
            for array, _, place in ins
        ],
    )
    return results


def sum_steps(axes):
    steps, last = [], []
    for axis in axes:
        count = lax.axis_size(axis)
        if count & (count - 1):
            steps.append(functools.partial(lax.psum, axis_name=axis))
            continue
        hop = 1
        while hop < count:
            hops = [hop]
            if axis == axes[-1] and 4 * hop >= count:
                hops = range(hop, count, hop)
            group = [
                functools.partial(
                    lax.ppermute, axis_name=axis, perm=[(at, at ^ far) for at in range(count)]
                )
                for far in hops
            ]
            if axis == axes[-1] and 4 * hop >= count:
                last = group
                break
            steps.append(lambda value, group=group: value + group[0](value))
            hop *= 2
    return steps, last


def per_device(
    hidden, bmat, cmat, tokens, table, step_size, log_decay, skip_gain,
    prev_state, ancestors, suffix_start, cotangent,
):
    prompts, parts, length, width = hidden.shape
    assert prompts * parts == 1
    heads = skip_gain.shape[0]
    head_dim = width // heads
    state_dim = bmat.shape[3]
    vocab = table.shape[0]
    count = lax.axis_size("ctx")
    doms = lax.axis_size("dom")
    place = lax.axis_index("ctx")
    chunks = CHUNKS
    per_chunk = heads // chunks
    part = width // chunks
    total_rows = length * count * doms * lax.axis_size("rep")
    bmat_scale = 1.0 / math.sqrt(width)
    total_scale = 1.0 / math.sqrt(total_rows)
    lines = -(-(vocab + 2) // 8) * 8
    slots = chunks + count - 2
    paired = count == 4

    hid = hidden.reshape(length, width)
    cot = cotangent.reshape(length, width)
    writes = bmat.reshape(length, state_dim)
    reads = cmat.reshape(length, state_dim)
    toks = tokens.reshape(1, length)
    steps_t = jnp.swapaxes(step_size, 2, 3).reshape(heads, length)
    rates_t = jnp.swapaxes(log_decay, 2, 3).reshape(heads, length)
    ancestor = ancestors[0, 0]
    here = ancestor == lax.axis_index("dom")

    times = jnp.arange(slots, dtype=jnp.int32)
    from_last = count - 1 - place
    odd = place % 2
    table_of = []
    for upward_here in (odd == 1, odd == 0):
        far = jnp.where(upward_here, place, from_last)
        lands = times - jnp.maximum(far, 1) + 1
        if paired:
            arrives = times + 2 == far
            pieces = jnp.where(arrives, jnp.where(upward_here, 0, 3), count)
            others = jnp.where(arrives, jnp.where(upward_here, 1, 2), count)
        else:
            pieces = place + jnp.where(upward_here, -1, 1) * (times + 2)
            pieces = jnp.where((pieces >= 0) & (pieces < count), pieces, count)
            others = jnp.full_like(times, count)
        table_of += [
            jnp.where((lands >= 0) & (lands < chunks), lands, chunks),
            jnp.clip(times + 1 - far, 0, chunks - 1),
            (times + 1 < far).astype(jnp.int32),
            pieces, others,
        ]
    base = [place * length, suffix_start[0], place, here, odd]
    base = jnp.stack([jnp.asarray(value, jnp.int32) for value in base])
    meta = jnp.concatenate([base] + [value.astype(jnp.int32) for value in table_of])
    tables = [[5 + (5 * side + at) * slots for at in range(5)] for side in range(2)]

    upward = [(at, at + 1) for at in range(count - 1)]
    downward = [(at + 1, at) for at in range(count - 1)]
    own_state = prev_state[0, 0]
    local_heads = own_state.shape[0]
    assert per_chunk % local_heads == 0
    if doms != 2:
        own_state = lax.dynamic_index_in_dim(
            lax.all_gather(own_state, "dom"), ancestor, 0, keepdims=False
        )
    if paired:
        swap = [(at, at ^ 1) for at in range(count)]
        pieces = [lax.ppermute(own_state, "ctx", swap), own_state]
    else:
        pieces = [lax.ppermute(own_state, "ctx", way) for way in (upward, downward)]

    anywhere = pl.BlockSpec(memory_space=pl.ANY)
    near = pl.BlockSpec(memory_space=pltpu.VMEM)
    by_chunk = pl.BlockSpec((length, part), lambda k, *_: (0, k))
    one_cols = pl.BlockSpec((1, length, 128), lambda k, *_: (k, 0, 0))
    pair = pl.BlockSpec((2, 1, 2, state_dim, part), lambda k, *_: (0, k, 0, 0, 0))
    one_small = pl.BlockSpec((1, 1, lines, part), lambda k, *_: (1, k, 0, 0))
    square = whole((length, state_dim))
    tok_spec = whole((1, length))
    full_rows = 2 * state_dim + chunks * lines
    small_shape = (2, chunks, lines, part)
    first = ((full_rows, part), F32, near, CHIP)

    x_first, y_first, small, cols, writer, hid, cot, kept = call(
        functools.partial(start_kernel, per_chunk, head_dim, vocab, chunks),
        (meta,), (1,),
        [
            (writes, square, HBM), (reads, square, HBM), (toks, tok_spec, HBM),
            (table, whole(table.shape), HBM), (steps_t, whole(steps_t.shape), HBM),
            (rates_t, whole(rates_t.shape), HBM), (hid, anywhere, HBM), (cot, anywhere, HBM),
            (own_state, anywhere, HBM),
        ],
        [
            first, first,
            (small_shape, F32, near, CHIP),
            ((chunks, length, 128), F32, near, CHIP), ((length, state_dim), BF16, near, CHIP),
            ((length, width), BF16, near, CHIP), ((length, width), BF16, near, CHIP),
            (own_state.shape, F32, near, CHIP),
        ],
        [pltpu.SemaphoreType.DMA((chunks + 1, 2))],
    )

    if paired:
        pieces[1] = kept
    x_first, y_first = call(
        functools.partial(relay_kernel, count - 1, paired),
        (meta,), (),
        [(piece, anywhere, CHIP if piece is kept else None) for piece in pieces]
        + [(x_first, near, CHIP), (y_first, near, CHIP)],
        [
            ((full_rows, part), F32, near, CHIP), ((full_rows, part), F32, near, CHIP),
        ],
        [pltpu.SemaphoreType.DMA((4, 2, local_heads))],
        aliases={3: 0, 4: 1},
    )
    begin_shape = (count + 1, head_dim, local_heads * state_dim)
    (begin_here,) = call(
        functools.partial(gather_kernel, count - 1, paired),
        (meta,), (),
        [
            (piece, anywhere, CHIP if piece is kept else None)
            for piece in (pieces if paired else pieces + [kept])
        ],
        [(begin_shape, F32, near, CHIP)],
        [pltpu.SemaphoreType.DMA((3, local_heads))],
    )

    ends, mixed_in, back_in, reader_in, writer_in, tab = call(
        functools.partial(inner_kernel, per_chunk, head_dim, vocab),
        (meta,), (chunks,),
        [
            (hid, by_chunk, CHIP), (cot, by_chunk, CHIP), (writer, square, CHIP),
            (reads, square, HBM), (toks, tok_spec, HBM), (cols, one_cols, CHIP),
        ],
        [
            ((2, chunks, 2, state_dim, part), F32, pair, CHIP),
            ((length, width), F32, by_chunk, CHIP),
            ((length, width), F32, by_chunk, CHIP),
            ((length, state_dim), F32, square, CHIP),
            ((length, state_dim), F32, square, CHIP),
            ((lines, state_dim), F32, whole((lines, state_dim)), CHIP),
        ],
        [pltpu.VMEM((length, length), F32)] * 3 + [pltpu.VMEM((state_dim, length), BF16)] * 2,
    )

    def step_chain(slot, side, received, held, begin, waits):
        has_small = slot < count - 2
        has_begin = slot < count - 2
        sends = side == 1 or slot + 1 < slots - 1
        rows = full_rows if has_small else 2 * state_dim
        held_shape = (2, chunks + 1, 2 * state_dim, part)
        ins = [(received, near, CHIP), (ends, near, CHIP), (small, near, CHIP)]
        outs = [((rows, part), F32, near, CHIP)] if sends else []
        outs.append((held_shape, BF16, near, CHIP))
        aliases = {}
        if held is not None:
            aliases[1 + len(ins)] = len(outs) - 1
            ins.append((held, near, CHIP))
        if has_begin:
            aliases[1 + len(ins)] = len(outs)
            ins.append((begin, near, CHIP))
            outs.append((begin_shape, F32, near, CHIP))
        ins += [(value, anywhere, None) for value in waits]
        results = call(
            functools.partial(
                combine_kernel, vocab, has_small, has_begin, sends, slot, side, tables[side]
            ),
            (meta,), (), ins, outs,
            aliases=aliases,
        )
        results = list(results) if has_begin else [*results, begin]
        return results if sends else [None, *results]

    lines_at = 2 * state_dim // lines
    from_slot = pl.BlockSpec((lines, part), lambda k, *_: (lines_at + k, 0))
    grad_parts = [
        pl.BlockSpec((1, 1, 1, state_dim, part), lambda k, *_, way=way: (way, k, 1, 0, 0))
        for way in range(2)
    ]
    sums, exchanges = sum_steps(("rep", "dom", "ctx"))
    assert count % 2 == 0
    even_links = [(at, at ^ 1) for at in range(count)]
    odd_links = [(at, (at - 1 ^ 1) + 1) for at in range(1, count - 1)]
    send_x, send_y, held = x_first, y_first, None
    for slot in range(slots):
        got_x = lax.ppermute(send_x, "ctx", even_links)
        if slot < slots - 1:
            got_y = lax.ppermute(send_y, "ctx", odd_links)
        waits_up, waits_down = [], []
        if slot == count - 2:
            from_x, from_y = got_x, got_y
        if slot == count - 1:
            begin_there = begin_here
            if doms == 2:
                begin_there = lax.ppermute(begin_here, "dom", [(0, 1), (1, 0)])
            (total,) = call(
                functools.partial(
                    sums_kernel, per_chunk, head_dim, vocab,
                    bmat_scale * total_scale, total_scale / math.sqrt(head_dim),
                ),
                (meta,), (chunks,),
                [
                    (from_x, from_slot, None), (from_y, from_slot, None),
                    (small, one_small, CHIP), (ends, grad_parts[0], CHIP),
                    (ends, grad_parts[1], CHIP), (tab, whole(tab.shape), CHIP),
                ],
                [((lines, state_dim), F32, whole((lines, state_dim)), None)],
                [pltpu.VMEM((lines, state_dim), F32)],
            )
        if slot == slots - 1:
            break
        if slot >= count - 1:
            if slot > count - 1:
                waits_down.append(begin_there)
                for step in sums[:1]:
                    total = step(total)
                sums = sums[1:]
            waits_down.append(total)
        send_y, held, begin_here = step_chain(slot, 0, got_x, held, begin_here, waits_down)
        if slot >= count - 1:
            for step in sums[:1]:
                total = step(total)
            sums = sums[1:]
            waits_up.append(total)
        send_x, held, begin_here = step_chain(slot, 1, got_y, held, begin_here, waits_up)

    def chunk_specs(at):
        return (
            pl.BlockSpec((length, part), lambda k, *_: (0, k + at)),
            pl.BlockSpec((1, length, 128), lambda k, *_: (k + at, 0, 0)),
            [
                pl.BlockSpec(
                    (1, 1, 2 * state_dim, part), lambda k, *_, way=way: (way, k + at, 0, 0)
                )
                for way in range(2)
            ],
            pl.BlockSpec(
                (per_chunk // local_heads, head_dim, local_heads * state_dim),
                lambda k, *_: (k + at, 0, 0),
            ),
            pl.BlockSpec((lines, part), lambda k, *_: (lines_at + k + at, 0)),
        )

    def finish_ins(at, sum_c, sum_w):
        slab, col, chain, states, rows = chunk_specs(at)
        return [
            (hid, slab, CHIP), (cot, slab, CHIP), (writer, square, CHIP), (reads, square, HBM),
            (cols, col, CHIP), (mixed_in, slab, CHIP), (back_in, slab, CHIP),
            (sum_c, square, CHIP), (sum_w, square, CHIP),
            (held, chain[0], CHIP), (held, chain[1], CHIP),
            (begin_here, states, CHIP), (begin_there, states, CHIP), (from_x, rows, None), (from_y, rows, None),
        ]

    for step in sums:
        total = step(total)
    slab = chunk_specs(0)[0]
    mixed, grad_hidden, sum_c, sum_w, total = call(
        functools.partial(early_kernel, per_chunk, head_dim, vocab),
        (meta, skip_gain), (chunks - 1,),
        finish_ins(0, reader_in, writer_in) + [(total, anywhere, None)],
        [
            ((length, width), BF16, slab, HBM), ((length, width), BF16, slab, HBM),
            ((length, state_dim), F32, square, CHIP), ((length, state_dim), F32, square, CHIP),
            (total.shape, F32, anywhere, None),
        ],
        aliases={17: 4},
    )
    exchanged = [exchange(total) for exchange in exchanges]
    ins = finish_ins(chunks - 1, sum_c, sum_w) + [
        (got_x, whole(got_x.shape), None),
        (mixed, anywhere, HBM), (grad_hidden, anywhere, HBM),
    ] + [(value, whole(value.shape), None) for value in [total] + exchanged]
    slab = chunk_specs(chunks - 1)[0]
    mixed, grad_hidden, grad_cmat, grad_bmat, grad_table, grad_skip = call(
        functools.partial(
            last_kernel, per_chunk, head_dim, vocab, bmat_scale,
            tables[0][0] + slots - 1, chunks - 1,
        ),
        (meta, skip_gain), (1,), ins,
        [
            ((length, width), BF16, slab, HBM), ((length, width), BF16, slab, HBM),
            ((length, state_dim), BF16, square, HBM), ((length, state_dim), BF16, square, HBM),
            (table.shape, F32, whole(table.shape), HBM),
            ((1, heads), F32, whole((1, heads)), HBM),
        ],
        [pltpu.VMEM((length, state_dim), F32)] * 2,
        aliases={18: 0, 19: 1},
    )
    return (
        mixed.reshape(hidden.shape),
        grad_hidden.reshape(hidden.shape),
        grad_bmat.reshape(bmat.shape),
        grad_cmat.reshape(cmat.shape),
        grad_table,
        grad_skip.reshape(heads),
    )


def solution(mesh):
    rows = P("rep", "dom", "ctx", None)
    return jax.shard_map(
        per_device,
        mesh=mesh,
        in_specs=(
            rows, rows, rows, P("rep", "dom", "ctx"), P(), rows, rows, P(),
            P("rep", "dom", "ctx", None, None), P("rep", "dom"), P("rep"), rows,
        ),
        out_specs=(rows, rows, rows, rows, P(), P()),
        check_vma=False,
    )
```

```python
import functools
import math

import jax
import jax.numpy as jnp
from jax import lax
from jax.experimental import pallas as pl
from jax.experimental.pallas import tpu as pltpu
from jax.sharding import PartitionSpec as P

F32 = jnp.float32
BF16 = jnp.bfloat16
EXACT = lax.Precision.HIGHEST
NN = (((1,), (0,)), ((), ()))
NT = (((1,), (1,)), ((), ()))
TN = (((0,), (0,)), ((), ()))
CHUNKS = 4
HBM, CHIP = pltpu.HBM, pltpu.VMEM


def dot(left, right, dims=NN, precision=None):
    return lax.dot_general(
        left, right, dims, precision=precision, preferred_element_type=F32
    )


def one_hot_rows(tokens_row, rows):
    kinds = lax.broadcasted_iota(jnp.int32, (rows, tokens_row.shape[1]), 0)
    return kinds == tokens_row


def live_rows(meta, shape):
    return meta[0] + lax.broadcasted_iota(jnp.int32, shape, 0) < meta[1]


def column(cols, kind, per_chunk, head):
    at = kind * per_chunk + head
    return cols[:, at : at + 1]


STEP, RISE, FALL, CUM = range(4)


def start_kernel(
    per_chunk, head_dim, vocab, chunks,
    meta, bmat, cmat, tokens, table, step_t, rate_t, hid_far, cot_far, state_far,
    x_first, y_first, small, cols, writer, hid, cot, state_near, sems,
):
    length = bmat.shape[0]
    state = bmat.shape[1]
    part = per_chunk * head_dim
    lines = small.shape[2]
    odd = meta[4] != 0
    copies = []
    for chunk in range(chunks):
        span = slice(chunk * part, (chunk + 1) * part)
        pair = [
            pltpu.make_async_copy(far.at[:, span], near.at[:, span], sems.at[chunk, at])
            for at, (far, near) in enumerate(((hid_far, hid), (cot_far, cot)))
        ]
        for copy in pair:
            copy.start()
        copies.append(pair)
    keep = pltpu.make_async_copy(state_far, state_near, sems.at[chunks, 0])
    keep.start()

    row = lax.broadcasted_iota(jnp.int32, (length, length), 0)
    col = lax.broadcasted_iota(jnp.int32, (length, length), 1)
    lower = jnp.where(col <= row, 1.0, 0.0).astype(F32)
    cumulative = dot(lower, rate_t[...], NT, EXACT)
    totals = cumulative[length - 1 : length, :]
    rising = jnp.exp(-cumulative)
    falling = jnp.exp(-(totals - cumulative))
    step = step_t[...].T
    for at in range(chunks):
        lo = at * per_chunk
        for kind, values in enumerate((step, rising, falling, cumulative)):
            cols[at, :, kind * per_chunk : (kind + 1) * per_chunk] = values[:, lo : lo + per_chunk]
    hot = one_hot_rows(tokens[...], vocab)
    looked = dot(jnp.where(hot, 1.0, 0.0).astype(F32), table[...], TN, EXACT)
    rows = (bmat[...].astype(F32) + looked).astype(BF16)
    writer[...] = rows
    chosen = jnp.where(one_hot_rows(tokens[...], lines), 1.0, 0.0).astype(BF16)
    kinds = lax.broadcasted_iota(jnp.int32, (lines, part), 0)
    live = live_rows(meta, (length, head_dim))
    for chunk in range(chunks):
        for copy in copies[chunk]:
            copy.wait()
        fallen, risen, grad_fallen, grad_risen, gone, skips = [], [], [], [], [], []
        for head in range(per_chunk):
            number = chunk * per_chunk + head
            at = slice(number * head_dim, (number + 1) * head_dim)
            rise = rising[:, number : number + 1]
            fall = falling[:, number : number + 1]
            values = hid[:, at].astype(F32)
            scaled = (step[:, number : number + 1] * values).astype(BF16).astype(F32)
            grads = jnp.where(live, cot[:, at].astype(F32), 0.0)
            fallen.append((fall * scaled).astype(BF16))
            risen.append((rise * scaled).astype(BF16))
            if chunk == 0:
                grad_fallen.append((fall * grads).astype(BF16))
                grad_risen.append((rise * grads).astype(BF16))
            gone.append(jnp.broadcast_to(rise[length - 1 : length, :], (1, head_dim)))
            skips.append(jnp.sum(values * grads, axis=0, keepdims=True))
        fallen, risen, gone, skips = (
            jnp.concatenate(parts, axis=1) for parts in (fallen, risen, gone, skips)
        )
        up_lines = jnp.where(
            kinds == vocab, jnp.where(meta[2] == 0, gone, 0.0), dot(chosen, fallen)
        )
        down_lines = jnp.where(
            kinds == vocab, gone, jnp.where(kinds == vocab + 1, skips, dot(chosen, risen))
        )
        small[0, chunk] = up_lines
        small[1, chunk] = down_lines
        small_rows = slice(2 * state + chunk * lines, 2 * state + (chunk + 1) * lines)
        x_first[small_rows, :] = jnp.where(odd, down_lines, up_lines)
        y_first[small_rows, :] = jnp.where(odd, up_lines, down_lines)
        if chunk == 0:
            ends = jnp.where(odd, risen, fallen)
            grad_ends = jnp.where(
                odd, jnp.concatenate(grad_risen, axis=1), jnp.concatenate(grad_fallen, axis=1)
            )
            x_first[0:state, :] = dot(rows.T, ends)
            x_first[state : 2 * state, :] = dot(cmat[...].T, grad_ends)
            y_first[0 : 2 * state, :] = jnp.zeros((2 * state, part), F32)
    keep.wait()


def head_copies(source, target, row, sems):
    heads, rows, width = source.shape
    return [
        pltpu.make_async_copy(
            source.at[head],
            target.at[pl.ds(row, rows), pl.ds(head * width, width)],
            sems.at[head],
        )
        for head in range(heads)
    ]


def relay_kernel(last, paired, meta, *refs):
    sources, (x, y, sems) = refs[:-5], refs[-3:]
    place, odd = meta[2], meta[4] != 0
    if paired:
        plans = [((place == 1) | (place == 2), y, sources)]
    else:
        before, after = sources
        inside, ahead = place > 0, place < last
        plans = [
            (inside & jnp.logical_not(odd), x, [before]), (inside & odd, y, [before]),
            (ahead & odd, x, [after]), (ahead & jnp.logical_not(odd), y, [after]),
        ]
    for at, (wanted, message, pieces) in enumerate(plans):
        copies = []
        for half, source in enumerate(pieces):
            copies += head_copies(source, message, half * source.shape[1], sems.at[at, half])

        @pl.when(wanted)
        def _():
            for copy in copies:
                copy.start()
            for copy in copies:
                copy.wait()


def gather_kernel(last, paired, meta, *refs):
    sources, begin, sems = refs[:-2], refs[-2], refs[-1]
    place = meta[2]
    if paired:
        rows = (lax.bitwise_xor(place, 1), place)
    else:
        rows = (jnp.where(place == 0, last + 1, place - 1), place + 1, place)
    copies = []
    for at, (source, row) in enumerate(zip(sources, rows, strict=True)):
        copies += head_copies(source, begin.at[row], 0, sems.at[at])
    for copy in copies:
        copy.start()
    for copy in copies:
        copy.wait()


def combine_kernel(vocab, has_small, has_begin, sends, slot, side, tables, *refs):
    meta, received, own, small = refs[:4]
    held = refs[-1 - has_begin]
    way = meta[4] if side else 1 - meta[4]
    state = own.shape[3]
    land, source, forward, piece, other = (at + slot for at in tables)
    if has_begin:
        begin = refs[-1]
        begin[meta[piece]] = received[0:state, 0 : begin.shape[2]]
        begin[meta[other]] = received[state : 2 * state, 0 : begin.shape[2]]
    held[way, meta[land]] = received[0 : 2 * state, :].astype(BF16)
    if not sends:
        return
    send = refs[-2 - has_begin]
    passing = meta[forward] != 0
    decay = jnp.where(passing, 1.0, small[1, meta[source], vocab : vocab + 1, :])
    adding = jnp.where(passing, 0.0, 1.0)
    if has_small:
        lines = small.shape[2]
        for at in range(small.shape[1]):
            rows = slice(2 * state + at * lines, 2 * state + (at + 1) * lines)
            send[rows, :] = (
                small[1, at, vocab : vocab + 1, :] * received[rows, :] + small[way, at]
            )
    for at in range(2):
        rows = slice(at * state, (at + 1) * state)
        send[rows, :] = decay * received[rows, :] + adding * own[way, meta[source], at]


def inner_kernel(
    per_chunk, head_dim, vocab,
    meta, hid, cot, writer, cmat, tokens, cols,
    ends, mixed_in, back_in, reader_in, writer_in, tab,
    inner, inner_t, cross, writer_t, reader_t,
):
    chunk = pl.program_id(0)
    length = hid.shape[0]

    @pl.when(chunk == 0)
    def _():
        inner[...] = dot(cmat[...], writer[...], NT)
        inner_t[...] = dot(writer[...], cmat[...], NT)
        cross[...] = jnp.zeros_like(cross)
        writer_t[...] = writer[...].T
        reader_t[...] = cmat[...].T

    mine = cols[0]
    across = mine.T
    live = live_rows(meta, (length, head_dim))
    fallen, risen, grad_fallen, grad_risen = [], [], [], []
    for head in range(per_chunk):
        at = slice(head * head_dim, (head + 1) * head_dim)
        row = CUM * per_chunk + head
        decay = jnp.exp(
            -jnp.abs(column(mine, CUM, per_chunk, head) - across[row : row + 1, :])
        )
        rise = column(mine, RISE, per_chunk, head)
        fall = column(mine, FALL, per_chunk, head)
        scaled = (column(mine, STEP, per_chunk, head) * hid[:, at].astype(F32)).astype(BF16)
        grads_wide = jnp.where(live, cot[:, at].astype(F32), 0.0)
        grads = grads_wide.astype(BF16)
        scaled_wide = scaled.astype(F32)
        fallen.append((fall * scaled_wide).astype(BF16))
        risen.append((rise * scaled_wide).astype(BF16))
        grad_fallen.append((fall * grads_wide).astype(BF16))
        grad_risen.append((rise * grads_wide).astype(BF16))
        mixed_in[:, at] = dot((decay * inner[...]).astype(BF16), scaled)
        back_in[:, at] = dot((decay * inner_t[...]).astype(BF16), grads)
        cross[...] += decay * dot(grads, scaled, NT)
    ends[0, 0, 0] = dot(writer_t[...], jnp.concatenate(fallen, axis=1))
    ends[0, 0, 1] = dot(reader_t[...], jnp.concatenate(grad_fallen, axis=1))
    ends[1, 0, 0] = dot(writer_t[...], jnp.concatenate(risen, axis=1))
    ends[1, 0, 1] = dot(reader_t[...], jnp.concatenate(grad_risen, axis=1))

    @pl.when(chunk == pl.num_programs(0) - 1)
    def _():
        crossed = cross[...].astype(BF16)
        reader_in[...] = dot(crossed, writer[...])
        into = dot(crossed.astype(F32).T.astype(BF16), cmat[...])
        writer_in[...] = into
        chosen = jnp.where(one_hot_rows(tokens[...], tab.shape[0]), 1.0, 0.0).astype(F32)
        tab[...] = dot(chosen, into, precision=EXACT)


def sums_kernel(
    per_chunk, head_dim, vocab, table_scale, skip_scale,
    meta, from_x, from_y, small, grad_up, grad_down, tab, total, acc,
):
    chunk = pl.program_id(0)
    lines, width = from_x.shape
    odd = meta[4] != 0
    earlier = jnp.where(odd, from_x[...], from_y[...])
    later = jnp.where(odd, from_y[...], from_x[...])

    @pl.when(chunk == 0)
    def _():
        acc[...] = jnp.zeros_like(acc)

    def split(lhs, rhs):
        high = lhs.astype(BF16)
        low = (lhs - high.astype(F32)).astype(BF16)
        both = dot(jnp.concatenate([high, low], axis=0), rhs.astype(BF16), NT)
        return both[0:lines] + both[lines:]

    head_of = chunk * per_chunk + lax.broadcasted_iota(jnp.int32, (128, width), 1) // head_dim
    picks = jnp.where(
        head_of == lax.broadcasted_iota(jnp.int32, (128, width), 0), 1.0, 0.0
    ).astype(F32)
    kinds = lax.broadcasted_iota(jnp.int32, (lines, 128), 0)
    tables = split(later, grad_up[0, 0, 0]) + split(earlier, grad_down[0, 0, 0])
    skips = jnp.broadcast_to(small[0, 0, vocab + 1 : vocab + 2, :], (lines, width))
    acc[...] += jnp.where(kinds < vocab, tables, split(skips, picks))

    @pl.when(chunk == pl.num_programs(0) - 1)
    def _():
        total[...] = jnp.where(
            kinds < vocab,
            (acc[...] + tab[...]) * table_scale,
            jnp.where(kinds == vocab, acc[...] * skip_scale, 0.0),
        )


def finish_chunk(
    per_chunk, head_dim, vocab, meta, chunk, gains, hid, cot, writer, cmat, mine,
    mixed_in, back_in, chain_in, chain_back, begin_here, begin_there, from_x, from_y,
    mixed, grad_hidden, acc_c, acc_w,
):
    length = hid.shape[0]
    state = chain_in.shape[0] // 2
    live = live_rows(meta, (length, head_dim))
    begins = []
    for at in range(begin_here.shape[0]):
        value = jnp.where(meta[3] != 0, begin_here[at], begin_there[at])
        for lane in range(0, value.shape[1], state):
            begins.append(value[:, lane : lane + state].T)
    begins = jnp.concatenate(begins, axis=1)
    row = slice(vocab, vocab + 1)
    passed = jnp.where(meta[4] != 0, from_x[row, :], from_y[row, :])
    passed = jnp.where(meta[2] == 0, 1.0, passed)
    state_in = (chain_in[0:state].astype(F32) + passed * begins).astype(BF16)
    grad_in = chain_in[state:]
    state_back = chain_back[0:state]
    grad_back = chain_back[state:]
    from_in = dot(cmat, state_in)
    from_back = dot(cmat, state_back)
    grad_from_in = dot(writer, grad_in)
    grad_from_back = dot(writer, grad_back)
    fallen, risen, grad_fallen, grad_risen = [], [], [], []
    for head in range(per_chunk):
        at = slice(head * head_dim, (head + 1) * head_dim)
        rise = column(mine, RISE, per_chunk, head)
        fall = column(mine, FALL, per_chunk, head)
        step = column(mine, STEP, per_chunk, head)
        gain = gains[chunk * per_chunk + head]
        values = hid[:, at].astype(F32)
        scaled = (step * values).astype(BF16).astype(F32)
        grads = jnp.where(live, cot[:, at].astype(F32), 0.0)
        mixed[:, at] = (
            mixed_in[:, at] + rise * from_in[:, at] + fall * from_back[:, at] + gain * values
        ).astype(BF16)
        back = back_in[:, at] + rise * grad_from_in[:, at] + fall * grad_from_back[:, at]
        grad_hidden[:, at] = (step * back + gain * grads).astype(BF16)
        fallen.append((fall * scaled).astype(BF16))
        risen.append((rise * scaled).astype(BF16))
        grad_fallen.append((fall * grads).astype(BF16))
        grad_risen.append((rise * grads).astype(BF16))
    fallen, risen, grad_fallen, grad_risen = (
        jnp.concatenate(parts, axis=1) for parts in (fallen, risen, grad_fallen, grad_risen)
    )
    acc_c[...] += dot(grad_risen, state_in, NT) + dot(grad_fallen, state_back, NT)
    acc_w[...] += dot(risen, grad_in, NT) + dot(fallen, grad_back, NT)


def early_kernel(
    per_chunk, head_dim, vocab,
    meta, gains, hid, cot, writer, cmat, cols, mixed_in, back_in, reader_in, writer_in,
    held_up, held_down, begin_here, begin_there, from_x, from_y, *refs,
):
    mixed, grad_hidden, acc_c, acc_w = refs[-5:-1]
    chunk = pl.program_id(0)

    @pl.when(chunk == 0)
    def _():
        acc_c[...] = reader_in[...]
        acc_w[...] = writer_in[...]

    finish_chunk(
        per_chunk, head_dim, vocab, meta, chunk, gains, hid, cot, writer[...], cmat[...],
        cols[0], mixed_in, back_in, held_up[0, 0], held_down[0, 0], begin_here, begin_there, from_x, from_y,
        mixed, grad_hidden, acc_c, acc_w,
    )


def last_kernel(
    per_chunk, head_dim, vocab, bmat_scale, land, chunk,
    meta, gains, hid, cot, writer, cmat, cols, mixed_in, back_in, sum_c, sum_w,
    held_up, held_down, begin_here, begin_there, from_x, from_y, got, *refs,
):
    sums = refs[2:-8]
    mixed, grad_hidden, grad_cmat, grad_bmat, grad_table, grad_skip, acc_c, acc_w = refs[-8:]
    total = sums[0][...]
    for value in sums[1:]:
        total = total + value[...]
    vocab_rows, heads = grad_table.shape[0], grad_skip.shape[1]
    grad_table[...] = total[0:vocab_rows, :]
    grad_skip[...] = total[vocab_rows : vocab_rows + 1, 0:heads]
    acc_c[...] = sum_c[...]
    acc_w[...] = sum_w[...]
    fresh, odd = meta[land] == chunk, meta[4] != 0
    arrived = got[...].astype(BF16)
    chain_in = jnp.where(fresh & odd, arrived, held_up[0, 0])
    chain_back = jnp.where(fresh & jnp.logical_not(odd), arrived, held_down[0, 0])
    finish_chunk(
        per_chunk, head_dim, vocab, meta, chunk, gains, hid, cot, writer[...], cmat[...],
        cols[0], mixed_in, back_in, chain_in, chain_back, begin_here, begin_there, from_x, from_y,
        mixed, grad_hidden, acc_c, acc_w,
    )
    grad_cmat[...] = acc_c[...].astype(BF16)
    grad_bmat[...] = (acc_w[...] * bmat_scale).astype(BF16)


def whole(shape):
    return pl.BlockSpec(shape, lambda *_: (0,) * len(shape))


def call(body, scalars, grid, ins, outs, scratch=(), aliases=None, limit=16 << 20):
    results = pl.pallas_call(
        body,
        out_shape=[
            jax.ShapeDtypeStruct(shape, kind) if place is None else place(shape, kind)
            for shape, kind, _, place in outs
        ],
        grid_spec=pltpu.PrefetchScalarGridSpec(
            num_scalar_prefetch=len(scalars),
            grid=grid,
            in_specs=[spec for _, spec, _ in ins],
            out_specs=[spec for _, _, spec, _ in outs],
            scratch_shapes=list(scratch),
        ),
        input_output_aliases=aliases or {},
        compiler_params=pltpu.CompilerParams(vmem_limit_bytes=limit),
    )(
        *scalars,
        *[
            array if place is None else pltpu.with_memory_space_constraint(array, place)
            for array, _, place in ins
        ],
    )
    return results


def sum_steps(axes):
    steps, last = [], []
    for axis in axes:
        count = lax.axis_size(axis)
        if count & (count - 1):
            steps.append(functools.partial(lax.psum, axis_name=axis))
            continue
        hop = 1
        while hop < count:
            hops = [hop]
            if axis == axes[-1] and 4 * hop >= count:
                hops = range(hop, count, hop)
            group = [
                functools.partial(
                    lax.ppermute, axis_name=axis, perm=[(at, at ^ far) for at in range(count)]
                )
                for far in hops
            ]
            if axis == axes[-1] and 4 * hop >= count:
                last = group
                break
            steps.append(lambda value, group=group: value + group[0](value))
            hop *= 2
    return steps, last


def per_device(
    hidden, bmat, cmat, tokens, table, step_size, log_decay, skip_gain,
    prev_state, ancestors, suffix_start, cotangent,
):
    prompts, parts, length, width = hidden.shape
    assert prompts * parts == 1
    heads = skip_gain.shape[0]
    head_dim = width // heads
    state_dim = bmat.shape[3]
    vocab = table.shape[0]
    count = lax.axis_size("ctx")
    doms = lax.axis_size("dom")
    place = lax.axis_index("ctx")
    chunks = CHUNKS
    per_chunk = heads // chunks
    part = width // chunks
    total_rows = length * count * doms * lax.axis_size("rep")
    bmat_scale = 1.0 / math.sqrt(width)
    total_scale = 1.0 / math.sqrt(total_rows)
    lines = -(-(vocab + 2) // 8) * 8
    slots = chunks + count - 2
    paired = count == 4

    hid = hidden.reshape(length, width)
    cot = cotangent.reshape(length, width)
    writes = bmat.reshape(length, state_dim)
    reads = cmat.reshape(length, state_dim)
    toks = tokens.reshape(1, length)
    steps_t = jnp.swapaxes(step_size, 2, 3).reshape(heads, length)
    rates_t = jnp.swapaxes(log_decay, 2, 3).reshape(heads, length)
    ancestor = ancestors[0, 0]
    here = ancestor == lax.axis_index("dom")

    times = jnp.arange(slots, dtype=jnp.int32)
    from_last = count - 1 - place
    odd = place % 2
    table_of = []
    for upward_here in (odd == 1, odd == 0):
        far = jnp.where(upward_here, place, from_last)
        lands = times - jnp.maximum(far, 1) + 1
        if paired:
            arrives = times + 2 == far
            pieces = jnp.where(arrives, jnp.where(upward_here, 0, 3), count)
            others = jnp.where(arrives, jnp.where(upward_here, 1, 2), count)
        else:
            pieces = place + jnp.where(upward_here, -1, 1) * (times + 2)
            pieces = jnp.where((pieces >= 0) & (pieces < count), pieces, count)
            others = jnp.full_like(times, count)
        table_of += [
            jnp.where((lands >= 0) & (lands < chunks), lands, chunks),
            jnp.clip(times + 1 - far, 0, chunks - 1),
            (times + 1 < far).astype(jnp.int32),
            pieces, others,
        ]
    base = [place * length, suffix_start[0], place, here, odd]
    base = jnp.stack([jnp.asarray(value, jnp.int32) for value in base])
    meta = jnp.concatenate([base] + [value.astype(jnp.int32) for value in table_of])
    tables = [[5 + (5 * side + at) * slots for at in range(5)] for side in range(2)]

    upward = [(at, at + 1) for at in range(count - 1)]
    downward = [(at + 1, at) for at in range(count - 1)]
    own_state = prev_state[0, 0]
    local_heads = own_state.shape[0]
    assert per_chunk % local_heads == 0
    if doms != 2:
        own_state = lax.dynamic_index_in_dim(
            lax.all_gather(own_state, "dom"), ancestor, 0, keepdims=False
        )
    if paired:
        swap = [(at, at ^ 1) for at in range(count)]
        pieces = [lax.ppermute(own_state, "ctx", swap), own_state]
    else:
        pieces = [lax.ppermute(own_state, "ctx", way) for way in (upward, downward)]

    anywhere = pl.BlockSpec(memory_space=pl.ANY)
    near = pl.BlockSpec(memory_space=pltpu.VMEM)
    by_chunk = pl.BlockSpec((length, part), lambda k, *_: (0, k))
    one_cols = pl.BlockSpec((1, length, 128), lambda k, *_: (k, 0, 0))
    pair = pl.BlockSpec((2, 1, 2, state_dim, part), lambda k, *_: (0, k, 0, 0, 0))
    one_small = pl.BlockSpec((1, 1, lines, part), lambda k, *_: (1, k, 0, 0))
    square = whole((length, state_dim))
    tok_spec = whole((1, length))
    full_rows = 2 * state_dim + chunks * lines
    small_shape = (2, chunks, lines, part)
    first = ((full_rows, part), F32, near, CHIP)

    x_first, y_first, small, cols, writer, hid, cot, kept = call(
        functools.partial(start_kernel, per_chunk, head_dim, vocab, chunks),
        (meta,), (1,),
        [
            (writes, square, HBM), (reads, square, HBM), (toks, tok_spec, HBM),
            (table, whole(table.shape), HBM), (steps_t, whole(steps_t.shape), HBM),
            (rates_t, whole(rates_t.shape), HBM), (hid, anywhere, HBM), (cot, anywhere, HBM),
            (own_state, anywhere, HBM),
        ],
        [
            first, first,
            (small_shape, F32, near, CHIP),
            ((chunks, length, 128), F32, near, CHIP), ((length, state_dim), BF16, near, CHIP),
            ((length, width), BF16, near, CHIP), ((length, width), BF16, near, CHIP),
            (own_state.shape, F32, near, CHIP),
        ],
        [pltpu.SemaphoreType.DMA((chunks + 1, 2))],
    )

    if paired:
        pieces[1] = kept
    x_first, y_first = call(
        functools.partial(relay_kernel, count - 1, paired),
        (meta,), (),
        [(piece, anywhere, CHIP if piece is kept else None) for piece in pieces]
        + [(x_first, near, CHIP), (y_first, near, CHIP)],
        [
            ((full_rows, part), F32, near, CHIP), ((full_rows, part), F32, near, CHIP),
        ],
        [pltpu.SemaphoreType.DMA((4, 2, local_heads))],
        aliases={3: 0, 4: 1},
    )
    begin_shape = (count + 1, head_dim, local_heads * state_dim)
    (begin_here,) = call(
        functools.partial(gather_kernel, count - 1, paired),
        (meta,), (),
        [
            (piece, anywhere, CHIP if piece is kept else None)
            for piece in (pieces if paired else pieces + [kept])
        ],
        [(begin_shape, F32, near, CHIP)],
        [pltpu.SemaphoreType.DMA((3, local_heads))],
    )

    ends, mixed_in, back_in, reader_in, writer_in, tab = call(
        functools.partial(inner_kernel, per_chunk, head_dim, vocab),
        (meta,), (chunks,),
        [
            (hid, by_chunk, CHIP), (cot, by_chunk, CHIP), (writer, square, CHIP),
            (reads, square, HBM), (toks, tok_spec, HBM), (cols, one_cols, CHIP),
        ],
        [
            ((2, chunks, 2, state_dim, part), F32, pair, CHIP),
            ((length, width), F32, by_chunk, CHIP),
            ((length, width), F32, by_chunk, CHIP),
            ((length, state_dim), F32, square, CHIP),
            ((length, state_dim), F32, square, CHIP),
            ((lines, state_dim), F32, whole((lines, state_dim)), CHIP),
        ],
        [pltpu.VMEM((length, length), F32)] * 3 + [pltpu.VMEM((state_dim, length), BF16)] * 2,
    )

    def step_chain(slot, side, received, held, begin, waits):
        has_small = slot < count - 2
        has_begin = slot < count - 2
        sends = side == 1 or slot + 1 < slots - 1
        rows = full_rows if has_small else 2 * state_dim
        held_shape = (2, chunks + 1, 2 * state_dim, part)
        ins = [(received, near, CHIP), (ends, near, CHIP), (small, near, CHIP)]
        outs = [((rows, part), F32, near, CHIP)] if sends else []
        outs.append((held_shape, BF16, near, CHIP))
        aliases = {}
        if held is not None:
            aliases[1 + len(ins)] = len(outs) - 1
            ins.append((held, near, CHIP))
        if has_begin:
            aliases[1 + len(ins)] = len(outs)
            ins.append((begin, near, CHIP))
            outs.append((begin_shape, F32, near, CHIP))
        ins += [(value, anywhere, None) for value in waits]
        results = call(
            functools.partial(
                combine_kernel, vocab, has_small, has_begin, sends, slot, side, tables[side]
            ),
            (meta,), (), ins, outs,
            aliases=aliases,
        )
        results = list(results) if has_begin else [*results, begin]
        return results if sends else [None, *results]

    lines_at = 2 * state_dim // lines
    from_slot = pl.BlockSpec((lines, part), lambda k, *_: (lines_at + k, 0))
    grad_parts = [
        pl.BlockSpec((1, 1, 1, state_dim, part), lambda k, *_, way=way: (way, k, 1, 0, 0))
        for way in range(2)
    ]
    sums, exchanges = sum_steps(("rep", "dom", "ctx"))
    assert count % 2 == 0
    even_links = [(at, at ^ 1) for at in range(count)]
    odd_links = [(at, (at - 1 ^ 1) + 1) for at in range(1, count - 1)]
    send_x, send_y, held = x_first, y_first, None
    for slot in range(slots):
        got_x = lax.ppermute(send_x, "ctx", even_links)
        if slot < slots - 1:
            got_y = lax.ppermute(send_y, "ctx", odd_links)
        waits_up, waits_down = [], []
        if slot == count - 2:
            from_x, from_y = got_x, got_y
        if slot == count - 1:
            begin_there = begin_here
            if doms == 2:
                begin_there = lax.ppermute(begin_here, "dom", [(0, 1), (1, 0)])
            (total,) = call(
                functools.partial(
                    sums_kernel, per_chunk, head_dim, vocab,
                    bmat_scale * total_scale, total_scale / math.sqrt(head_dim),
                ),
                (meta,), (chunks,),
                [
                    (from_x, from_slot, None), (from_y, from_slot, None),
                    (small, one_small, CHIP), (ends, grad_parts[0], CHIP),
                    (ends, grad_parts[1], CHIP), (tab, whole(tab.shape), CHIP),
                ],
                [((lines, state_dim), F32, whole((lines, state_dim)), None)],
                [pltpu.VMEM((lines, state_dim), F32)],
            )
        if slot == slots - 1:
            break
        if slot >= count - 1:
            if slot > count - 1:
                waits_up.append(begin_there)
                for step in sums[:1]:
                    total = step(total)
                sums = sums[1:]
            waits_down.append(total)
        send_y, held, begin_here = step_chain(slot, 0, got_x, held, begin_here, waits_down)
        if slot >= count - 1:
            for step in sums[:1]:
                total = step(total)
            sums = sums[1:]
            waits_up.append(total)
        send_x, held, begin_here = step_chain(slot, 1, got_y, held, begin_here, waits_up)

    def chunk_specs(at):
        return (
            pl.BlockSpec((length, part), lambda k, *_: (0, k + at)),
            pl.BlockSpec((1, length, 128), lambda k, *_: (k + at, 0, 0)),
            [
                pl.BlockSpec(
                    (1, 1, 2 * state_dim, part), lambda k, *_, way=way: (way, k + at, 0, 0)
                )
                for way in range(2)
            ],
            pl.BlockSpec(
                (per_chunk // local_heads, head_dim, local_heads * state_dim),
                lambda k, *_: (k + at, 0, 0),
            ),
            pl.BlockSpec((lines, part), lambda k, *_: (lines_at + k + at, 0)),
        )

    def finish_ins(at, sum_c, sum_w):
        slab, col, chain, states, rows = chunk_specs(at)
        return [
            (hid, slab, CHIP), (cot, slab, CHIP), (writer, square, CHIP), (reads, square, HBM),
            (cols, col, CHIP), (mixed_in, slab, CHIP), (back_in, slab, CHIP),
            (sum_c, square, CHIP), (sum_w, square, CHIP),
            (held, chain[0], CHIP), (held, chain[1], CHIP),
            (begin_here, states, CHIP), (begin_there, states, CHIP), (from_x, rows, None), (from_y, rows, None),
        ]

    for step in sums:
        total = step(total)
    slab = chunk_specs(0)[0]
    mixed, grad_hidden, sum_c, sum_w, total = call(
        functools.partial(early_kernel, per_chunk, head_dim, vocab),
        (meta, skip_gain), (chunks - 1,),
        finish_ins(0, reader_in, writer_in) + [(total, anywhere, None)],
        [
            ((length, width), BF16, slab, HBM), ((length, width), BF16, slab, HBM),
            ((length, state_dim), F32, square, CHIP), ((length, state_dim), F32, square, CHIP),
            (total.shape, F32, anywhere, None),
        ],
        aliases={17: 4},
    )
    exchanged = [exchange(total) for exchange in exchanges]
    ins = finish_ins(chunks - 1, sum_c, sum_w) + [
        (got_x, whole(got_x.shape), None),
        (mixed, anywhere, HBM), (grad_hidden, anywhere, HBM),
    ] + [(value, whole(value.shape), None) for value in [total] + exchanged]
    slab = chunk_specs(chunks - 1)[0]
    mixed, grad_hidden, grad_cmat, grad_bmat, grad_table, grad_skip = call(
        functools.partial(
            last_kernel, per_chunk, head_dim, vocab, bmat_scale,
            tables[0][0] + slots - 1, chunks - 1,
        ),
        (meta, skip_gain), (1,), ins,
        [
            ((length, width), BF16, slab, HBM), ((length, width), BF16, slab, HBM),
            ((length, state_dim), BF16, square, HBM), ((length, state_dim), BF16, square, HBM),
            (table.shape, F32, whole(table.shape), HBM),
            ((1, heads), F32, whole((1, heads)), HBM),
        ],
        [pltpu.VMEM((length, state_dim), F32)] * 2,
        aliases={18: 0, 19: 1},
    )
    return (
        mixed.reshape(hidden.shape),
        grad_hidden.reshape(hidden.shape),
        grad_bmat.reshape(bmat.shape),
        grad_cmat.reshape(cmat.shape),
        grad_table,
        grad_skip.reshape(heads),
    )


def solution(mesh):
    rows = P("rep", "dom", "ctx", None)
    return jax.shard_map(
        per_device,
        mesh=mesh,
        in_specs=(
            rows, rows, rows, P("rep", "dom", "ctx"), P(), rows, rows, P(),
            P("rep", "dom", "ctx", None, None), P("rep", "dom"), P("rep"), rows,
        ),
        out_specs=(rows, rows, rows, rows, P(), P()),
        check_vma=False,
    )
```
